256 devices in a mesh: sample: 64 (over z, y, core), rep: 4 (over x).
Axes of the slice: x: 4, y: 4, z: 8, core: 2. Of those that a mesh axis runs over, the one named last changes fastest.
Arguments:
- tokens: bfloat16 [32768, 128], P(('sample', 'rep')), may hold values from -6 to 6
- cache: bfloat16 [32768, 48, 256], P(('sample', 'rep')), may hold values from -144 to 144
- gain: float32 [128], replicated, may hold values from 0.25 to 1.75
- w_query: bfloat16 [128, 128], replicated, may hold values from -0.5 to 0.5
- w_key: bfloat16 [128, 128], replicated, may hold values from -0.5 to 0.5
- w_value: bfloat16 [128, 128], replicated, may hold values from -0.5 to 0.5
- w_out: bfloat16 [128, 128], replicated, may hold values from -0.5 to 0.5
- w_head: bfloat16 [128, 4], replicated, may hold values from -0.5 to 0.5
- coef: float32 [32768], P(('sample', 'rep')), may hold values from -0.625 to 0.625
- chosen: int32 [32768], P(('sample', 'rep')), may hold values from 0 to 3
- dest: int32 [32768, 1], P(('sample', 'rep')), may hold values from 0 to 63; in each aligned block of 128 rows (0 to 127, 128 to 255, ...) at most 4 rows name the same one
Outputs:
- new_cache: bfloat16 [65536, 49, 256], P(('sample', 'rep'))
- log_probs: float32 [65536, 4], P(('sample', 'rep'))
- grad_out: float32 [128, 128], replicated
- grad_head: float32 [128, 4], replicated
The draws below stay inside these ranges and needn't reach their ends.
Inputs may be any that keep to these rules, and one draw needn't show every extreme that they name: `dest`: within the rows of one device, no value is named by more than 4 rows, a bound that some block reaches.
All inputs are finite; a program needn't handle non-finite values.
Results may differ from the reference program's by a relative error of at most 0.022.
Values may be sent and summed in bfloat16 or wider, within the bound.
No kernel may reach another device: no remote copies, remote signals or barrier semaphores. Data moves between devices by JAX's collectives and lax.ppermute only.
A program may use at most 64 MiB of HBM per device.

```python
import math
import jax
import jax.numpy as jnp
import numpy as np
from jax import lax

D = 128
HEADS = 4
OUTCOMES = 4
LEVELS = 48
ROWS_DEV = 128
CAP = 4
SLOTS = 256
ROWS = 32768
RECV = 65536
N_SAMPLE = 64
N_REP = 4


def draw_cache(key, part):
    base = jax.random.truncated_normal(key, -6.0, 6.0, (ROWS, LEVELS, 2 * D), jnp.float32)
    return base.astype(jnp.bfloat16)


def place_ends(result, rng, least, top_value):
    dims = result.shape
    spot = [jax.random.randint(jax.random.fold_in(rng, axis), (), 0, dims[axis]) for axis in range(len(dims))]
    result = result.at[tuple(spot)].set(least)
    longest = dims.index(max(dims))
    spot[longest] = (spot[longest] + 1) % dims[longest]
    return result.at[tuple(spot)].set(top_value)


def levels(rng, extent, split, least, largest):
    def one(axis_at, parts):
        draws = jax.random.uniform(jax.random.fold_in(jax.random.fold_in(rng, 6), axis_at), (parts,), jnp.float32, least / len(split), largest / len(split))
        return jnp.repeat(jnp.exp(draws), extent[axis_at] // parts).reshape((-1,) + (1,) * (len(extent) - axis_at - 1))

    level = one(*split[0])
    for cut in split[1:]:
        level = level * one(*cut)
    return level


def assign_block(own_key, own, number, rows, amount, top, reach, slope):
    sequence = jax.random.permutation(own_key, amount)
    crowded, usual = portions_of(amount, rows * top, reach, slope, True), portions_of(amount, rows * top, reach, slope, False)
    places = jnp.arange(amount)

    def named(tallies, turn):
        used = int((tallies > 0).sum())
        fixed = max(1, used // 4)
        passed = fixed + (places - fixed + turn * (used - fixed)) % max(1, amount - fixed)
        return jnp.zeros((amount,), jnp.int32).at[sequence[jnp.where(places < fixed, places, passed)]].set(jnp.asarray(tallies, jnp.int32))

    tallies = jnp.where(number % 4 == 0, named(crowded, number // 4), named(usual, number - number // 4 - 1))
    mixed = jax.random.permutation(jax.random.fold_in(own, 3), amount)
    source_of, sink = mixed[0:amount // 2 * 2:2], mixed[1:amount // 2 * 2:2]
    margin = jnp.minimum(tallies[source_of] - 1, reach - tallies[sink]) // 2
    margin = jnp.where((source_of == sequence[0]) | (sink == sequence[0]) | (tallies[sink] == 0), 0, jnp.maximum(margin, 0))
    passed = jax.random.randint(jax.random.fold_in(own, 4), (amount // 2,), 0, 1 << 20) % (margin + 1)
    tallies = tallies.at[source_of].add(-passed).at[sink].add(passed)
    items = jnp.searchsorted(jnp.cumsum(tallies), jnp.arange(rows * top), side="right").astype(jnp.int32)
    listing = items.reshape(top, rows).T
    listing = listing[jax.random.permutation(jax.random.fold_in(own, 1), rows)]
    turn = jax.random.randint(jax.random.fold_in(own, 2), (rows, 1), 0, top)
    return jnp.take_along_axis(listing, (jnp.arange(top)[None, :] + turn) % top, axis=1)


def portions_of(amount, total, reach, skew, full):
    portions = [(1 << 20) // math.isqrt(standing ** skew) + 1 for standing in range(1, amount + 1)]
    largest = reach if full else min(reach, max(-(-total // amount), total * portions[0] // sum(portions)))
    least = 1 if total - largest >= amount - 1 else 0
    given, surplus = [largest] + [least] * (amount - 1), total - largest - least * (amount - 1)
    while surplus > 0:
        movable = [i for i in range(1, amount) if given[i] < largest] or [i for i in range(1, amount) if given[i] < reach]
        whole, left = sum([portions[i] for i in movable]), surplus
        for i in movable:
            more = min(reach - given[i], max(1, left * portions[i] // whole), surplus)
            given[i] = given[i] + more
            surplus = surplus - more
    return np.array(given)


def gaussian(key, dims, spread, limit, split=(), held_as=jnp.bfloat16):
    level = levels(key, dims, split, -0.22, 0.18) if split else 1.0
    result = jax.random.normal(key, dims, jnp.float32) * spread * level
    return jnp.minimum(jnp.maximum(result, -limit), limit).astype(held_as)


def setup_inputs(seed: int = 0) -> dict:
    streams_of = jax.random.split(jax.random.key(seed), 12)
    tokens = gaussian(streams_of[0], (ROWS, D), 1.0, 6.0, ((0, 256),))
    cache = draw_cache(jax.random.fold_in(streams_of[11], 71), 0)
    gain = jnp.clip(1.0 + 0.15 * jax.random.normal(streams_of[2], (D,), jnp.float32), 0.25, 1.75)
    w_query = gaussian(streams_of[3], (D, D), D ** -0.5, 0.5)
    w_key = gaussian(streams_of[4], (D, D), D ** -0.5, 0.5)
    w_value = gaussian(streams_of[5], (D, D), D ** -0.5, 0.5)
    w_out = gaussian(streams_of[6], (D, D), D ** -0.5, 0.5)
    w_head = gaussian(streams_of[7], (D, OUTCOMES), D ** -0.5, 0.5)
    coef = gaussian(streams_of[8], (ROWS,), (8.0 / (ROWS * 1.0) ** 0.5), 0.625, ((0, 256),), jnp.float32)
    chosen = place_ends(jax.random.randint(streams_of[9], (ROWS,), 0, 4), jax.random.fold_in(streams_of[9], 1), 0, 3).astype(jnp.int32)
    dest_keys = jax.random.split(jax.random.fold_in(streams_of[10], 1), ROWS // ROWS_DEV)
    dest_turns = jax.random.permutation(jax.random.fold_in(streams_of[10], 3), ROWS // ROWS_DEV)
    dest = jax.vmap(lambda own, number: assign_block(jax.random.fold_in(streams_of[10], 2), own, number, ROWS_DEV, N_SAMPLE, 1, CAP, 2))(dest_keys, dest_turns).reshape((ROWS, 1))
    return {"tokens": tokens, "cache": cache, "gain": gain, "w_query": w_query, "w_key": w_key, "w_value": w_value, "w_out": w_out, "w_head": w_head, "coef": coef, "chosen": chosen, "dest": dest}


def decode_rows(tokens, cache, coef, chosen, gain, w_query, w_key, w_value, w_out, w_head):
    count = tokens.shape[0]
    size = D // HEADS
    xf = tokens.astype(jnp.float32)
    normed = (xf * lax.rsqrt(lax.optimization_barrier(jnp.mean(xf * xf, -1, keepdims=True)) + 1e-05) * gain).astype(jnp.bfloat16)
    query = (jnp.dot(normed, w_query, preferred_element_type=jnp.float32) * (1.0 / math.sqrt(size))).astype(jnp.bfloat16)
    key_new = jnp.dot(normed, w_key, preferred_element_type=jnp.float32).astype(jnp.bfloat16)
    value_new = jnp.dot(normed, w_value, preferred_element_type=jnp.float32).astype(jnp.bfloat16)
    query_heads = query.astype(jnp.float32).reshape(count, HEADS, size)
    key_rows = cache[:, :, :D].astype(jnp.float32).reshape(count, LEVELS, HEADS, size)
    value_rows = cache[:, :, D:].astype(jnp.float32).reshape(count, LEVELS, HEADS, size)
    cached_scores = jnp.einsum('yfn,yjfn->yfj', query_heads, key_rows)
    score_self = lax.optimization_barrier(jnp.sum(query_heads * key_new.astype(jnp.float32).reshape(count, HEADS, size), -1))
    top = jnp.maximum(lax.optimization_barrier(jnp.max(cached_scores, -1)), score_self)
    exp_cache = jnp.exp(cached_scores - top[..., None])
    exp_self = jnp.exp(score_self - top)
    total = lax.optimization_barrier(jnp.sum(exp_cache, -1)) + exp_self
    cached_weights = (exp_cache / total[..., None]).astype(jnp.bfloat16)
    weight_self = (exp_self / total).astype(jnp.bfloat16)
    attention_output = jnp.einsum('jat,jtaf->jaf', cached_weights.astype(jnp.float32), value_rows)
    attention_output = attention_output + weight_self.astype(jnp.float32)[..., None] * value_new.astype(jnp.float32).reshape(count, HEADS, size)
    attention_output = attention_output.reshape(count, D).astype(jnp.bfloat16)
    hidden = (xf + jnp.dot(attention_output, w_out, preferred_element_type=jnp.float32)).astype(jnp.bfloat16)
    logits = jnp.dot(hidden, w_head, preferred_element_type=jnp.float32)
    logp = jax.nn.log_softmax(logits, -1)
    picked = (chosen[:, None] == jnp.arange(OUTCOMES, dtype=jnp.int32)[None, :]).astype(jnp.float32)
    dlog = coef[:, None] * (picked - jnp.exp(logp))
    grad_head = jnp.dot(hidden.astype(jnp.float32).T, dlog, precision=lax.Precision.HIGHEST)
    hidden_gradient = jnp.dot(dlog, w_head.astype(jnp.float32).T, precision=lax.Precision.HIGHEST)
    grad_out = jnp.dot(attention_output.astype(jnp.float32).T, hidden_gradient, precision=lax.Precision.HIGHEST)
    both = jnp.concatenate([key_new, value_new], -1)
    return (both, logp, grad_out, grad_head)

def reference(tokens, cache, gain, w_query, w_key, w_value, w_out, w_head, coef, chosen, dest):
    blocks = ROWS // ROWS_DEV

    def one_block(items):
        return decode_rows(items[0], items[1], items[2], items[3], gain, w_query, w_key, w_value, w_out, w_head)
    both, logp, grad_out, grad_head = lax.map(one_block, (tokens.reshape(blocks, ROWS_DEV, D), cache.reshape(blocks, ROWS_DEV, LEVELS, 2 * D), coef.reshape(blocks, ROWS_DEV), chosen.reshape(blocks, ROWS_DEV)))
    target = dest[:, 0].reshape(blocks, ROWS_DEV)
    onehot = (target[..., None] == jnp.arange(N_SAMPLE, dtype=jnp.int32)[None, None, :]).astype(jnp.int32)
    rank = lax.optimization_barrier(jnp.sum(jnp.cumsum(onehot, 1) * onehot, -1)) - 1
    device = jnp.arange(blocks, dtype=jnp.int32)[:, None]
    place = ((target * N_REP + device % N_REP) * SLOTS + device // N_REP * CAP + rank).reshape(ROWS).astype(jnp.int32)
    new_cache = jnp.zeros((RECV, LEVELS + 1, 2 * D), jnp.bfloat16)
    new_cache = new_cache.at[place, :LEVELS].set(cache)
    new_cache = new_cache.at[place, LEVELS].set(both.reshape(ROWS, 2 * D))
    log_probs = jnp.zeros((RECV, OUTCOMES), jnp.float32).at[place].set(logp.reshape(ROWS, OUTCOMES))
    return (new_cache, log_probs, lax.optimization_barrier(jnp.sum(grad_out, 0)), lax.optimization_barrier(jnp.sum(grad_head, 0)))
```

```python
import functools
import math

import jax
import jax.numpy as jnp
from jax import lax
from jax.experimental import pallas as pl
from jax.experimental.pallas import tpu as pltpu
from jax.sharding import PartitionSpec as P

HEADS = 4
OUTCOMES = 4
ROWS = 128
LEVELS = 48
WIDTH = 256
PEERS = 64
PLANES = 8
SIDE = 8
RELAY = 8
DIRECT = 2 * LEVELS + 8
PIECE = RELAY * LEVELS + 8
LAST = 2 * PLANES * LEVELS + 8
ANY = pl.BlockSpec(memory_space=pl.ANY)
SMEM = pl.BlockSpec(memory_space=pltpu.SMEM)


def decode_rows(tokens, cache, coef, chosen, gain, w_query, w_key, w_value, w_out, w_head):
    count = tokens.shape[0]
    width = tokens.shape[1]
    levels = cache.shape[1]
    size = width // HEADS
    xf = tokens.astype(jnp.float32)
    normed = (xf * lax.rsqrt(jnp.mean(xf * xf, -1, keepdims=True) + 1e-05) * gain).astype(
        jnp.bfloat16
    )
    query = (
        jnp.dot(normed, w_query, preferred_element_type=jnp.float32) * (1.0 / math.sqrt(size))
    ).astype(jnp.bfloat16)
    key_new = jnp.dot(normed, w_key, preferred_element_type=jnp.float32).astype(jnp.bfloat16)
    value_new = jnp.dot(normed, w_value, preferred_element_type=jnp.float32).astype(jnp.bfloat16)
    query_heads = query.reshape(count, HEADS, size)
    key_rows = cache[:, :, :width].reshape(count, levels, HEADS, size)
    value_rows = cache[:, :, width:].reshape(count, levels, HEADS, size)
    cached_scores = jnp.einsum(
        "yfn,yjfn->yfj", query_heads, key_rows, preferred_element_type=jnp.float32
    )
    score_self = jnp.sum(
        query_heads.astype(jnp.float32) * key_new.astype(jnp.float32).reshape(count, HEADS, size),
        -1,
    )
    top = jnp.maximum(jnp.max(cached_scores, -1), score_self)
    exp_cache = jnp.exp(cached_scores - top[..., None])
    exp_self = jnp.exp(score_self - top)
    total = jnp.sum(exp_cache, -1) + exp_self
    cached_weights = (exp_cache / total[..., None]).astype(jnp.bfloat16)
    weight_self = (exp_self / total).astype(jnp.bfloat16)
    attention_output = jnp.einsum(
        "jat,jtaf->jaf", cached_weights, value_rows, preferred_element_type=jnp.float32
    )
    attention_output = attention_output + weight_self.astype(jnp.float32)[
        ..., None
    ] * value_new.astype(jnp.float32).reshape(count, HEADS, size)
    attention_output = attention_output.reshape(count, width).astype(jnp.bfloat16)
    hidden = (xf + jnp.dot(attention_output, w_out, preferred_element_type=jnp.float32)).astype(
        jnp.bfloat16
    )
    logits = jnp.dot(hidden, w_head, preferred_element_type=jnp.float32)
    logp = jax.nn.log_softmax(logits, -1)
    picked = (chosen[:, None] == jnp.arange(OUTCOMES, dtype=jnp.int32)[None, :]).astype(jnp.float32)
    dlog = coef[:, None] * (picked - jnp.exp(logp))
    grad_head = jnp.dot(dlog.T, hidden.astype(jnp.float32), precision=lax.Precision.HIGHEST)
    hidden_gradient = jnp.dot(dlog, w_head.astype(jnp.float32).T, precision=lax.Precision.HIGHEST)
    grad_out = jnp.dot(
        attention_output.astype(jnp.float32).T, hidden_gradient, precision=lax.Precision.HIGHEST
    )
    both = jnp.concatenate([key_new, value_new], -1)
    return (both, logp, grad_out, grad_head)


def cleared(ref, count):
    @pl.loop(0, count)
    def _(i):
        ref[i] = 0


def relay_kernel(dest, cache, out, count, filled, meta, tile, rows_sem, tile_sem):
    cleared(count, PEERS)
    cleared(filled, PLANES + 1)
    meta[...] = jnp.full(meta.shape, -1.0, jnp.float32)
    lane = lax.broadcasted_iota(jnp.int32, (8, WIDTH), 1)

    @pl.loop(0, ROWS)
    def _(i):
        d = dest[i]
        rank = count[d]
        count[d] = rank + 1

        @pl.when(rank >= 2)
        def _():
            plane = lax.div(d, SIDE)
            at = filled[plane]
            filled[plane] = at + 1

            @pl.when(at < RELAY)
            def _():
                start = pl.multiple_of(at * LEVELS, LEVELS)
                pltpu.make_async_copy(
                    cache.at[i], out.at[plane, pl.ds(start, LEVELS)], rows_sem
                ).start()
                code = lax.rem(d, SIDE) * 2 + rank - 2
                meta[plane] = jnp.where(lane == at, code.astype(jnp.float32), meta[plane])
                filled[PLANES] += 1

    most = filled[0]
    for plane in range(1, PLANES):
        most = jnp.maximum(most, filled[plane])
    over = jnp.where(most > RELAY, 1.0, 0.0)
    for plane in range(PLANES):
        tile[plane] = jnp.where(lane == RELAY, over, meta[plane]).astype(jnp.bfloat16)
    last = pltpu.make_async_copy(tile, out.at[:, pl.ds(RELAY * LEVELS, 8)], tile_sem)
    last.start()

    @pl.loop(0, filled[PLANES])
    def _(i):
        pltpu.make_async_copy(cache.at[0], out.at[0, pl.ds(0, LEVELS)], rows_sem).wait()

    last.wait()


def direct_kernel(low, dest, cache, tiles, out, count, zero, rows_sem, tile_sem):
    cleared(count, PEERS)
    zero[...] = jnp.zeros(zero.shape, zero.dtype)
    last = pltpu.make_async_copy(tiles, out.at[:, pl.ds(2 * LEVELS, 8)], tile_sem)
    last.start()

    @pl.loop(0, ROWS)
    def _(i):
        d = dest[i]
        rank = count[d]
        count[d] = rank + 1

        @pl.when((rank >= low) & (rank < low + 2))
        def _():
            start = pl.multiple_of((rank - low) * LEVELS, LEVELS)
            pltpu.make_async_copy(cache.at[i], out.at[d, pl.ds(start, LEVELS)], rows_sem).start()

    @pl.loop(0, PEERS)
    def _(d):
        for r in range(2):

            @pl.when(count[d] <= low + r)
            def _():
                pltpu.make_async_copy(zero, out.at[d, pl.ds(r * LEVELS, LEVELS)], rows_sem).start()

    whole = out.at[:, pl.ds(0, 2 * LEVELS)]
    pltpu.make_async_copy(whole, whole, rows_sem).wait()
    last.wait()


def forward_kernel(codes, side, got, *refs):
    outs, (source, zero, tile, rows_sem, tile_sem) = refs[:SIDE], refs[SIDE:]
    zero[...] = jnp.zeros(zero.shape, zero.dtype)

    @pl.loop(0, SIDE * 2 * PLANES)
    def _(i):
        source[i] = -1

    over = jnp.int32(0)
    for plane in range(PLANES):
        over = jnp.maximum(over, codes[plane, RELAY])
        for at in range(RELAY):
            code = codes[plane, at]

            @pl.when(code >= 0)
            def _():
                source[code * PLANES + plane] = at

    tile[...] = jnp.full(tile.shape, over.astype(jnp.float32)).astype(jnp.bfloat16)
    for k, out in enumerate(outs):
        pltpu.make_async_copy(tile, out.at[pl.ds(2 * PLANES * LEVELS, 8)], tile_sem.at[k]).start()
        peer = side[k]

        @pl.loop(0, 2 * PLANES)
        def _(i):
            plane = lax.div(i, 2)
            r = lax.rem(i, 2)
            at = source[(peer * 2 + r) * PLANES + plane]
            to = out.at[pl.ds(pl.multiple_of(i * LEVELS, LEVELS), LEVELS)]

            @pl.when(at >= 0)
            def _():
                start = pl.multiple_of(at * LEVELS, LEVELS)
                pltpu.make_async_copy(
                    got.at[plane, pl.ds(start, LEVELS)], to, rows_sem.at[k]
                ).start()

            @pl.when(at < 0)
            def _():
                pltpu.make_async_copy(zero, to, rows_sem.at[k]).start()

    for k, out in enumerate(outs):
        whole = out.at[pl.ds(0, 2 * PLANES * LEVELS)]
        pltpu.make_async_copy(whole, whole, rows_sem.at[k]).wait()
        pltpu.make_async_copy(tile, out.at[pl.ds(2 * PLANES * LEVELS, 8)], tile_sem.at[k]).wait()


def settle_kernel(side, direct, *refs):
    lasts, out, (held, sems) = refs[:SIDE], refs[SIDE], refs[SIDE + 1 :]
    t = pl.program_id(0)
    rows = 2 * PLANES * LEVELS

    @pl.when(t == 0)
    def _():
        copies = [
            pltpu.make_async_copy(last.at[pl.ds(0, rows)], held.at[side[k]], sems.at[k])
            for k, last in enumerate(lasts)
        ]
        for copy in copies:
            copy.start()
        for copy in copies:
            copy.wait()

    plane = lax.div(t, SIDE // 2)
    pair = lax.rem(t, SIDE // 2) * 2
    parts = []
    for j in range(2):
        for r in range(2):
            parts.append(direct[j, r * LEVELS : (r + 1) * LEVELS, :])
        for r in range(2):
            start = pl.multiple_of((plane * 2 + r) * LEVELS, LEVELS)
            parts.append(held[pair + j, pl.ds(start, LEVELS), :])
    stacked = jnp.stack([p.astype(jnp.float32) for p in parts], 0)
    out[:LEVELS] = jnp.swapaxes(stacked, 0, 1).astype(out.dtype)
    new = [direct[j, 2 * LEVELS : 2 * LEVELS + 4, :] for j in range(2)]
    out[LEVELS] = jnp.concatenate(new, 0)


def settle(side, direct, lasts):
    return pl.pallas_call(
        settle_kernel,
        grid=(PEERS // 2,),
        out_shape=jax.ShapeDtypeStruct((LEVELS + 1, 4 * PEERS, WIDTH), jnp.bfloat16),
        in_specs=[SMEM, pl.BlockSpec((2, DIRECT, WIDTH), lambda t: (t, 0, 0))] + [ANY] * SIDE,
        out_specs=pl.BlockSpec((LEVELS + 1, 8, WIDTH), lambda t: (0, t, 0)),
        scratch_shapes=[
            pltpu.VMEM((SIDE, 2 * PLANES * LEVELS, WIDTH), jnp.bfloat16),
            pltpu.SemaphoreType.DMA((SIDE,)),
        ],
        compiler_params=pltpu.CompilerParams(vmem_limit_bytes=32 << 20),
        name="settle",
    )(side, direct, *lasts)


def pack_direct(low, dest, cache, tiles):
    return pl.pallas_call(
        functools.partial(direct_kernel, low),
        out_shape=jax.ShapeDtypeStruct((PEERS, DIRECT, WIDTH), jnp.bfloat16),
        in_specs=[SMEM, ANY, ANY],
        out_specs=ANY,
        scratch_shapes=[
            pltpu.SMEM((PEERS,), jnp.int32),
            pltpu.VMEM((LEVELS, WIDTH), jnp.bfloat16),
            pltpu.SemaphoreType.DMA,
            pltpu.SemaphoreType.DMA,
        ],
        name="pack_direct",
    )(dest, cache, tiles)


def exchanged(x, groups=None):
    return lax.all_to_all(
        x, "sample", split_axis=0, concat_axis=0, tiled=True, axis_index_groups=groups
    )


def xor_pairs(size, bit):
    return [(i, i ^ bit) for i in range(size)]


def summed_in_plane(grads):
    for axis, size, bit in (
        ("sample", PEERS, 1),
        ("rep", 4, 1),
        ("rep", 4, 2),
        ("sample", PEERS, 2),
        ("sample", PEERS, 4),
    ):
        grads = grads + lax.ppermute(grads, axis, xor_pairs(size, bit))
    return grads


def summed_over_planes(grads):
    terms = [grads] + [
        lax.ppermute(grads, "sample", xor_pairs(PEERS, SIDE * k)) for k in range(1, PLANES)
    ]
    while len(terms) > 1:
        terms = [terms[i] + terms[i + 1] for i in range(0, len(terms), 2)]
    return terms[0]


def bf16_terms(x):
    terms = []
    for _ in range(3):
        term = lax.reduce_precision(x, 8, 7)
        terms.append(term.astype(jnp.bfloat16))
        x = x - term
    return terms


def on_device(tokens, cache, gain, w_query, w_key, w_value, w_out, w_head, coef, chosen, dest):
    target = dest[:, 0]
    me = lax.axis_index("sample")
    y, core = lax.rem(lax.div(me, 2), 4), lax.rem(me, 2)

    relay = pl.pallas_call(
        relay_kernel,
        out_shape=jax.ShapeDtypeStruct((PLANES, PIECE, WIDTH), jnp.bfloat16),
        in_specs=[SMEM, ANY],
        out_specs=ANY,
        scratch_shapes=[
            pltpu.SMEM((PEERS,), jnp.int32),
            pltpu.SMEM((PLANES + 1,), jnp.int32),
            pltpu.VMEM((PLANES, 8, WIDTH), jnp.float32),
            pltpu.VMEM((PLANES, 8, WIDTH), jnp.bfloat16),
            pltpu.SemaphoreType.DMA,
            pltpu.SemaphoreType.DMA,
        ],
        name="pack_relay",
    )(target, cache)
    relayed = exchanged(relay, [[z * SIDE + i for z in range(PLANES)] for i in range(SIDE)])

    both, logp, grad_out, grad_head = decode_rows(
        tokens, cache, coef, chosen, gain, w_query, w_key, w_value, w_out, w_head
    )
    grads = summed_in_plane(jnp.concatenate([grad_out, grad_head], 0))

    rows = jnp.arange(ROWS, dtype=jnp.int32)
    same = (target[:, None] == target[None, :]) & (rows[:, None] < rows[None, :])
    place = target * 4 + jnp.sum(same.astype(jnp.int32), 0)
    slot = (jnp.arange(4 * PEERS, dtype=jnp.int32)[:, None] == place[None, :]).astype(jnp.bfloat16)
    small = jnp.concatenate([both] + bf16_terms(logp), -1)
    slotted = jnp.dot(slot, small, preferred_element_type=jnp.float32).astype(jnp.bfloat16)
    new_rows = slotted[:, :WIDTH].reshape(PEERS, 4, WIDTH)
    logp_row = jnp.pad(
        slotted[:, WIDTH:].reshape(PEERS, 1, 4 * 3 * OUTCOMES),
        ((0, 0), (0, 3), (0, WIDTH - 12 * OUTCOMES)),
    )
    tiles = jnp.concatenate([new_rows, logp_row], 1)
    direct = exchanged(pack_direct(0, target, cache, tiles))

    codes = relayed[:, RELAY * LEVELS, : 2 * RELAY].astype(jnp.int32)
    shifts = [(dy, dc) for dy in range(4) for dc in range(2)]
    onto = jnp.stack([lax.rem(y + dy, 4) * 2 + (core ^ dc) for dy, dc in shifts])
    came = jnp.stack([lax.rem(y - dy + 4, 4) * 2 + (core ^ dc) for dy, dc in shifts])
    onward = pl.pallas_call(
        forward_kernel,
        out_shape=[jax.ShapeDtypeStruct((LAST, WIDTH), jnp.bfloat16)] * SIDE,
        in_specs=[SMEM, SMEM, ANY],
        out_specs=[ANY] * SIDE,
        scratch_shapes=[
            pltpu.SMEM((SIDE * 2 * PLANES,), jnp.int32),
            pltpu.VMEM((LEVELS, WIDTH), jnp.bfloat16),
            pltpu.VMEM((8, WIDTH), jnp.bfloat16),
            pltpu.SemaphoreType.DMA((SIDE,)),
            pltpu.SemaphoreType.DMA((SIDE,)),
        ],
        name="pack_plane",
    )(codes, onto.astype(jnp.int32), relayed)
    lasts = [onward[0]]
    for k in range(1, SIDE):
        dy, dc = shifts[k]
        pairs = [
            ((z * 4 + y0) * 2 + c0, (z * 4 + (y0 + dy) % 4) * 2 + (c0 ^ dc))
            for z in range(PLANES)
            for y0 in range(4)
            for c0 in range(2)
        ]
        lasts.append(lax.ppermute(onward[k], "sample", pairs))
    grads, lasts = lax.optimization_barrier((grads, lasts))
    grads = summed_over_planes(grads)
    over = jnp.max(jnp.stack([last[2 * PLANES * LEVELS, 0] for last in lasts]))
    came = came.astype(jnp.int32)

    def by_relay(direct, lasts):
        return settle(came, direct, lasts)

    def by_pairs(direct, lasts):
        high = exchanged(pack_direct(2, target, cache, jnp.zeros_like(tiles)))
        high = high[:, : 2 * LEVELS].reshape(PLANES, SIDE, 2 * LEVELS, WIDTH)
        high = jnp.swapaxes(high, 0, 1).reshape(SIDE, 2 * PLANES * LEVELS, WIDTH)
        high = [
            lax.dynamic_index_in_dim(high, came[k], 0, keepdims=False) for k in range(SIDE)
        ]
        return settle(came, direct, [jnp.pad(h, ((0, 8), (0, 0))) for h in high])

    new_cache = lax.cond(over > 0, by_pairs, by_relay, direct, lasts)
    terms = direct[:, 2 * LEVELS + 4, : 12 * OUTCOMES].astype(jnp.float32)
    terms = terms.reshape(4 * PEERS, 3, OUTCOMES)
    log_probs = (terms[:, 2] + terms[:, 1]) + terms[:, 0]
    return (jnp.swapaxes(new_cache, 0, 1), log_probs, grads[:ROWS], grads[ROWS:].T)


def solution(mesh):
    split = P(("sample", "rep"))
    whole = P()
    return jax.shard_map(
        on_device,
        mesh=mesh,
        in_specs=(split, split) + (whole,) * 6 + (split,) * 3,
        out_specs=(split, split, whole, whole),
        check_vma=False,
    )
```

```python
import functools
import math

import jax
import jax.numpy as jnp
from jax import lax
from jax.experimental import pallas as pl
from jax.experimental.pallas import tpu as pltpu
from jax.sharding import PartitionSpec as P

HEADS = 4
OUTCOMES = 4
ROWS = 128
LEVELS = 48
WIDTH = 256
PEERS = 64
PLANES = 8
SIDE = 8
RELAY = 8
DIRECT = 2 * LEVELS + 8
PIECE = RELAY * LEVELS + 8
LAST = 2 * PLANES * LEVELS
ANY = pl.BlockSpec(memory_space=pl.ANY)
SMEM = pl.BlockSpec(memory_space=pltpu.SMEM)


def decode_rows(tokens, cache, coef, chosen, gain, w_query, w_key, w_value, w_out, w_head):
    count = tokens.shape[0]
    width = tokens.shape[1]
    levels = cache.shape[1]
    size = width // HEADS
    xf = tokens.astype(jnp.float32)
    normed = (xf * lax.rsqrt(jnp.mean(xf * xf, -1, keepdims=True) + 1e-05) * gain).astype(
        jnp.bfloat16
    )
    query = (
        jnp.dot(normed, w_query, preferred_element_type=jnp.float32) * (1.0 / math.sqrt(size))
    ).astype(jnp.bfloat16)
    key_new = jnp.dot(normed, w_key, preferred_element_type=jnp.float32).astype(jnp.bfloat16)
    value_new = jnp.dot(normed, w_value, preferred_element_type=jnp.float32).astype(jnp.bfloat16)
    query_heads = query.reshape(count, HEADS, size)
    key_rows = cache[:, :, :width].reshape(count, levels, HEADS, size)
    value_rows = cache[:, :, width:].reshape(count, levels, HEADS, size)
    cached_scores = jnp.einsum(
        "yfn,yjfn->yfj", query_heads, key_rows, preferred_element_type=jnp.float32
    )
    score_self = jnp.sum(
        query_heads.astype(jnp.float32) * key_new.astype(jnp.float32).reshape(count, HEADS, size),
        -1,
    )
    top = jnp.maximum(jnp.max(cached_scores, -1), score_self)
    exp_cache = jnp.exp(cached_scores - top[..., None])
    exp_self = jnp.exp(score_self - top)
    total = jnp.sum(exp_cache, -1) + exp_self
    cached_weights = (exp_cache / total[..., None]).astype(jnp.bfloat16)
    weight_self = (exp_self / total).astype(jnp.bfloat16)
    attention_output = jnp.einsum(
        "jat,jtaf->jaf", cached_weights, value_rows, preferred_element_type=jnp.float32
    )
    attention_output = attention_output + weight_self.astype(jnp.float32)[
        ..., None
    ] * value_new.astype(jnp.float32).reshape(count, HEADS, size)
    attention_output = attention_output.reshape(count, width).astype(jnp.bfloat16)
    hidden = (xf + jnp.dot(attention_output, w_out, preferred_element_type=jnp.float32)).astype(
        jnp.bfloat16
    )
    logits = jnp.dot(hidden, w_head, preferred_element_type=jnp.float32)
    logp = jax.nn.log_softmax(logits, -1)
    picked = (chosen[:, None] == jnp.arange(OUTCOMES, dtype=jnp.int32)[None, :]).astype(jnp.float32)
    dlog = coef[:, None] * (picked - jnp.exp(logp))
    grad_head = jnp.dot(dlog.T, hidden.astype(jnp.float32), precision=lax.Precision.HIGHEST)
    hidden_gradient = jnp.dot(dlog, w_head.astype(jnp.float32).T, precision=lax.Precision.HIGHEST)
    grad_out = jnp.dot(
        attention_output.astype(jnp.float32).T, hidden_gradient, precision=lax.Precision.HIGHEST
    )
    both = jnp.concatenate([key_new, value_new], -1)
    return (both, logp, grad_out, grad_head)


def cleared(ref, count):
    @pl.loop(0, count)
    def _(i):
        ref[i] = 0


def relay_kernel(dest, cache, out, over, count, filled, meta, held, rows_sem, out_sem):
    cleared(count, PEERS)
    cleared(filled, PLANES + 1)
    meta[...] = jnp.full(meta.shape, -1.0, jnp.float32)
    lane = lax.broadcasted_iota(jnp.int32, (8, WIDTH), 1)

    @pl.loop(0, ROWS)
    def _(i):
        d = dest[i]
        rank = count[d]
        count[d] = rank + 1

        @pl.when(rank >= 2)
        def _():
            plane = lax.div(d, SIDE)
            at = filled[plane]
            filled[plane] = at + 1

            @pl.when(at < RELAY)
            def _():
                start = pl.multiple_of(at * LEVELS, LEVELS)
                pltpu.make_async_copy(
                    cache.at[i], held.at[plane, pl.ds(start, LEVELS)], rows_sem
                ).start()
                code = lax.rem(d, SIDE) * 2 + rank - 2
                meta[plane] = jnp.where(lane == at, code.astype(jnp.float32), meta[plane])
                filled[PLANES] += 1

    most = filled[0]
    for plane in range(1, PLANES):
        most = jnp.maximum(most, filled[plane])
    over[...] = jnp.full(over.shape, jnp.where(most > RELAY, 1.0, 0.0), jnp.float32)
    for plane in range(PLANES):
        held[plane, RELAY * LEVELS :, :] = meta[plane].astype(jnp.bfloat16)

    @pl.loop(0, filled[PLANES])
    def _(i):
        pltpu.make_async_copy(cache.at[0], held.at[0, pl.ds(0, LEVELS)], rows_sem).wait()

    whole = pltpu.make_async_copy(held, out, out_sem)
    whole.start()
    whole.wait()


def direct_kernel(low, dest, cache, tiles, out, count, zero, rows_sem, tile_sem):
    cleared(count, PEERS)
    zero[...] = jnp.zeros(zero.shape, zero.dtype)
    last = pltpu.make_async_copy(tiles, out.at[:, pl.ds(2 * LEVELS, 8)], tile_sem)
    last.start()

    @pl.loop(0, ROWS)
    def _(i):
        d = dest[i]
        rank = count[d]
        count[d] = rank + 1

        @pl.when((rank >= low) & (rank < low + 2))
        def _():
            start = pl.multiple_of((rank - low) * LEVELS, LEVELS)
            pltpu.make_async_copy(cache.at[i], out.at[d, pl.ds(start, LEVELS)], rows_sem).start()

    @pl.loop(0, PEERS)
    def _(d):
        for r in range(2):

            @pl.when(count[d] <= low + r)
            def _():
                pltpu.make_async_copy(zero, out.at[d, pl.ds(r * LEVELS, LEVELS)], rows_sem).start()

    whole = out.at[:, pl.ds(0, 2 * LEVELS)]
    pltpu.make_async_copy(whole, whole, rows_sem).wait()
    last.wait()


def forward_kernel(codes, side, got, *refs):
    outs, (source, zero, rows_sem) = refs[:SIDE], refs[SIDE:]
    zero[...] = jnp.zeros(zero.shape, zero.dtype)

    @pl.loop(0, SIDE * 2 * PLANES)
    def _(i):
        source[i] = -1

    for plane in range(PLANES):
        for at in range(RELAY):
            code = codes[plane, at]

            @pl.when(code >= 0)
            def _():
                source[code * PLANES + plane] = at

    for k, out in enumerate(outs):
        peer = side[k]

        @pl.loop(0, 2 * PLANES)
        def _(i):
            plane = lax.div(i, 2)
            r = lax.rem(i, 2)
            at = source[(peer * 2 + r) * PLANES + plane]
            to = out.at[pl.ds(pl.multiple_of(i * LEVELS, LEVELS), LEVELS)]

            @pl.when(at >= 0)
            def _():
                start = pl.multiple_of(at * LEVELS, LEVELS)
                pltpu.make_async_copy(
                    got.at[plane, pl.ds(start, LEVELS)], to, rows_sem.at[k]
                ).start()

            @pl.when(at < 0)
            def _():
                pltpu.make_async_copy(zero, to, rows_sem.at[k]).start()

    for k, out in enumerate(outs):
        pltpu.make_async_copy(out, out, rows_sem.at[k]).wait()


def chosen_rows(count, size, pick):
    i = lax.broadcasted_iota(jnp.int32, (count, size), 0)
    j = lax.broadcasted_iota(jnp.int32, (count, size), 1)
    return (j == pick(i)).astype(jnp.float32).astype(jnp.bfloat16)


def settle_kernel(side, direct, *refs):
    lasts, (out, logp, held) = refs[:SIDE], refs[SIDE:]
    for k, last in enumerate(lasts):
        held[side[k]] = last[...]
    turn = chosen_rows(WIDTH, WIDTH, lambda i: lax.rem(i, 16) * 16 + lax.div(i, 16))
    for group in range(2):
        for low in range(0, LEVELS, 16):
            parts = []
            for j in range(4 * group, 4 * group + 4):
                for ref in (direct, held):
                    for r in range(2):
                        start = r * LEVELS + low
                        parts.append(ref[j, start : start + 16, :])
            turned = jnp.dot(turn, jnp.concatenate(parts, 0), preferred_element_type=jnp.float32)
            turned = turned.astype(jnp.bfloat16).reshape(16, 16, WIDTH)
            out[low : low + 16, 16 * group : 16 * group + 16, :] = turned
    tiles = jnp.concatenate([direct[j, 2 * LEVELS :, :] for j in range(SIDE)], 0)
    new = chosen_rows(4 * SIDE, 8 * SIDE, lambda i: lax.div(i, 4) * 8 + lax.rem(i, 4))
    out[LEVELS] = jnp.dot(new, tiles, preferred_element_type=jnp.float32).astype(jnp.bfloat16)
    spread = chosen_rows(4 * SIDE, 8 * SIDE, lambda i: lax.div(i, 4) * 8 + 4)
    terms = jnp.dot(spread, tiles, preferred_element_type=jnp.float32)
    slot = lax.broadcasted_iota(jnp.int32, terms.shape, 0)
    lane = lax.broadcasted_iota(jnp.int32, terms.shape, 1)
    mine = lax.div(lane, 3 * OUTCOMES) == lax.rem(slot, 4)
    terms = jnp.where(mine, terms, 0.0).astype(jnp.bfloat16)
    lane = lax.broadcasted_iota(jnp.int32, (WIDTH, 128), 0)
    outcome = lax.broadcasted_iota(jnp.int32, (WIDTH, 128), 1)
    gather = (lax.rem(lane, OUTCOMES) == outcome).astype(jnp.float32).astype(jnp.bfloat16)
    logp[...] = jnp.dot(terms, gather, preferred_element_type=jnp.float32)


def settle(side, direct, lasts):
    return pl.pallas_call(
        settle_kernel,
        grid=(PLANES,),
        out_shape=(
            jax.ShapeDtypeStruct((LEVELS + 1, 4 * PEERS, WIDTH), jnp.bfloat16),
            jax.ShapeDtypeStruct((4 * PEERS, 128), jnp.float32),
        ),
        in_specs=[SMEM, pl.BlockSpec((SIDE, DIRECT, WIDTH), lambda t: (t, 0, 0))]
        + [pl.BlockSpec((2 * LEVELS, WIDTH), lambda t: (t, 0))] * SIDE,
        out_specs=(
            pl.BlockSpec((LEVELS + 1, 4 * SIDE, WIDTH), lambda t: (0, t, 0)),
            pl.BlockSpec((4 * SIDE, 128), lambda t: (t, 0)),
        ),
        scratch_shapes=[pltpu.VMEM((SIDE, 2 * LEVELS, WIDTH), jnp.bfloat16)],
        compiler_params=pltpu.CompilerParams(vmem_limit_bytes=24 << 20),
        name="settle",
    )(side, direct, *lasts)


def pack_direct(low, dest, cache, tiles):
    return pl.pallas_call(
        functools.partial(direct_kernel, low),
        out_shape=jax.ShapeDtypeStruct((PEERS, DIRECT, WIDTH), jnp.bfloat16),
        in_specs=[SMEM, ANY, ANY],
        out_specs=ANY,
        scratch_shapes=[
            pltpu.SMEM((PEERS,), jnp.int32),
            pltpu.VMEM((LEVELS, WIDTH), jnp.bfloat16),
            pltpu.SemaphoreType.DMA,
            pltpu.SemaphoreType.DMA,
        ],
        name="pack_direct",
    )(dest, cache, tiles)


def exchanged(x, groups=None):
    return lax.all_to_all(
        x, "sample", split_axis=0, concat_axis=0, tiled=True, axis_index_groups=groups
    )


def xor_pairs(size, bit):
    return [(i, i ^ bit) for i in range(size)]


def tree_sum(x, axis, size, bits):
    terms = [x] + [lax.ppermute(x, axis, xor_pairs(size, bit)) for bit in bits]
    while len(terms) > 1:
        terms = [terms[i] + terms[i + 1] for i in range(0, len(terms), 2)]
    return terms[0]


def bf16_terms(x):
    terms = []
    for _ in range(3):
        term = lax.reduce_precision(x, 8, 7)
        terms.append(term.astype(jnp.bfloat16))
        x = x - term
    return terms


def on_device(tokens, cache, gain, w_query, w_key, w_value, w_out, w_head, coef, chosen, dest):
    target = dest[:, 0]
    me = lax.axis_index("sample")
    y, core = lax.rem(lax.div(me, 2), 4), lax.rem(me, 2)

    relay, over = pl.pallas_call(
        relay_kernel,
        out_shape=(
            jax.ShapeDtypeStruct((PLANES, PIECE, WIDTH), jnp.bfloat16),
            jax.ShapeDtypeStruct((4, 128), jnp.float32),
        ),
        in_specs=[SMEM, ANY],
        out_specs=(ANY, pl.BlockSpec(memory_space=pltpu.VMEM)),
        scratch_shapes=[
            pltpu.SMEM((PEERS,), jnp.int32),
            pltpu.SMEM((PLANES + 1,), jnp.int32),
            pltpu.VMEM((PLANES, 8, WIDTH), jnp.float32),
            pltpu.VMEM((PLANES, PIECE, WIDTH), jnp.bfloat16),
            pltpu.SemaphoreType.DMA,
            pltpu.SemaphoreType.DMA,
        ],
        name="pack_relay",
    )(target, cache)
    relayed = exchanged(relay, [[z * SIDE + i for z in range(PLANES)] for i in range(SIDE)])

    both, logp, grad_out, grad_head = decode_rows(
        tokens, cache, coef, chosen, gain, w_query, w_key, w_value, w_out, w_head
    )
    sums = jnp.concatenate([grad_out, grad_head, over], 0)
    sums = tree_sum(sums, "rep", 4, (1, 2, 3))
    sums = tree_sum(sums, "sample", PEERS, (2, 4, 6))
    sums = tree_sum(sums, "sample", PEERS, (1,))
    share = sums.shape[0] // SIDE
    piece = lax.dynamic_slice_in_dim(sums, (y * 2 + core) * share, share, 0)
    piece = jnp.concatenate([piece, sums[-1:]], 0)
    piece = tree_sum(piece, "sample", PEERS, [SIDE * k for k in range(1, PLANES)])

    rows = jnp.arange(ROWS, dtype=jnp.int32)
    same = (target[:, None] == target[None, :]) & (rows[:, None] < rows[None, :])
    place = target * 4 + jnp.sum(same.astype(jnp.int32), 0)
    slot = (jnp.arange(4 * PEERS, dtype=jnp.int32)[:, None] == place[None, :]).astype(jnp.bfloat16)
    small = jnp.concatenate([both] + bf16_terms(logp), -1)
    slotted = jnp.dot(slot, small, preferred_element_type=jnp.float32).astype(jnp.bfloat16)
    new_rows = slotted[:, :WIDTH].reshape(PEERS, 4, WIDTH)
    logp_row = jnp.pad(
        slotted[:, WIDTH:].reshape(PEERS, 1, 4 * 3 * OUTCOMES),
        ((0, 0), (0, 3), (0, WIDTH - 12 * OUTCOMES)),
    )
    tiles = jnp.concatenate([new_rows, logp_row], 1)
    packed, piece = lax.optimization_barrier((pack_direct(0, target, cache, tiles), piece))
    direct = exchanged(packed)

    codes = relayed[:, RELAY * LEVELS, :RELAY].astype(jnp.int32)
    shifts = [(dy, dc) for dy in range(4) for dc in range(2)]
    onto = jnp.stack([lax.rem(y + dy, 4) * 2 + (core ^ dc) for dy, dc in shifts])
    came = jnp.stack([lax.rem(y - dy + 4, 4) * 2 + (core ^ dc) for dy, dc in shifts])
    onward = pl.pallas_call(
        forward_kernel,
        out_shape=[jax.ShapeDtypeStruct((LAST, WIDTH), jnp.bfloat16)] * SIDE,
        in_specs=[SMEM, SMEM, ANY],
        out_specs=[ANY] * SIDE,
        scratch_shapes=[
            pltpu.SMEM((SIDE * 2 * PLANES,), jnp.int32),
            pltpu.VMEM((LEVELS, WIDTH), jnp.bfloat16),
            pltpu.SemaphoreType.DMA((SIDE,)),
        ],
        name="pack_plane",
    )(codes, onto.astype(jnp.int32), relayed)
    def in_plane(x, k):
        dy, dc = shifts[k]
        pairs = [
            ((z * 4 + y0) * 2 + c0, (z * 4 + (y0 + dy) % 4) * 2 + (c0 ^ dc))
            for z in range(PLANES)
            for y0 in range(4)
            for c0 in range(2)
        ]
        return lax.ppermute(x, "sample", pairs)

    lasts = [onward[0]] + [in_plane(onward[k], k) for k in range(1, SIDE)]
    piece, lasts = lax.optimization_barrier((piece, lasts))
    came = came.astype(jnp.int32)
    shares = jnp.stack([piece[:share]] + [in_plane(piece[:share], k) for k in range(1, SIDE)])
    peers = jnp.arange(SIDE, dtype=jnp.int32)
    order = lax.rem(y - lax.div(peers, 2) + 4, 4) * 2 + (core ^ lax.rem(peers, 2))
    ours = (order[:, None] == peers[None, :])[..., None, None]
    grads = jnp.sum(jnp.where(ours, shares[None], 0.0), 1).reshape(sums.shape)

    def by_relay(direct, lasts):
        return settle(came, direct, lasts)

    def by_pairs(direct, lasts):
        high = exchanged(pack_direct(2, target, cache, jnp.zeros_like(tiles)))
        high = high[:, : 2 * LEVELS].reshape(PLANES, SIDE, 2 * LEVELS, WIDTH)
        high = jnp.swapaxes(high, 0, 1).reshape(SIDE, 2 * PLANES * LEVELS, WIDTH)
        high = [
            lax.dynamic_index_in_dim(high, came[k], 0, keepdims=False) for k in range(SIDE)
        ]
        return settle(came, direct, high)

    new_cache, log_probs = lax.cond(piece[share, 0] > 0, by_pairs, by_relay, direct, lasts)
    return (
        jnp.swapaxes(new_cache, 0, 1),
        log_probs[:, :OUTCOMES],
        grads[:ROWS],
        grads[ROWS : ROWS + OUTCOMES].T,
    )


def solution(mesh):
    split = P(("sample", "rep"))
    whole = P()
    return jax.shard_map(
        on_device,
        mesh=mesh,
        in_specs=(split, split) + (whole,) * 6 + (split,) * 3,
        out_specs=(split, split, whole, whole),
        check_vma=False,
    )
```

```python
import functools
import math

import jax
import jax.numpy as jnp
from jax import lax
from jax.experimental import pallas as pl
from jax.experimental.pallas import tpu as pltpu
from jax.sharding import PartitionSpec as P

HEADS = 4
OUTCOMES = 4
ROWS = 128
LEVELS = 48
WIDTH = 256
PEERS = 64
PLANES = 8
SIDE = 8
RELAY = 8
DIRECT = 2 * LEVELS + 8
PIECE = RELAY * LEVELS + 8
LAST = 2 * PLANES * LEVELS + 8
ANY = pl.BlockSpec(memory_space=pl.ANY)
SMEM = pl.BlockSpec(memory_space=pltpu.SMEM)


def decode_rows(tokens, cache, coef, chosen, gain, w_query, w_key, w_value, w_out, w_head):
    count = tokens.shape[0]
    width = tokens.shape[1]
    levels = cache.shape[1]
    size = width // HEADS
    xf = tokens.astype(jnp.float32)
    normed = (xf * lax.rsqrt(jnp.mean(xf * xf, -1, keepdims=True) + 1e-05) * gain).astype(
        jnp.bfloat16
    )
    query = (
        jnp.dot(normed, w_query, preferred_element_type=jnp.float32) * (1.0 / math.sqrt(size))
    ).astype(jnp.bfloat16)
    key_new = jnp.dot(normed, w_key, preferred_element_type=jnp.float32).astype(jnp.bfloat16)
    value_new = jnp.dot(normed, w_value, preferred_element_type=jnp.float32).astype(jnp.bfloat16)
    query_heads = query.reshape(count, HEADS, size)
    key_rows = cache[:, :, :width].reshape(count, levels, HEADS, size)
    value_rows = cache[:, :, width:].reshape(count, levels, HEADS, size)
    cached_scores = jnp.einsum(
        "yfn,yjfn->yfj", query_heads, key_rows, preferred_element_type=jnp.float32
    )
    score_self = jnp.sum(
        query_heads.astype(jnp.float32) * key_new.astype(jnp.float32).reshape(count, HEADS, size),
        -1,
    )
    top = jnp.maximum(jnp.max(cached_scores, -1), score_self)
    exp_cache = jnp.exp(cached_scores - top[..., None])
    exp_self = jnp.exp(score_self - top)
    total = jnp.sum(exp_cache, -1) + exp_self
    cached_weights = (exp_cache / total[..., None]).astype(jnp.bfloat16)
    weight_self = (exp_self / total).astype(jnp.bfloat16)
    attention_output = jnp.einsum(
        "jat,jtaf->jaf", cached_weights, value_rows, preferred_element_type=jnp.float32
    )
    attention_output = attention_output + weight_self.astype(jnp.float32)[
        ..., None
    ] * value_new.astype(jnp.float32).reshape(count, HEADS, size)
    attention_output = attention_output.reshape(count, width).astype(jnp.bfloat16)
    hidden = (xf + jnp.dot(attention_output, w_out, preferred_element_type=jnp.float32)).astype(
        jnp.bfloat16
    )
    logits = jnp.dot(hidden, w_head, preferred_element_type=jnp.float32)
    logp = jax.nn.log_softmax(logits, -1)
    picked = (chosen[:, None] == jnp.arange(OUTCOMES, dtype=jnp.int32)[None, :]).astype(jnp.float32)
    dlog = coef[:, None] * (picked - jnp.exp(logp))
    grad_head = jnp.dot(dlog.T, hidden.astype(jnp.float32), precision=lax.Precision.HIGHEST)
    hidden_gradient = jnp.dot(dlog, w_head.astype(jnp.float32).T, precision=lax.Precision.HIGHEST)
    grad_out = jnp.dot(
        attention_output.astype(jnp.float32).T, hidden_gradient, precision=lax.Precision.HIGHEST
    )
    both = jnp.concatenate([key_new, value_new], -1)
    return (both, logp, grad_out, grad_head)


def cleared(ref, count):
    @pl.loop(0, count)
    def _(i):
        ref[i] = 0


def relay_kernel(dest, cache, out, count, filled, meta, held, rows_sem, out_sem):
    cleared(count, PEERS)
    cleared(filled, PLANES + 1)
    meta[...] = jnp.full(meta.shape, -1.0, jnp.float32)
    lane = lax.broadcasted_iota(jnp.int32, (8, WIDTH), 1)

    @pl.loop(0, ROWS)
    def _(i):
        d = dest[i]
        rank = count[d]
        count[d] = rank + 1

        @pl.when(rank >= 2)
        def _():
            plane = lax.div(d, SIDE)
            at = filled[plane]
            filled[plane] = at + 1

            @pl.when(at < RELAY)
            def _():
                start = pl.multiple_of(at * LEVELS, LEVELS)
                pltpu.make_async_copy(
                    cache.at[i], held.at[plane, pl.ds(start, LEVELS)], rows_sem
                ).start()
                code = lax.rem(d, SIDE) * 2 + rank - 2
                meta[plane] = jnp.where(lane == at, code.astype(jnp.float32), meta[plane])
                filled[PLANES] += 1

    most = filled[0]
    for plane in range(1, PLANES):
        most = jnp.maximum(most, filled[plane])
    over = jnp.where(most > RELAY, 1.0, 0.0)
    for plane in range(PLANES):
        tile = jnp.where(lane == RELAY, over, meta[plane])
        held[plane, RELAY * LEVELS :, :] = tile.astype(jnp.bfloat16)

    @pl.loop(0, filled[PLANES])
    def _(i):
        pltpu.make_async_copy(cache.at[0], held.at[0, pl.ds(0, LEVELS)], rows_sem).wait()

    whole = pltpu.make_async_copy(held, out, out_sem)
    whole.start()
    whole.wait()


def direct_kernel(low, dest, cache, tiles, out, count, zero, rows_sem, tile_sem):
    cleared(count, PEERS)
    zero[...] = jnp.zeros(zero.shape, zero.dtype)
    last = pltpu.make_async_copy(tiles, out.at[:, pl.ds(2 * LEVELS, 8)], tile_sem)
    last.start()

    @pl.loop(0, ROWS)
    def _(i):
        d = dest[i]
        rank = count[d]
        count[d] = rank + 1

        @pl.when((rank >= low) & (rank < low + 2))
        def _():
            start = pl.multiple_of((rank - low) * LEVELS, LEVELS)
            pltpu.make_async_copy(cache.at[i], out.at[d, pl.ds(start, LEVELS)], rows_sem).start()

    @pl.loop(0, PEERS)
    def _(d):
        for r in range(2):

            @pl.when(count[d] <= low + r)
            def _():
                pltpu.make_async_copy(zero, out.at[d, pl.ds(r * LEVELS, LEVELS)], rows_sem).start()

    whole = out.at[:, pl.ds(0, 2 * LEVELS)]
    pltpu.make_async_copy(whole, whole, rows_sem).wait()
    last.wait()


def forward_kernel(codes, side, got, *refs):
    outs, (source, held, zero, tile, rows_sem, tile_sem, got_sem) = refs[:SIDE], refs[SIDE:]
    load = pltpu.make_async_copy(got, held, got_sem)
    load.start()
    zero[...] = jnp.zeros(zero.shape, zero.dtype)

    @pl.loop(0, SIDE * 2 * PLANES)
    def _(i):
        source[i] = -1

    over = codes[0, RELAY]
    for plane in range(PLANES):
        over = jnp.maximum(over, codes[plane, RELAY])
        for at in range(RELAY):
            code = codes[plane, at]

            @pl.when(code >= 0)
            def _():
                source[code * PLANES + plane] = at

    tile[...] = jnp.full(tile.shape, over.astype(jnp.float32)).astype(jnp.bfloat16)
    load.wait()
    for k, out in enumerate(outs):
        pltpu.make_async_copy(tile, out.at[pl.ds(LAST - 8, 8)], tile_sem.at[k]).start()
        peer = side[k]

        @pl.loop(0, 2 * PLANES)
        def _(i):
            plane = lax.div(i, 2)
            r = lax.rem(i, 2)
            at = source[(peer * 2 + r) * PLANES + plane]
            to = out.at[pl.ds(pl.multiple_of(i * LEVELS, LEVELS), LEVELS)]

            @pl.when(at >= 0)
            def _():
                start = pl.multiple_of(at * LEVELS, LEVELS)
                pltpu.make_async_copy(
                    held.at[plane, pl.ds(start, LEVELS)], to, rows_sem.at[k]
                ).start()

            @pl.when(at < 0)
            def _():
                pltpu.make_async_copy(zero, to, rows_sem.at[k]).start()

    for k, out in enumerate(outs):
        whole = out.at[pl.ds(0, LAST - 8)]
        pltpu.make_async_copy(whole, whole, rows_sem.at[k]).wait()
        pltpu.make_async_copy(tile, out.at[pl.ds(LAST - 8, 8)], tile_sem.at[k]).wait()


def flag_kernel(*refs):
    most = refs[0][...].astype(jnp.float32)
    for ref in refs[1:SIDE]:
        most = jnp.maximum(most, ref[...].astype(jnp.float32))
    refs[SIDE][0] = jnp.where(jnp.max(most) > 0, 1, 0).astype(jnp.int32)


def chosen_rows(count, size, pick):
    i = lax.broadcasted_iota(jnp.int32, (count, size), 0)
    j = lax.broadcasted_iota(jnp.int32, (count, size), 1)
    return (j == pick(i)).astype(jnp.float32).astype(jnp.bfloat16)


def settle_kernel(side, direct, *refs):
    lasts, (out, logp, held) = refs[:SIDE], refs[SIDE:]
    for k, last in enumerate(lasts):
        held[side[k]] = last[...]
    turn = chosen_rows(WIDTH, WIDTH, lambda i: lax.rem(i, 16) * 16 + lax.div(i, 16))
    for group in range(2):
        for low in range(0, LEVELS, 16):
            parts = []
            for j in range(4 * group, 4 * group + 4):
                for ref in (direct, held):
                    for r in range(2):
                        start = r * LEVELS + low
                        parts.append(ref[j, start : start + 16, :])
            turned = jnp.dot(turn, jnp.concatenate(parts, 0), preferred_element_type=jnp.float32)
            turned = turned.astype(jnp.bfloat16).reshape(16, 16, WIDTH)
            out[low : low + 16, 16 * group : 16 * group + 16, :] = turned
    tiles = jnp.concatenate([direct[j, 2 * LEVELS :, :] for j in range(SIDE)], 0)
    new = chosen_rows(4 * SIDE, 8 * SIDE, lambda i: lax.div(i, 4) * 8 + lax.rem(i, 4))
    out[LEVELS] = jnp.dot(new, tiles, preferred_element_type=jnp.float32).astype(jnp.bfloat16)
    spread = chosen_rows(4 * SIDE, 8 * SIDE, lambda i: lax.div(i, 4) * 8 + 4)
    terms = jnp.dot(spread, tiles, preferred_element_type=jnp.float32)
    slot = lax.broadcasted_iota(jnp.int32, terms.shape, 0)
    lane = lax.broadcasted_iota(jnp.int32, terms.shape, 1)
    mine = lax.div(lane, 3 * OUTCOMES) == lax.rem(slot, 4)
    terms = jnp.where(mine, terms, 0.0).astype(jnp.bfloat16)
    lane = lax.broadcasted_iota(jnp.int32, (WIDTH, 128), 0)
    outcome = lax.broadcasted_iota(jnp.int32, (WIDTH, 128), 1)
    gather = (lax.rem(lane, OUTCOMES) == outcome).astype(jnp.float32).astype(jnp.bfloat16)
    logp[...] = jnp.dot(terms, gather, preferred_element_type=jnp.float32)


def settle(side, direct, lasts):
    return pl.pallas_call(
        settle_kernel,
        grid=(PLANES,),
        out_shape=(
            jax.ShapeDtypeStruct((LEVELS + 1, 4 * PEERS, WIDTH), jnp.bfloat16),
            jax.ShapeDtypeStruct((4 * PEERS, 128), jnp.float32),
        ),
        in_specs=[SMEM, pl.BlockSpec((SIDE, DIRECT, WIDTH), lambda t: (t, 0, 0))]
        + [pl.BlockSpec((2 * LEVELS, WIDTH), lambda t: (t, 0))] * SIDE,
        out_specs=(
            pl.BlockSpec((LEVELS + 1, 4 * SIDE, WIDTH), lambda t: (0, t, 0)),
            pl.BlockSpec((4 * SIDE, 128), lambda t: (t, 0)),
        ),
        scratch_shapes=[pltpu.VMEM((SIDE, 2 * LEVELS, WIDTH), jnp.bfloat16)],
        compiler_params=pltpu.CompilerParams(vmem_limit_bytes=24 << 20),
        cost_estimate=pl.CostEstimate(flops=2 << 30, bytes_accessed=14 << 20, transcendentals=0),
        name="settle",
    )(side, direct, *lasts)


def pack_direct(low, dest, cache, tiles):
    return pl.pallas_call(
        functools.partial(direct_kernel, low),
        out_shape=jax.ShapeDtypeStruct((PEERS, DIRECT, WIDTH), jnp.bfloat16),
        in_specs=[SMEM, ANY, ANY],
        out_specs=ANY,
        scratch_shapes=[
            pltpu.SMEM((PEERS,), jnp.int32),
            pltpu.VMEM((LEVELS, WIDTH), jnp.bfloat16),
            pltpu.SemaphoreType.DMA,
            pltpu.SemaphoreType.DMA,
        ],
        cost_estimate=pl.CostEstimate(flops=0, bytes_accessed=10 << 20, transcendentals=0),
        name="pack_direct",
    )(dest, cache, tiles)


def exchanged(x, groups=None):
    return lax.all_to_all(
        x, "sample", split_axis=0, concat_axis=0, tiled=True, axis_index_groups=groups
    )


def xor_pairs(size, bit):
    return [(i, i ^ bit) for i in range(size)]


def tree_sum(x, axis, size, bits):
    terms = [x] + [lax.ppermute(x, axis, xor_pairs(size, bit)) for bit in bits]
    while len(terms) > 1:
        terms = [terms[i] + terms[i + 1] for i in range(0, len(terms), 2)]
    return terms[0]


def bf16_terms(x):
    terms = []
    for _ in range(3):
        term = lax.reduce_precision(x, 8, 7)
        terms.append(term.astype(jnp.bfloat16))
        x = x - term
    return terms


def on_device(tokens, cache, gain, w_query, w_key, w_value, w_out, w_head, coef, chosen, dest):
    target = dest[:, 0]
    me = lax.axis_index("sample")
    y, core = lax.rem(lax.div(me, 2), 4), lax.rem(me, 2)

    relay = pl.pallas_call(
        relay_kernel,
        out_shape=jax.ShapeDtypeStruct((PLANES, PIECE, WIDTH), jnp.bfloat16),
        in_specs=[SMEM, ANY],
        out_specs=ANY,
        scratch_shapes=[
            pltpu.SMEM((PEERS,), jnp.int32),
            pltpu.SMEM((PLANES + 1,), jnp.int32),
            pltpu.VMEM((PLANES, 8, WIDTH), jnp.float32),
            pltpu.VMEM((PLANES, PIECE, WIDTH), jnp.bfloat16),
            pltpu.SemaphoreType.DMA,
            pltpu.SemaphoreType.DMA,
        ],
        name="pack_relay",
    )(target, cache)
    relayed = exchanged(relay, [[z * SIDE + i for z in range(PLANES)] for i in range(SIDE)])

    both, logp, grad_out, grad_head = decode_rows(
        tokens, cache, coef, chosen, gain, w_query, w_key, w_value, w_out, w_head
    )
    sums = jnp.pad(jnp.concatenate([grad_out, grad_head], 0), ((0, OUTCOMES), (0, 0)))
    sums = tree_sum(sums, "rep", 4, (1, 2, 3))
    sums = tree_sum(sums, "sample", PEERS, (2, 4, 6))
    sums = tree_sum(sums, "sample", PEERS, (1,))
    share = sums.shape[0] // 4
    piece = lax.dynamic_slice_in_dim(sums, y * share, share, 0)

    rows = jnp.arange(ROWS, dtype=jnp.int32)
    same = (target[:, None] == target[None, :]) & (rows[:, None] < rows[None, :])
    place = target * 4 + jnp.sum(same.astype(jnp.int32), 0)
    slot = (jnp.arange(4 * PEERS, dtype=jnp.int32)[:, None] == place[None, :]).astype(jnp.bfloat16)
    small = jnp.concatenate([both] + bf16_terms(logp), -1)
    slotted = jnp.dot(slot, small, preferred_element_type=jnp.float32).astype(jnp.bfloat16)
    new_rows = slotted[:, :WIDTH].reshape(PEERS, 4, WIDTH)
    logp_row = jnp.pad(
        slotted[:, WIDTH:].reshape(PEERS, 1, 4 * 3 * OUTCOMES),
        ((0, 0), (0, 3), (0, WIDTH - 12 * OUTCOMES)),
    )
    tiles = jnp.concatenate([new_rows, logp_row], 1)
    packed, piece = lax.optimization_barrier((pack_direct(0, target, cache, tiles), piece))
    direct = exchanged(packed)

    codes = relayed[:, RELAY * LEVELS, : 2 * RELAY].astype(jnp.int32)
    shifts = [(dy, dc) for dy in range(4) for dc in range(2)]
    onto = jnp.stack([lax.rem(y + dy, 4) * 2 + (core ^ dc) for dy, dc in shifts])
    came = jnp.stack([lax.rem(y - dy + 4, 4) * 2 + (core ^ dc) for dy, dc in shifts])
    onward = pl.pallas_call(
        forward_kernel,
        out_shape=[jax.ShapeDtypeStruct((LAST, WIDTH), jnp.bfloat16)] * SIDE,
        in_specs=[SMEM, SMEM, ANY],
        out_specs=[ANY] * SIDE,
        scratch_shapes=[
            pltpu.SMEM((SIDE * 2 * PLANES,), jnp.int32),
            pltpu.VMEM((PLANES, PIECE, WIDTH), jnp.bfloat16),
            pltpu.VMEM((LEVELS, WIDTH), jnp.bfloat16),
            pltpu.VMEM((8, WIDTH), jnp.bfloat16),
            pltpu.SemaphoreType.DMA((SIDE,)),
            pltpu.SemaphoreType.DMA((SIDE,)),
            pltpu.SemaphoreType.DMA,
        ],
        cost_estimate=pl.CostEstimate(flops=0, bytes_accessed=5 << 20, transcendentals=0),
        name="pack_plane",
    )(codes, onto.astype(jnp.int32), relayed)
    def in_plane(x, k):
        dy, dc = shifts[k]
        pairs = [
            ((z * 4 + y0) * 2 + c0, (z * 4 + (y0 + dy) % 4) * 2 + (c0 ^ dc))
            for z in range(PLANES)
            for y0 in range(4)
            for c0 in range(2)
        ]
        return lax.ppermute(x, "sample", pairs)

    lasts = [onward[0]] + [in_plane(onward[k], k) for k in range(1, SIDE)]
    piece, lasts = lax.optimization_barrier((piece, lasts))
    came = came.astype(jnp.int32)
    piece = tree_sum(piece, "sample", PEERS, [SIDE * k for k in range(1, PLANES)])
    over = pl.pallas_call(
        flag_kernel,
        grid=(1,),
        out_shape=jax.ShapeDtypeStruct((1,), jnp.int32),
        in_specs=[pl.BlockSpec((8, 128), lambda t: (LAST // 8 - 1, 0))] * SIDE,
        out_specs=SMEM,
        name="flag",
    )(*lasts)

    def by_relay(lasts):
        return lasts

    def by_pairs(lasts):
        high = exchanged(pack_direct(2, target, cache, jnp.zeros_like(tiles)))
        high = high[:, : 2 * LEVELS].reshape(PLANES, SIDE, 2 * LEVELS, WIDTH)
        high = jnp.swapaxes(high, 0, 1).reshape(SIDE, 2 * PLANES * LEVELS, WIDTH)
        high = jnp.pad(high, ((0, 0), (0, LAST - 2 * PLANES * LEVELS), (0, 0)))
        return [lax.dynamic_index_in_dim(high, came[k], 0, keepdims=False) for k in range(SIDE)]

    direct, lasts, piece = lax.optimization_barrier((direct, lasts, piece))
    lasts = lax.cond(over[0] > 0, by_pairs, by_relay, lasts)
    piece, lasts = lax.optimization_barrier((piece, lasts))
    shares = jnp.stack([piece] + [in_plane(piece, k) for k in range(2, SIDE, 2)])
    rows_y = jnp.arange(4, dtype=jnp.int32)
    ours = (lax.rem(y - rows_y + 4, 4)[:, None] == rows_y[None, :])[..., None, None]
    grads = jnp.sum(jnp.where(ours, shares[None], 0.0), 1).reshape(sums.shape)
    new_cache, log_probs = settle(came, direct, lasts)
    return (
        jnp.swapaxes(new_cache, 0, 1),
        log_probs[:, :OUTCOMES],
        grads[:ROWS],
        grads[ROWS : ROWS + OUTCOMES].T,
    )


def solution(mesh):
    split = P(("sample", "rep"))
    whole = P()
    return jax.shard_map(
        on_device,
        mesh=mesh,
        in_specs=(split, split) + (whole,) * 6 + (split,) * 3,
        out_specs=(split, split, whole, whole),
        check_vma=False,
    )
```

```python
import functools
import math

import jax
import jax.numpy as jnp
from jax import lax
from jax.experimental import pallas as pl
from jax.experimental.pallas import tpu as pltpu
from jax.sharding import PartitionSpec as P

HEADS = 4
OUTCOMES = 4
HEAD = 64
ROWS = 128
LEVELS = 48
WIDTH = 256
PEERS = 64
PLANES = 8
SIDE = 8
RELAY = 8
DIRECT = 2 * LEVELS + 8
PIECE = RELAY * LEVELS + 8
LAST = 2 * PLANES * LEVELS + 8
ANY = pl.BlockSpec(memory_space=pl.ANY)
SMEM = pl.BlockSpec(memory_space=pltpu.SMEM)


def decode_rows(tokens, cache, coef, chosen, gain, w_query, w_key, w_value, w_out, w_head):
    count = tokens.shape[0]
    width = tokens.shape[1]
    levels = cache.shape[1]
    size = width // HEADS
    xf = tokens.astype(jnp.float32)
    normed = (xf * lax.rsqrt(jnp.mean(xf * xf, -1, keepdims=True) + 1e-05) * gain).astype(
        jnp.bfloat16
    )
    query = (
        jnp.dot(normed, w_query, preferred_element_type=jnp.float32) * (1.0 / math.sqrt(size))
    ).astype(jnp.bfloat16)
    key_new = jnp.dot(normed, w_key, preferred_element_type=jnp.float32).astype(jnp.bfloat16)
    value_new = jnp.dot(normed, w_value, preferred_element_type=jnp.float32).astype(jnp.bfloat16)
    query_heads = query.reshape(count, HEADS, size)
    key_rows = cache[:, :, :width].reshape(count, levels, HEADS, size)
    value_rows = cache[:, :, width:].reshape(count, levels, HEADS, size)
    cached_scores = jnp.einsum(
        "yfn,yjfn->yfj", query_heads, key_rows, preferred_element_type=jnp.float32
    )
    score_self = jnp.sum(
        query_heads.astype(jnp.float32) * key_new.astype(jnp.float32).reshape(count, HEADS, size),
        -1,
    )
    top = jnp.maximum(jnp.max(cached_scores, -1), score_self)
    exp_cache = jnp.exp(cached_scores - top[..., None])
    exp_self = jnp.exp(score_self - top)
    total = jnp.sum(exp_cache, -1) + exp_self
    cached_weights = (exp_cache / total[..., None]).astype(jnp.bfloat16)
    weight_self = (exp_self / total).astype(jnp.bfloat16)
    attention_output = jnp.einsum(
        "jat,jtaf->jaf", cached_weights, value_rows, preferred_element_type=jnp.float32
    )
    attention_output = attention_output + weight_self.astype(jnp.float32)[
        ..., None
    ] * value_new.astype(jnp.float32).reshape(count, HEADS, size)
    attention_output = attention_output.reshape(count, width).astype(jnp.bfloat16)
    hidden = (xf + jnp.dot(attention_output, w_out, preferred_element_type=jnp.float32)).astype(
        jnp.bfloat16
    )
    logits = jnp.dot(hidden, w_head, preferred_element_type=jnp.float32)
    logp = jax.nn.log_softmax(logits, -1)
    picked = (chosen[:, None] == jnp.arange(OUTCOMES, dtype=jnp.int32)[None, :]).astype(jnp.float32)
    dlog = coef[:, None] * (picked - jnp.exp(logp))
    grad_head = jnp.dot(dlog.T, hidden.astype(jnp.float32), precision=lax.Precision.HIGHEST)
    hidden_gradient = jnp.dot(dlog, w_head.astype(jnp.float32).T, precision=lax.Precision.HIGHEST)
    grad_out = jnp.dot(
        attention_output.astype(jnp.float32).T, hidden_gradient, precision=lax.Precision.HIGHEST
    )
    both = jnp.concatenate([key_new, value_new], -1)
    return (both, logp, grad_out, grad_head)


def cleared(ref, count):
    @pl.loop(0, count)
    def _(i):
        ref[i] = 0


def relay_kernel(dest, cache, out, count, filled, meta, held, rows_sem, out_sem):
    cleared(count, PEERS)
    cleared(filled, PLANES + 1)
    meta[...] = jnp.full(meta.shape, -1.0, jnp.float32)
    lane = lax.broadcasted_iota(jnp.int32, (8, WIDTH), 1)

    @pl.loop(0, ROWS)
    def _(i):
        d = dest[i]
        rank = count[d]
        count[d] = rank + 1

        @pl.when(rank >= 2)
        def _():
            plane = lax.div(d, SIDE)
            at = filled[plane]
            filled[plane] = at + 1

            @pl.when(at < RELAY)
            def _():
                start = pl.multiple_of(at * LEVELS, LEVELS)
                pltpu.make_async_copy(
                    cache.at[i], held.at[plane, pl.ds(start, LEVELS)], rows_sem
                ).start()
                code = lax.rem(d, SIDE) * 2 + rank - 2
                meta[plane] = jnp.where(lane == at, code.astype(jnp.float32), meta[plane])
                filled[PLANES] += 1

    most = filled[0]
    for plane in range(1, PLANES):
        most = jnp.maximum(most, filled[plane])
    over = jnp.where(most > RELAY, 1.0, 0.0)
    for plane in range(PLANES):
        tile = jnp.where(lane == RELAY, over, meta[plane])
        held[plane, RELAY * LEVELS :, :] = tile.astype(jnp.bfloat16)

    @pl.loop(0, filled[PLANES])
    def _(i):
        pltpu.make_async_copy(cache.at[0], held.at[0, pl.ds(0, LEVELS)], rows_sem).wait()

    whole = pltpu.make_async_copy(held, out, out_sem)
    whole.start()
    whole.wait()


def direct_kernel(low, dest, cache, out, count, zero, rows_sem):
    cleared(count, PEERS)
    zero[...] = jnp.zeros(zero.shape, zero.dtype)

    @pl.loop(0, ROWS)
    def _(i):
        d = dest[i]
        rank = count[d]
        count[d] = rank + 1

        @pl.when((rank >= low) & (rank < low + 2))
        def _():
            start = pl.multiple_of((rank - low) * LEVELS, LEVELS)
            pltpu.make_async_copy(cache.at[i], out.at[d, pl.ds(start, LEVELS)], rows_sem).start()

    @pl.loop(0, PEERS)
    def _(d):
        for r in range(2):

            @pl.when(count[d] <= low + r)
            def _():
                pltpu.make_async_copy(zero, out.at[d, pl.ds(r * LEVELS, LEVELS)], rows_sem).start()

    whole = out.at[:, pl.ds(0, 2 * LEVELS)]
    pltpu.make_async_copy(whole, whole, rows_sem).wait()


def tile_kernel(tiles, rows, out, sem):
    copy = pltpu.make_async_copy(tiles, out.at[:, pl.ds(2 * LEVELS, 8)], sem)
    copy.start()
    copy.wait()


def plane_sum_kernel(tiles, out, head):
    x = jnp.sum(tiles[...].astype(jnp.float32).reshape(PLANES, SIDE, 8, WIDTH), 0)
    out[...] = x[:, 5, :] + (x[:, 6, :] + x[:, 7, :])
    head[...] = x[:, 4, :]


def forward_kernel(codes, side, got, *refs):
    outs, (source, held, zero, tile, rows_sem, tile_sem, got_sem) = refs[:SIDE], refs[SIDE:]
    load = pltpu.make_async_copy(got, held, got_sem)
    load.start()
    zero[...] = jnp.zeros(zero.shape, zero.dtype)

    @pl.loop(0, SIDE * 2 * PLANES)
    def _(i):
        source[i] = -1

    over = codes[0, RELAY]
    for plane in range(PLANES):
        over = jnp.maximum(over, codes[plane, RELAY])
        for at in range(RELAY):
            code = codes[plane, at]

            @pl.when(code >= 0)
            def _():
                source[code * PLANES + plane] = at

    tile[...] = jnp.full(tile.shape, over.astype(jnp.float32)).astype(jnp.bfloat16)
    load.wait()
    for k, out in enumerate(outs):
        pltpu.make_async_copy(tile, out.at[pl.ds(LAST - 8, 8)], tile_sem.at[k]).start()
        peer = side[k]

        @pl.loop(0, 2 * PLANES)
        def _(i):
            plane = lax.div(i, 2)
            r = lax.rem(i, 2)
            at = source[(peer * 2 + r) * PLANES + plane]
            to = out.at[pl.ds(pl.multiple_of(i * LEVELS, LEVELS), LEVELS)]

            @pl.when(at >= 0)
            def _():
                start = pl.multiple_of(at * LEVELS, LEVELS)
                pltpu.make_async_copy(
                    held.at[plane, pl.ds(start, LEVELS)], to, rows_sem.at[k]
                ).start()

            @pl.when(at < 0)
            def _():
                pltpu.make_async_copy(zero, to, rows_sem.at[k]).start()

    for k, out in enumerate(outs):
        whole = out.at[pl.ds(0, LAST - 8)]
        pltpu.make_async_copy(whole, whole, rows_sem.at[k]).wait()
        pltpu.make_async_copy(tile, out.at[pl.ds(LAST - 8, 8)], tile_sem.at[k]).wait()


def flag_kernel(*refs):
    most = refs[0][...].astype(jnp.float32)
    for ref in refs[1:SIDE]:
        most = jnp.maximum(most, ref[...].astype(jnp.float32))
    refs[SIDE][0] = jnp.where(jnp.max(most) > 0, 1, 0).astype(jnp.int32)


def chosen_rows(count, size, pick):
    i = lax.broadcasted_iota(jnp.int32, (count, size), 0)
    j = lax.broadcasted_iota(jnp.int32, (count, size), 1)
    return (j == pick(i)).astype(jnp.float32).astype(jnp.bfloat16)


def settle_kernel(side, direct, *refs):
    lasts, (out, logp, held) = refs[:SIDE], refs[SIDE:]
    for k, last in enumerate(lasts):
        held[side[k]] = last[...]
    turn = chosen_rows(WIDTH, WIDTH, lambda i: lax.rem(i, 16) * 16 + lax.div(i, 16))
    for group in range(2):
        for low in range(0, LEVELS, 16):
            parts = []
            for j in range(4 * group, 4 * group + 4):
                for ref in (direct, held):
                    for r in range(2):
                        start = r * LEVELS + low
                        parts.append(ref[j, start : start + 16, :])
            turned = jnp.dot(turn, jnp.concatenate(parts, 0), preferred_element_type=jnp.float32)
            turned = turned.astype(jnp.bfloat16).reshape(16, 16, WIDTH)
            out[low : low + 16, 16 * group : 16 * group + 16, :] = turned
    tiles = jnp.concatenate([direct[j, 2 * LEVELS :, :] for j in range(SIDE)], 0)
    new = chosen_rows(4 * SIDE, 8 * SIDE, lambda i: lax.div(i, 4) * 8 + lax.rem(i, 4))
    out[LEVELS] = jnp.dot(new, tiles, preferred_element_type=jnp.float32).astype(jnp.bfloat16)
    spread = chosen_rows(4 * SIDE, 8 * SIDE, lambda i: lax.div(i, 4) * 8 + 4)
    terms = jnp.dot(spread, tiles, preferred_element_type=jnp.float32)
    slot = lax.broadcasted_iota(jnp.int32, terms.shape, 0)
    lane = lax.broadcasted_iota(jnp.int32, terms.shape, 1)
    mine = lax.div(lane, 3 * OUTCOMES) == lax.rem(slot, 4)
    terms = jnp.where(mine, terms, 0.0).astype(jnp.bfloat16)
    lane = lax.broadcasted_iota(jnp.int32, (WIDTH, 128), 0)
    outcome = lax.broadcasted_iota(jnp.int32, (WIDTH, 128), 1)
    gather = (lax.rem(lane, OUTCOMES) == outcome).astype(jnp.float32).astype(jnp.bfloat16)
    logp[...] = jnp.dot(terms, gather, preferred_element_type=jnp.float32)


def settle(side, direct, lasts):
    return pl.pallas_call(
        settle_kernel,
        grid=(PLANES,),
        out_shape=(
            jax.ShapeDtypeStruct((LEVELS + 1, 4 * PEERS, WIDTH), jnp.bfloat16),
            jax.ShapeDtypeStruct((4 * PEERS, 128), jnp.float32),
        ),
        in_specs=[SMEM, pl.BlockSpec((SIDE, DIRECT, WIDTH), lambda t: (t, 0, 0))]
        + [pl.BlockSpec((2 * LEVELS, WIDTH), lambda t: (t, 0))] * SIDE,
        out_specs=(
            pl.BlockSpec((LEVELS + 1, 4 * SIDE, WIDTH), lambda t: (0, t, 0)),
            pl.BlockSpec((4 * SIDE, 128), lambda t: (t, 0)),
        ),
        scratch_shapes=[pltpu.VMEM((SIDE, 2 * LEVELS, WIDTH), jnp.bfloat16)],
        compiler_params=pltpu.CompilerParams(vmem_limit_bytes=24 << 20),
        cost_estimate=pl.CostEstimate(flops=2 << 30, bytes_accessed=14 << 20, transcendentals=0),
        name="settle",
    )(side, direct, *lasts)


def pack_direct(low, dest, cache):
    return pl.pallas_call(
        functools.partial(direct_kernel, low),
        out_shape=jax.ShapeDtypeStruct((PEERS, DIRECT, WIDTH), jnp.bfloat16),
        in_specs=[SMEM, ANY],
        out_specs=ANY,
        scratch_shapes=[
            pltpu.SMEM((PEERS,), jnp.int32),
            pltpu.VMEM((LEVELS, WIDTH), jnp.bfloat16),
            pltpu.SemaphoreType.DMA,
        ],
        cost_estimate=pl.CostEstimate(flops=0, bytes_accessed=10 << 20, transcendentals=0),
        name="pack_direct",
    )(dest, cache)


def exchanged(x, groups=None):
    return lax.all_to_all(
        x, "sample", split_axis=0, concat_axis=0, tiled=True, axis_index_groups=groups
    )


def xor_pairs(size, bit):
    return [(i, i ^ bit) for i in range(size)]


def tree_sum(x, axis, size, bits):
    terms = [x] + [lax.ppermute(x, axis, xor_pairs(size, bit)) for bit in bits]
    while len(terms) > 1:
        terms = [terms[i] + terms[i + 1] for i in range(0, len(terms), 2)]
    return terms[0]


def bf16_terms(x):
    terms = []
    for _ in range(3):
        term = lax.reduce_precision(x, 8, 7)
        terms.append(term.astype(jnp.bfloat16))
        x = x - term
    return terms


def on_device(tokens, cache, gain, w_query, w_key, w_value, w_out, w_head, coef, chosen, dest):
    target = dest[:, 0]
    me = lax.axis_index("sample")
    y, core = lax.rem(lax.div(me, 2), 4), lax.rem(me, 2)

    relay = pl.pallas_call(
        relay_kernel,
        out_shape=jax.ShapeDtypeStruct((PLANES, PIECE, WIDTH), jnp.bfloat16),
        in_specs=[SMEM, ANY],
        out_specs=ANY,
        scratch_shapes=[
            pltpu.SMEM((PEERS,), jnp.int32),
            pltpu.SMEM((PLANES + 1,), jnp.int32),
            pltpu.VMEM((PLANES, 8, WIDTH), jnp.float32),
            pltpu.VMEM((PLANES, PIECE, WIDTH), jnp.bfloat16),
            pltpu.SemaphoreType.DMA,
            pltpu.SemaphoreType.DMA,
        ],
        name="pack_relay",
    )(target, cache)
    relayed = exchanged(relay, [[z * SIDE + i for z in range(PLANES)] for i in range(SIDE)])

    both, logp, grad_out, grad_head = decode_rows(
        tokens, cache, coef, chosen, gain, w_query, w_key, w_value, w_out, w_head
    )
    sums = jnp.concatenate([grad_out, grad_head], 0)
    target_now, sums = lax.optimization_barrier((target, sums))
    packed = pack_direct(0, target_now, cache)
    sums = tree_sum(sums, "rep", 4, (1, 2, 3))
    packed, sums = lax.optimization_barrier((packed, sums))
    sums = tree_sum(sums, "sample", PEERS, (2, 4, 6))
    sums = tree_sum(sums, "sample", PEERS, (1,))
    rows = jnp.arange(ROWS, dtype=jnp.int32)
    same = (target[:, None] == target[None, :]) & (rows[:, None] < rows[None, :])
    place = target * 4 + jnp.sum(same.astype(jnp.int32), 0)
    slot = (jnp.arange(4 * PEERS, dtype=jnp.int32)[:, None] == place[None, :]).astype(jnp.bfloat16)
    small = jnp.concatenate([both] + bf16_terms(logp), -1)
    slotted = jnp.dot(slot, small, preferred_element_type=jnp.float32).astype(jnp.bfloat16)
    new_rows = slotted[:, :WIDTH].reshape(PEERS, 4, WIDTH)
    mine = y * 2 + core
    share = sums[:ROWS].reshape(SIDE, SIDE, WIDTH)
    share = lax.dynamic_index_in_dim(share, mine, 1, keepdims=False)
    share = jnp.stack(bf16_terms(share), 1)[None]
    share = jnp.broadcast_to(share, (PLANES, SIDE, 3, WIDTH)).reshape(PEERS, 3, WIDTH)
    head = sums[ROWS:].reshape(SIDE, HEAD)
    head = lax.dynamic_index_in_dim(head, mine, 0, keepdims=False)
    head = jnp.broadcast_to(jnp.concatenate(bf16_terms(head)), (PEERS, 3 * HEAD))
    logp_row = slotted[:, WIDTH:].reshape(PEERS, 12 * OUTCOMES)
    gap = jnp.zeros((PEERS, WIDTH - 12 * OUTCOMES - 3 * HEAD), jnp.bfloat16)
    mixed = jnp.concatenate([logp_row, gap, head], -1)[:, None]
    tiles = jnp.concatenate([new_rows, mixed, share], 1)
    packed = pl.pallas_call(
        tile_kernel,
        out_shape=jax.ShapeDtypeStruct(packed.shape, packed.dtype),
        in_specs=[ANY, ANY],
        out_specs=ANY,
        scratch_shapes=[pltpu.SemaphoreType.DMA],
        input_output_aliases={1: 0},
        name="pack_tiles",
    )(tiles, packed)
    direct = exchanged(packed)

    codes = relayed[:, RELAY * LEVELS, : 2 * RELAY].astype(jnp.int32)
    shifts = [(dy, dc) for dy in range(4) for dc in range(2)]
    onto = jnp.stack([lax.rem(y + dy, 4) * 2 + (core ^ dc) for dy, dc in shifts])
    came = jnp.stack([lax.rem(y - dy + 4, 4) * 2 + (core ^ dc) for dy, dc in shifts])
    onward = pl.pallas_call(
        forward_kernel,
        out_shape=[jax.ShapeDtypeStruct((LAST, WIDTH), jnp.bfloat16)] * SIDE,
        in_specs=[SMEM, SMEM, ANY],
        out_specs=[ANY] * SIDE,
        scratch_shapes=[
            pltpu.SMEM((SIDE * 2 * PLANES,), jnp.int32),
            pltpu.VMEM((PLANES, PIECE, WIDTH), jnp.bfloat16),
            pltpu.VMEM((LEVELS, WIDTH), jnp.bfloat16),
            pltpu.VMEM((8, WIDTH), jnp.bfloat16),
            pltpu.SemaphoreType.DMA((SIDE,)),
            pltpu.SemaphoreType.DMA((SIDE,)),
            pltpu.SemaphoreType.DMA,
        ],
        cost_estimate=pl.CostEstimate(flops=0, bytes_accessed=5 << 20, transcendentals=0),
        name="pack_plane",
    )(codes, onto.astype(jnp.int32), relayed)
    def in_plane(x, k):
        dy, dc = shifts[k]
        pairs = [
            ((z * 4 + y0) * 2 + c0, (z * 4 + (y0 + dy) % 4) * 2 + (c0 ^ dc))
            for z in range(PLANES)
            for y0 in range(4)
            for c0 in range(2)
        ]
        return lax.ppermute(x, "sample", pairs)

    lasts = [onward[0]] + [in_plane(onward[k], k) for k in range(1, SIDE)]
    came = came.astype(jnp.int32)
    over = pl.pallas_call(
        flag_kernel,
        grid=(1,),
        out_shape=jax.ShapeDtypeStruct((1,), jnp.int32),
        in_specs=[pl.BlockSpec((8, 128), lambda t: (LAST // 8 - 1, 0))] * SIDE,
        out_specs=SMEM,
        name="flag",
    )(*lasts)

    def by_relay(lasts):
        return lasts

    def by_pairs(lasts):
        high = exchanged(pack_direct(2, target, cache))
        high = high[:, : 2 * LEVELS].reshape(PLANES, SIDE, 2 * LEVELS, WIDTH)
        high = jnp.swapaxes(high, 0, 1).reshape(SIDE, 2 * PLANES * LEVELS, WIDTH)
        high = jnp.pad(high, ((0, 0), (0, LAST - 2 * PLANES * LEVELS), (0, 0)))
        return [lax.dynamic_index_in_dim(high, came[k], 0, keepdims=False) for k in range(SIDE)]

    piece, head = pl.pallas_call(
        plane_sum_kernel,
        grid=(1,),
        out_shape=(jax.ShapeDtypeStruct((SIDE, WIDTH), jnp.float32),) * 2,
        in_specs=[pl.BlockSpec((PEERS, 8, WIDTH), lambda t: (0, 2 * LEVELS // 8, 0))],
        out_specs=(pl.BlockSpec((SIDE, WIDTH), lambda t: (0, 0)),) * 2,
        name="plane_sum",
    )(direct)
    piece = piece.reshape(2 * SIDE, ROWS)
    other = lax.ppermute(piece, "sample", xor_pairs(PEERS, 1))
    piece = jnp.where(
        core == 0, jnp.concatenate([piece, other], 0), jnp.concatenate([other, piece], 0)
    )
    direct, lasts, piece = lax.optimization_barrier((direct, lasts, piece))
    lasts = lax.cond(over[0] > 0, by_pairs, by_relay, lasts)
    piece, lasts = lax.optimization_barrier((piece, lasts))
    shares = jnp.stack([piece] + [in_plane(piece, k) for k in range(2, SIDE, 2)])
    rows_y = jnp.arange(4, dtype=jnp.int32)
    ours = (lax.rem(y - rows_y + 4, 4)[:, None] == rows_y[None, :])[..., None, None]
    grad_out = jnp.sum(jnp.where(ours, shares[None], 0.0), 1).reshape(ROWS, ROWS)
    head = head[:, WIDTH - 3 * HEAD :].reshape(SIDE, 3, HEAD)
    grad_head = (head[:, 0] + (head[:, 1] + head[:, 2])).reshape(OUTCOMES, ROWS).T
    new_cache, log_probs = settle(came, direct, lasts)
    return (jnp.swapaxes(new_cache, 0, 1), log_probs[:, :OUTCOMES], grad_out, grad_head)


def solution(mesh):
    split = P(("sample", "rep"))
    whole = P()
    return jax.shard_map(
        on_device,
        mesh=mesh,
        in_specs=(split, split) + (whole,) * 6 + (split,) * 3,
        out_specs=(split, split, whole, whole),
        check_vma=False,
    )
```

```python
import functools
import math

import jax
import jax.numpy as jnp
from jax import lax
from jax.experimental import pallas as pl
from jax.experimental.pallas import tpu as pltpu
from jax.sharding import PartitionSpec as P

HEADS = 4
OUTCOMES = 4
HEAD = 64
ROWS = 128
LEVELS = 48
WIDTH = 256
PEERS = 64
PLANES = 8
SIDE = 8
RELAY = 8
DIRECT = 2 * LEVELS + 8
PIECE = RELAY * LEVELS + 8
LAST = 2 * PLANES * LEVELS + 8
ANY = pl.BlockSpec(memory_space=pl.ANY)
SMEM = pl.BlockSpec(memory_space=pltpu.SMEM)


def decode_rows(tokens, cache, coef, chosen, gain, w_query, w_key, w_value, w_out, w_head):
    count = tokens.shape[0]
    width = tokens.shape[1]
    levels = cache.shape[1]
    size = width // HEADS
    xf = tokens.astype(jnp.float32)
    normed = (xf * lax.rsqrt(jnp.mean(xf * xf, -1, keepdims=True) + 1e-05) * gain).astype(
        jnp.bfloat16
    )
    query = (
        jnp.dot(normed, w_query, preferred_element_type=jnp.float32) * (1.0 / math.sqrt(size))
    ).astype(jnp.bfloat16)
    key_new = jnp.dot(normed, w_key, preferred_element_type=jnp.float32).astype(jnp.bfloat16)
    value_new = jnp.dot(normed, w_value, preferred_element_type=jnp.float32).astype(jnp.bfloat16)
    query_heads = query.reshape(count, HEADS, size)
    key_rows = cache[:, :, :width].reshape(count, levels, HEADS, size)
    value_rows = cache[:, :, width:].reshape(count, levels, HEADS, size)
    cached_scores = jnp.einsum(
        "yfn,yjfn->yfj", query_heads, key_rows, preferred_element_type=jnp.float32
    )
    score_self = jnp.sum(
        query_heads.astype(jnp.float32) * key_new.astype(jnp.float32).reshape(count, HEADS, size),
        -1,
    )
    top = jnp.maximum(jnp.max(cached_scores, -1), score_self)
    exp_cache = jnp.exp(cached_scores - top[..., None])
    exp_self = jnp.exp(score_self - top)
    total = jnp.sum(exp_cache, -1) + exp_self
    cached_weights = (exp_cache / total[..., None]).astype(jnp.bfloat16)
    weight_self = (exp_self / total).astype(jnp.bfloat16)
    attention_output = jnp.einsum(
        "jat,jtaf->jaf", cached_weights, value_rows, preferred_element_type=jnp.float32
    )
    attention_output = attention_output + weight_self.astype(jnp.float32)[
        ..., None
    ] * value_new.astype(jnp.float32).reshape(count, HEADS, size)
    attention_output = attention_output.reshape(count, width).astype(jnp.bfloat16)
    hidden = (xf + jnp.dot(attention_output, w_out, preferred_element_type=jnp.float32)).astype(
        jnp.bfloat16
    )
    logits = jnp.dot(hidden, w_head, preferred_element_type=jnp.float32)
    logp = jax.nn.log_softmax(logits, -1)
    picked = (chosen[:, None] == jnp.arange(OUTCOMES, dtype=jnp.int32)[None, :]).astype(jnp.float32)
    dlog = coef[:, None] * (picked - jnp.exp(logp))
    grad_head = jnp.dot(dlog.T, hidden.astype(jnp.float32), precision=lax.Precision.HIGHEST)
    hidden_gradient = jnp.dot(dlog, w_head.astype(jnp.float32).T, precision=lax.Precision.HIGHEST)
    grad_out = jnp.dot(
        attention_output.astype(jnp.float32).T, hidden_gradient, precision=lax.Precision.HIGHEST
    )
    both = jnp.concatenate([key_new, value_new], -1)
    return (both, logp, grad_out, grad_head)


def cleared(ref, count):
    @pl.loop(0, count)
    def _(i):
        ref[i] = 0


def relay_kernel(dest, cache, out, count, filled, meta, held, rows_sem, out_sem):
    cleared(count, PEERS)
    cleared(filled, PLANES + 1)
    meta[...] = jnp.full(meta.shape, -1.0, jnp.float32)
    lane = lax.broadcasted_iota(jnp.int32, (8, WIDTH), 1)

    @pl.loop(0, ROWS)
    def _(i):
        d = dest[i]
        rank = count[d]
        count[d] = rank + 1

        @pl.when(rank >= 2)
        def _():
            plane = lax.div(d, SIDE)
            at = filled[plane]
            filled[plane] = at + 1

            @pl.when(at < RELAY)
            def _():
                start = pl.multiple_of(at * LEVELS, LEVELS)
                pltpu.make_async_copy(
                    cache.at[i], held.at[plane, pl.ds(start, LEVELS)], rows_sem
                ).start()
                code = lax.rem(d, SIDE) * 2 + rank - 2
                meta[plane] = jnp.where(lane == at, code.astype(jnp.float32), meta[plane])
                filled[PLANES] += 1

    most = filled[0]
    for plane in range(1, PLANES):
        most = jnp.maximum(most, filled[plane])
    over = jnp.where(most > RELAY, 1.0, 0.0)
    for plane in range(PLANES):
        tile = jnp.where(lane == RELAY, over, meta[plane])
        held[plane, RELAY * LEVELS :, :] = tile.astype(jnp.bfloat16)

    @pl.loop(0, filled[PLANES])
    def _(i):
        pltpu.make_async_copy(cache.at[0], held.at[0, pl.ds(0, LEVELS)], rows_sem).wait()

    whole = pltpu.make_async_copy(held, out, out_sem)
    whole.start()
    whole.wait()


def direct_kernel(low, dest, cache, out, count, zero, rows_sem):
    cleared(count, PEERS)
    zero[...] = jnp.zeros(zero.shape, zero.dtype)

    @pl.loop(0, ROWS)
    def _(i):
        d = dest[i]
        rank = count[d]
        count[d] = rank + 1

        @pl.when((rank >= low) & (rank < low + 2))
        def _():
            start = pl.multiple_of((rank - low) * LEVELS, LEVELS)
            pltpu.make_async_copy(cache.at[i], out.at[d, pl.ds(start, LEVELS)], rows_sem).start()

    @pl.loop(0, PEERS)
    def _(d):
        for r in range(2):

            @pl.when(count[d] <= low + r)
            def _():
                pltpu.make_async_copy(zero, out.at[d, pl.ds(r * LEVELS, LEVELS)], rows_sem).start()

    whole = out.at[:, pl.ds(0, 2 * LEVELS)]
    pltpu.make_async_copy(whole, whole, rows_sem).wait()


def tile_kernel(tiles, rows, out, sem):
    copy = pltpu.make_async_copy(tiles, out.at[:, pl.ds(2 * LEVELS, 8)], sem)
    copy.start()
    copy.wait()


def plane_sum_kernel(tiles, out, head):
    x = jnp.sum(tiles[...].astype(jnp.float32).reshape(PLANES, SIDE, 8, WIDTH), 0)
    piece = x[:, 5, :] + (x[:, 6, :] + x[:, 7, :])
    out[...] = jnp.concatenate([piece[:, :ROWS], piece[:, ROWS:]], 0)
    part = x[:, 4, HEAD : 2 * HEAD] + (x[:, 4, 2 * HEAD : 3 * HEAD] + x[:, 4, 3 * HEAD :])
    head[...] = jnp.concatenate([part[:OUTCOMES], part[OUTCOMES:]], 1)


def forward_kernel(codes, side, got, *refs):
    outs, (source, held, zero, tile, rows_sem, tile_sem, got_sem) = refs[:SIDE], refs[SIDE:]
    load = pltpu.make_async_copy(got, held, got_sem)
    load.start()
    zero[...] = jnp.zeros(zero.shape, zero.dtype)

    @pl.loop(0, SIDE * 2 * PLANES)
    def _(i):
        source[i] = -1

    over = codes[0, RELAY]
    for plane in range(PLANES):
        over = jnp.maximum(over, codes[plane, RELAY])
        for at in range(RELAY):
            code = codes[plane, at]

            @pl.when(code >= 0)
            def _():
                source[code * PLANES + plane] = at

    tile[...] = jnp.full(tile.shape, over.astype(jnp.float32)).astype(jnp.bfloat16)
    load.wait()
    for k, out in enumerate(outs):
        pltpu.make_async_copy(tile, out.at[pl.ds(LAST - 8, 8)], tile_sem.at[k]).start()
        peer = side[k]

        @pl.loop(0, 2 * PLANES)
        def _(i):
            plane = lax.div(i, 2)
            r = lax.rem(i, 2)
            at = source[(peer * 2 + r) * PLANES + plane]
            to = out.at[pl.ds(pl.multiple_of(i * LEVELS, LEVELS), LEVELS)]

            @pl.when(at >= 0)
            def _():
                start = pl.multiple_of(at * LEVELS, LEVELS)
                pltpu.make_async_copy(
                    held.at[plane, pl.ds(start, LEVELS)], to, rows_sem.at[k]
                ).start()

            @pl.when(at < 0)
            def _():
                pltpu.make_async_copy(zero, to, rows_sem.at[k]).start()

    for k, out in enumerate(outs):
        whole = out.at[pl.ds(0, LAST - 8)]
        pltpu.make_async_copy(whole, whole, rows_sem.at[k]).wait()
        pltpu.make_async_copy(tile, out.at[pl.ds(LAST - 8, 8)], tile_sem.at[k]).wait()


def flag_kernel(*refs):
    most = refs[0][...].astype(jnp.float32)
    for ref in refs[1:SIDE]:
        most = jnp.maximum(most, ref[...].astype(jnp.float32))
    refs[SIDE][0] = jnp.where(jnp.max(most) > 0, 1, 0).astype(jnp.int32)


def chosen_rows(count, size, pick):
    i = lax.broadcasted_iota(jnp.int32, (count, size), 0)
    j = lax.broadcasted_iota(jnp.int32, (count, size), 1)
    return (j == pick(i)).astype(jnp.float32).astype(jnp.bfloat16)


def settle_kernel(side, direct, *refs):
    lasts, (out, logp, held, kept) = refs[:SIDE], refs[SIDE:]
    t = pl.program_id(0)
    for k, last in enumerate(lasts):
        held[side[k]] = last[...]
    turn = chosen_rows(WIDTH, WIDTH, lambda i: lax.rem(i, 16) * 16 + lax.div(i, 16))
    for group in range(2):
        for low in range(0, LEVELS, 16):
            parts = []
            for j in range(4 * group, 4 * group + 4):
                for ref in (direct, held):
                    for r in range(2):
                        start = r * LEVELS + low
                        parts.append(ref[j, start : start + 16, :])
            turned = jnp.dot(turn, jnp.concatenate(parts, 0), preferred_element_type=jnp.float32)
            turned = turned.astype(jnp.bfloat16).reshape(16, 16, WIDTH)
            out[low : low + 16, 16 * group : 16 * group + 16, :] = turned
    tiles = jnp.concatenate([direct[j, 2 * LEVELS :, :] for j in range(SIDE)], 0)
    new = chosen_rows(4 * SIDE, 8 * SIDE, lambda i: lax.div(i, 4) * 8 + lax.rem(i, 4))
    out[LEVELS] = jnp.dot(new, tiles, preferred_element_type=jnp.float32).astype(jnp.bfloat16)
    spread = chosen_rows(4 * SIDE, 8 * SIDE, lambda i: lax.div(i, 4) * 8 + 4)
    terms = jnp.dot(spread, tiles, preferred_element_type=jnp.float32)
    slot = lax.broadcasted_iota(jnp.int32, terms.shape, 0)
    lane = lax.broadcasted_iota(jnp.int32, terms.shape, 1)
    mine = lax.div(lane, 3 * OUTCOMES) == lax.rem(slot, 4)
    rows = pl.ds(pl.multiple_of(t * 4 * SIDE, 4 * SIDE), 4 * SIDE)
    kept[rows, :] = jnp.where(mine, terms, 0.0).astype(jnp.bfloat16)

    @pl.when(t == PLANES - 1)
    def _():
        outcome = lax.broadcasted_iota(jnp.int32, (8, WIDTH), 0)
        lane = lax.broadcasted_iota(jnp.int32, (8, WIDTH), 1)
        gather = (lax.rem(lane, OUTCOMES) == outcome).astype(jnp.float32).astype(jnp.bfloat16)
        found = lax.dot_general(
            gather, kept[...], (((1,), (1,)), ((), ())), preferred_element_type=jnp.float32
        )
        logp[...] = found[:OUTCOMES]


def settle(side, direct, lasts):
    return pl.pallas_call(
        settle_kernel,
        grid=(PLANES,),
        out_shape=(
            jax.ShapeDtypeStruct((LEVELS + 1, 4 * PEERS, WIDTH), jnp.bfloat16),
            jax.ShapeDtypeStruct((OUTCOMES, 4 * PEERS), jnp.float32),
        ),
        in_specs=[SMEM, pl.BlockSpec((SIDE, DIRECT, WIDTH), lambda t: (t, 0, 0))]
        + [pl.BlockSpec((2 * LEVELS, WIDTH), lambda t: (t, 0))] * SIDE,
        out_specs=(
            pl.BlockSpec((LEVELS + 1, 4 * SIDE, WIDTH), lambda t: (0, t, 0)),
            pl.BlockSpec((OUTCOMES, 4 * PEERS), lambda t: (0, 0)),
        ),
        scratch_shapes=[
            pltpu.VMEM((SIDE, 2 * LEVELS, WIDTH), jnp.bfloat16),
            pltpu.VMEM((4 * PEERS, WIDTH), jnp.bfloat16),
        ],
        compiler_params=pltpu.CompilerParams(vmem_limit_bytes=24 << 20),
        cost_estimate=pl.CostEstimate(flops=2 << 30, bytes_accessed=14 << 20, transcendentals=0),
        name="settle",
    )(side, direct, *lasts)


def pack_direct(low, dest, cache):
    return pl.pallas_call(
        functools.partial(direct_kernel, low),
        out_shape=jax.ShapeDtypeStruct((PEERS, DIRECT, WIDTH), jnp.bfloat16),
        in_specs=[SMEM, ANY],
        out_specs=ANY,
        scratch_shapes=[
            pltpu.SMEM((PEERS,), jnp.int32),
            pltpu.VMEM((LEVELS, WIDTH), jnp.bfloat16),
            pltpu.SemaphoreType.DMA,
        ],
        cost_estimate=pl.CostEstimate(flops=0, bytes_accessed=10 << 20, transcendentals=0),
        name="pack_direct",
    )(dest, cache)


def exchanged(x, groups=None):
    return lax.all_to_all(
        x, "sample", split_axis=0, concat_axis=0, tiled=True, axis_index_groups=groups
    )


def xor_pairs(size, bit):
    return [(i, i ^ bit) for i in range(size)]


def tree_sum(x, axis, size, bits):
    terms = [x] + [lax.ppermute(x, axis, xor_pairs(size, bit)) for bit in bits]
    while len(terms) > 1:
        terms = [terms[i] + terms[i + 1] for i in range(0, len(terms), 2)]
    return terms[0]


def bf16_terms(x):
    terms = []
    for _ in range(3):
        term = lax.reduce_precision(x, 8, 7)
        terms.append(term.astype(jnp.bfloat16))
        x = x - term
    return terms


def on_device(tokens, cache, gain, w_query, w_key, w_value, w_out, w_head, coef, chosen, dest):
    target = dest[:, 0]
    me = lax.axis_index("sample")
    y, core = lax.rem(lax.div(me, 2), 4), lax.rem(me, 2)

    relay = pl.pallas_call(
        relay_kernel,
        out_shape=jax.ShapeDtypeStruct((PLANES, PIECE, WIDTH), jnp.bfloat16),
        in_specs=[SMEM, ANY],
        out_specs=ANY,
        scratch_shapes=[
            pltpu.SMEM((PEERS,), jnp.int32),
            pltpu.SMEM((PLANES + 1,), jnp.int32),
            pltpu.VMEM((PLANES, 8, WIDTH), jnp.float32),
            pltpu.VMEM((PLANES, PIECE, WIDTH), jnp.bfloat16),
            pltpu.SemaphoreType.DMA,
            pltpu.SemaphoreType.DMA,
        ],
        name="pack_relay",
    )(target, cache)
    relayed = exchanged(relay, [[z * SIDE + i for z in range(PLANES)] for i in range(SIDE)])

    both, logp, grad_out, grad_head = decode_rows(
        tokens, cache, coef, chosen, gain, w_query, w_key, w_value, w_out, w_head
    )
    sums = jnp.concatenate([grad_out, grad_head], 0)
    target_now, sums = lax.optimization_barrier((target, sums))
    packed = pack_direct(0, target_now, cache)
    sums = tree_sum(sums, "rep", 4, (1, 2, 3))
    packed, sums = lax.optimization_barrier((packed, sums))
    sums = tree_sum(sums, "sample", PEERS, (2, 4, 6))
    sums = tree_sum(sums, "sample", PEERS, (1,))
    rows = jnp.arange(ROWS, dtype=jnp.int32)
    same = (target[:, None] == target[None, :]) & (rows[:, None] < rows[None, :])
    place = target * 4 + jnp.sum(same.astype(jnp.int32), 0)
    slot = (jnp.arange(4 * PEERS, dtype=jnp.int32)[:, None] == place[None, :]).astype(jnp.bfloat16)
    small = jnp.concatenate([both] + bf16_terms(logp), -1)
    slotted = jnp.dot(slot, small, preferred_element_type=jnp.float32).astype(jnp.bfloat16)
    new_rows = slotted[:, :WIDTH].reshape(PEERS, 4, WIDTH)
    mine = y * 2 + core
    share = sums[:ROWS].reshape(SIDE, 2, SIDE, ROWS)
    share = lax.dynamic_index_in_dim(share, mine, 2, keepdims=False).reshape(SIDE, WIDTH)
    share = jnp.stack(bf16_terms(share), 1)[None]
    share = jnp.broadcast_to(share, (PLANES, SIDE, 3, WIDTH)).reshape(PEERS, 3, WIDTH)
    head = jnp.swapaxes(sums[ROWS:].reshape(OUTCOMES, 2, HEAD), 0, 1).reshape(SIDE, HEAD)
    head = lax.dynamic_index_in_dim(head, mine, 0, keepdims=False)
    head = jnp.broadcast_to(jnp.concatenate(bf16_terms(head)), (PEERS, 3 * HEAD))
    logp_row = slotted[:, WIDTH:].reshape(PEERS, 12 * OUTCOMES)
    gap = jnp.zeros((PEERS, WIDTH - 12 * OUTCOMES - 3 * HEAD), jnp.bfloat16)
    mixed = jnp.concatenate([logp_row, gap, head], -1)[:, None]
    tiles = jnp.concatenate([new_rows, mixed, share], 1)
    packed = pl.pallas_call(
        tile_kernel,
        out_shape=jax.ShapeDtypeStruct(packed.shape, packed.dtype),
        in_specs=[pl.BlockSpec(memory_space=pltpu.VMEM), ANY],
        out_specs=ANY,
        scratch_shapes=[pltpu.SemaphoreType.DMA],
        input_output_aliases={1: 0},
        name="pack_tiles",
    )(tiles, packed)
    direct = exchanged(packed)

    codes = relayed[:, RELAY * LEVELS, : 2 * RELAY].astype(jnp.int32)
    shifts = [(dy, dc) for dy in range(4) for dc in range(2)]
    onto = jnp.stack([lax.rem(y + dy, 4) * 2 + (core ^ dc) for dy, dc in shifts])
    came = jnp.stack([lax.rem(y - dy + 4, 4) * 2 + (core ^ dc) for dy, dc in shifts])
    onward = pl.pallas_call(
        forward_kernel,
        out_shape=[jax.ShapeDtypeStruct((LAST, WIDTH), jnp.bfloat16)] * SIDE,
        in_specs=[SMEM, SMEM, ANY],
        out_specs=[ANY] * SIDE,
        scratch_shapes=[
            pltpu.SMEM((SIDE * 2 * PLANES,), jnp.int32),
            pltpu.VMEM((PLANES, PIECE, WIDTH), jnp.bfloat16),
            pltpu.VMEM((LEVELS, WIDTH), jnp.bfloat16),
            pltpu.VMEM((8, WIDTH), jnp.bfloat16),
            pltpu.SemaphoreType.DMA((SIDE,)),
            pltpu.SemaphoreType.DMA((SIDE,)),
            pltpu.SemaphoreType.DMA,
        ],
        cost_estimate=pl.CostEstimate(flops=0, bytes_accessed=5 << 20, transcendentals=0),
        name="pack_plane",
    )(codes, onto.astype(jnp.int32), relayed)
    def in_plane(x, k):
        dy, dc = shifts[k]
        pairs = [
            ((z * 4 + y0) * 2 + c0, (z * 4 + (y0 + dy) % 4) * 2 + (c0 ^ dc))
            for z in range(PLANES)
            for y0 in range(4)
            for c0 in range(2)
        ]
        return lax.ppermute(x, "sample", pairs)

    lasts = [onward[0]] + [in_plane(onward[k], k) for k in range(1, SIDE)]
    came = came.astype(jnp.int32)
    over = pl.pallas_call(
        flag_kernel,
        grid=(1,),
        out_shape=jax.ShapeDtypeStruct((1,), jnp.int32),
        in_specs=[pl.BlockSpec((8, 128), lambda t: (LAST // 8 - 1, 0))] * SIDE,
        out_specs=SMEM,
        name="flag",
    )(*lasts)

    def by_relay(lasts):
        return lasts

    def by_pairs(lasts):
        high = exchanged(pack_direct(2, target, cache))
        high = high[:, : 2 * LEVELS].reshape(PLANES, SIDE, 2 * LEVELS, WIDTH)
        high = jnp.swapaxes(high, 0, 1).reshape(SIDE, 2 * PLANES * LEVELS, WIDTH)
        high = jnp.pad(high, ((0, 0), (0, LAST - 2 * PLANES * LEVELS), (0, 0)))
        return [lax.dynamic_index_in_dim(high, came[k], 0, keepdims=False) for k in range(SIDE)]

    piece, head = pl.pallas_call(
        plane_sum_kernel,
        grid=(1,),
        out_shape=(
            jax.ShapeDtypeStruct((2 * SIDE, ROWS), jnp.float32),
            jax.ShapeDtypeStruct((OUTCOMES, ROWS), jnp.float32),
        ),
        in_specs=[pl.BlockSpec((PEERS, 8, WIDTH), lambda t: (0, 2 * LEVELS // 8, 0))],
        out_specs=(
            pl.BlockSpec((2 * SIDE, ROWS), lambda t: (0, 0)),
            pl.BlockSpec((OUTCOMES, ROWS), lambda t: (0, 0)),
        ),
        name="plane_sum",
    )(direct)
    other = lax.ppermute(piece, "sample", xor_pairs(PEERS, 1))
    piece = jnp.where(
        core == 0, jnp.concatenate([piece, other], 0), jnp.concatenate([other, piece], 0)
    )
    direct, lasts, piece = lax.optimization_barrier((direct, lasts, piece))
    lasts = lax.cond(over[0] > 0, by_pairs, by_relay, lasts)
    piece, lasts = lax.optimization_barrier((piece, lasts))
    shares = jnp.stack([piece] + [in_plane(piece, k) for k in range(2, SIDE, 2)])
    rows_y = jnp.arange(4, dtype=jnp.int32)
    ours = (lax.rem(y - rows_y + 4, 4)[:, None] == rows_y[None, :])[..., None, None]
    grad_out = jnp.sum(jnp.where(ours, shares[None], 0.0), 1).reshape(ROWS, ROWS)
    new_cache, log_probs = settle(came, direct, lasts)
    return (jnp.swapaxes(new_cache, 0, 1), log_probs.T, grad_out, head.T)


def solution(mesh):
    split = P(("sample", "rep"))
    whole = P()
    return jax.shard_map(
        on_device,
        mesh=mesh,
        in_specs=(split, split) + (whole,) * 6 + (split,) * 3,
        out_specs=(split, split, whole, whole),
        check_vma=False,
    )
```

```python
import functools
import math

import jax
import jax.numpy as jnp
from jax import lax
from jax.experimental import pallas as pl
from jax.experimental.pallas import tpu as pltpu
from jax.sharding import PartitionSpec as P

HEADS = 4
OUTCOMES = 4
HEAD = 64
ROWS = 128
LEVELS = 48
WIDTH = 256
PEERS = 64
PLANES = 8
SIDE = 8
RELAY = 8
DIRECT = 2 * LEVELS + 8
PIECE = RELAY * LEVELS + 8
LAST = 2 * PLANES * LEVELS + 8
ANY = pl.BlockSpec(memory_space=pl.ANY)
SMEM = pl.BlockSpec(memory_space=pltpu.SMEM)


def decode_rows(tokens, cache, coef, chosen, gain, w_query, w_key, w_value, w_out, w_head):
    count = tokens.shape[0]
    width = tokens.shape[1]
    levels = cache.shape[1]
    size = width // HEADS
    xf = tokens.astype(jnp.float32)
    normed = (xf * lax.rsqrt(jnp.mean(xf * xf, -1, keepdims=True) + 1e-05) * gain).astype(
        jnp.bfloat16
    )
    query = (
        jnp.dot(normed, w_query, preferred_element_type=jnp.float32) * (1.0 / math.sqrt(size))
    ).astype(jnp.bfloat16)
    key_new = jnp.dot(normed, w_key, preferred_element_type=jnp.float32).astype(jnp.bfloat16)
    value_new = jnp.dot(normed, w_value, preferred_element_type=jnp.float32).astype(jnp.bfloat16)
    query_heads = query.reshape(count, HEADS, size)
    key_rows = cache[:, :, :width].reshape(count, levels, HEADS, size)
    value_rows = cache[:, :, width:].reshape(count, levels, HEADS, size)
    cached_scores = jnp.einsum(
        "yfn,yjfn->yfj", query_heads, key_rows, preferred_element_type=jnp.float32
    )
    score_self = jnp.sum(
        query_heads.astype(jnp.float32) * key_new.astype(jnp.float32).reshape(count, HEADS, size),
        -1,
    )
    top = jnp.maximum(jnp.max(cached_scores, -1), score_self)
    exp_cache = jnp.exp(cached_scores - top[..., None])
    exp_self = jnp.exp(score_self - top)
    total = jnp.sum(exp_cache, -1) + exp_self
    cached_weights = (exp_cache / total[..., None]).astype(jnp.bfloat16)
    weight_self = (exp_self / total).astype(jnp.bfloat16)
    attention_output = jnp.einsum(
        "jat,jtaf->jaf", cached_weights, value_rows, preferred_element_type=jnp.float32
    )
    attention_output = attention_output + weight_self.astype(jnp.float32)[
        ..., None
    ] * value_new.astype(jnp.float32).reshape(count, HEADS, size)
    attention_output = attention_output.reshape(count, width).astype(jnp.bfloat16)
    hidden = (xf + jnp.dot(attention_output, w_out, preferred_element_type=jnp.float32)).astype(
        jnp.bfloat16
    )
    logits = jnp.dot(hidden, w_head, preferred_element_type=jnp.float32)
    logp = jax.nn.log_softmax(logits, -1)
    picked = (chosen[:, None] == jnp.arange(OUTCOMES, dtype=jnp.int32)[None, :]).astype(jnp.float32)
    dlog = coef[:, None] * (picked - jnp.exp(logp))
    grad_head = jnp.dot(dlog.T, hidden.astype(jnp.float32), precision=lax.Precision.HIGHEST)
    hidden_gradient = jnp.dot(dlog, w_head.astype(jnp.float32).T, precision=lax.Precision.HIGHEST)
    grad_out = jnp.dot(
        attention_output.astype(jnp.float32).T, hidden_gradient, precision=lax.Precision.HIGHEST
    )
    both = jnp.concatenate([key_new, value_new], -1)
    return (both, logp, grad_out, grad_head)


def cleared(ref, count):
    @pl.loop(0, count)
    def _(i):
        ref[i] = 0


def relay_kernel(dest, cache, out, count, filled, meta, held, rows_sem, out_sem):
    cleared(count, PEERS)
    cleared(filled, PLANES + 1)
    meta[...] = jnp.full(meta.shape, -1.0, jnp.float32)
    lane = lax.broadcasted_iota(jnp.int32, (8, WIDTH), 1)

    @pl.loop(0, ROWS)
    def _(i):
        d = dest[i]
        rank = count[d]
        count[d] = rank + 1

        @pl.when(rank >= 2)
        def _():
            plane = lax.div(d, SIDE)
            at = filled[plane]
            filled[plane] = at + 1

            @pl.when(at < RELAY)
            def _():
                start = pl.multiple_of(at * LEVELS, LEVELS)
                pltpu.make_async_copy(
                    cache.at[i], held.at[plane, pl.ds(start, LEVELS)], rows_sem
                ).start()
                code = lax.rem(d, SIDE) * 2 + rank - 2
                meta[plane] = jnp.where(lane == at, code.astype(jnp.float32), meta[plane])
                filled[PLANES] += 1

    most = filled[0]
    for plane in range(1, PLANES):
        most = jnp.maximum(most, filled[plane])
    over = jnp.where(most > RELAY, 1.0, 0.0)
    for plane in range(PLANES):
        tile = jnp.where(lane == RELAY, over, meta[plane])
        held[plane, RELAY * LEVELS :, :] = tile.astype(jnp.bfloat16)

    @pl.loop(0, filled[PLANES])
    def _(i):
        pltpu.make_async_copy(cache.at[0], held.at[0, pl.ds(0, LEVELS)], rows_sem).wait()

    whole = pltpu.make_async_copy(held, out, out_sem)
    whole.start()
    whole.wait()


def direct_kernel(low, dest, cache, out, count, zero, rows_sem):
    cleared(count, PEERS)
    zero[...] = jnp.zeros(zero.shape, zero.dtype)

    @pl.loop(0, ROWS)
    def _(i):
        d = dest[i]
        rank = count[d]
        count[d] = rank + 1

        @pl.when((rank >= low) & (rank < low + 2))
        def _():
            start = pl.multiple_of((rank - low) * LEVELS, LEVELS)
            pltpu.make_async_copy(cache.at[i], out.at[d, pl.ds(start, LEVELS)], rows_sem).start()

    @pl.loop(0, PEERS)
    def _(d):
        for r in range(2):

            @pl.when(count[d] <= low + r)
            def _():
                pltpu.make_async_copy(zero, out.at[d, pl.ds(r * LEVELS, LEVELS)], rows_sem).start()

    whole = out.at[:, pl.ds(0, 2 * LEVELS)]
    pltpu.make_async_copy(whole, whole, rows_sem).wait()


def tile_kernel(tiles, rows, out, sem):
    copy = pltpu.make_async_copy(tiles, out.at[:, pl.ds(2 * LEVELS, 8)], sem)
    copy.start()
    copy.wait()


def plane_sum_kernel(tiles, out, head):
    x = jnp.sum(tiles[...].astype(jnp.float32).reshape(PLANES, SIDE, 8, WIDTH), 0)
    piece = x[:, 5, :] + (x[:, 6, :] + x[:, 7, :])
    out[...] = jnp.concatenate([piece[:, :ROWS], piece[:, ROWS:]], 0)
    part = x[:, 4, HEAD : 2 * HEAD] + (x[:, 4, 2 * HEAD : 3 * HEAD] + x[:, 4, 3 * HEAD :])
    head[...] = jnp.concatenate([part[:OUTCOMES], part[OUTCOMES:]], 1)


def forward_kernel(codes, side, got, *refs):
    outs, (source, held, zero, tile, rows_sem, tile_sem, got_sem) = refs[:SIDE], refs[SIDE:]
    load = pltpu.make_async_copy(got, held, got_sem)
    load.start()
    zero[...] = jnp.zeros(zero.shape, zero.dtype)

    @pl.loop(0, SIDE * 2 * PLANES)
    def _(i):
        source[i] = -1

    over = codes[0, RELAY]
    for plane in range(PLANES):
        over = jnp.maximum(over, codes[plane, RELAY])
        for at in range(RELAY):
            code = codes[plane, at]

            @pl.when(code >= 0)
            def _():
                source[code * PLANES + plane] = at

    tile[...] = jnp.full(tile.shape, over.astype(jnp.float32)).astype(jnp.bfloat16)
    load.wait()
    for k, out in enumerate(outs):
        pltpu.make_async_copy(tile, out.at[pl.ds(LAST - 8, 8)], tile_sem.at[k]).start()
        peer = side[k]

        @pl.loop(0, 2 * PLANES)
        def _(i):
            plane = lax.div(i, 2)
            r = lax.rem(i, 2)
            at = source[(peer * 2 + r) * PLANES + plane]
            to = out.at[pl.ds(pl.multiple_of(i * LEVELS, LEVELS), LEVELS)]

            @pl.when(at >= 0)
            def _():
                start = pl.multiple_of(at * LEVELS, LEVELS)
                pltpu.make_async_copy(
                    held.at[plane, pl.ds(start, LEVELS)], to, rows_sem.at[k]
                ).start()

            @pl.when(at < 0)
            def _():
                pltpu.make_async_copy(zero, to, rows_sem.at[k]).start()

    for k, out in enumerate(outs):
        whole = out.at[pl.ds(0, LAST - 8)]
        pltpu.make_async_copy(whole, whole, rows_sem.at[k]).wait()
        pltpu.make_async_copy(tile, out.at[pl.ds(LAST - 8, 8)], tile_sem.at[k]).wait()


def flag_kernel(*refs):
    most = refs[0][...].astype(jnp.float32)
    for ref in refs[1:SIDE]:
        most = jnp.maximum(most, ref[...].astype(jnp.float32))
    refs[SIDE][0] = jnp.where(jnp.max(most) > 0, 1, 0).astype(jnp.int32)


def chosen_rows(count, size, pick):
    i = lax.broadcasted_iota(jnp.int32, (count, size), 0)
    j = lax.broadcasted_iota(jnp.int32, (count, size), 1)
    return (j == pick(i)).astype(jnp.float32).astype(jnp.bfloat16)


def settle_kernel(side, direct, *refs):
    lasts, (out, logp, held, kept) = refs[:SIDE], refs[SIDE:]
    t = pl.program_id(0)
    for k, last in enumerate(lasts):
        held[side[k]] = last[...]
    turn = chosen_rows(WIDTH, WIDTH, lambda i: lax.rem(i, 16) * 16 + lax.div(i, 16))
    for group in range(2):
        for low in range(0, LEVELS, 16):
            parts = []
            for j in range(4 * group, 4 * group + 4):
                for ref in (direct, held):
                    for r in range(2):
                        start = r * LEVELS + low
                        parts.append(ref[j, start : start + 16, :])
            turned = jnp.dot(turn, jnp.concatenate(parts, 0), preferred_element_type=jnp.float32)
            turned = turned.astype(jnp.bfloat16).reshape(16, 16, WIDTH)
            out[low : low + 16, 16 * group : 16 * group + 16, :] = turned
    tiles = jnp.concatenate([direct[j, 2 * LEVELS :, :] for j in range(SIDE)], 0)
    new = chosen_rows(4 * SIDE, 8 * SIDE, lambda i: lax.div(i, 4) * 8 + lax.rem(i, 4))
    out[LEVELS] = jnp.dot(new, tiles, preferred_element_type=jnp.float32).astype(jnp.bfloat16)
    spread = chosen_rows(4 * SIDE, 8 * SIDE, lambda i: lax.div(i, 4) * 8 + 4)
    terms = jnp.dot(spread, tiles, preferred_element_type=jnp.float32)
    slot = lax.broadcasted_iota(jnp.int32, terms.shape, 0)
    lane = lax.broadcasted_iota(jnp.int32, terms.shape, 1)
    mine = lax.div(lane, 3 * OUTCOMES) == lax.rem(slot, 4)
    rows = pl.ds(pl.multiple_of(t * 4 * SIDE, 4 * SIDE), 4 * SIDE)
    kept[rows, :] = jnp.where(mine, terms, 0.0).astype(jnp.bfloat16)

    @pl.when(t == PLANES - 1)
    def _():
        outcome = lax.broadcasted_iota(jnp.int32, (8, WIDTH), 0)
        lane = lax.broadcasted_iota(jnp.int32, (8, WIDTH), 1)
        gather = (lax.rem(lane, OUTCOMES) == outcome).astype(jnp.float32).astype(jnp.bfloat16)
        found = lax.dot_general(
            gather, kept[...], (((1,), (1,)), ((), ())), preferred_element_type=jnp.float32
        )
        logp[...] = found[:OUTCOMES]


def settle(side, direct, lasts):
    return pl.pallas_call(
        settle_kernel,
        grid=(PLANES,),
        out_shape=(
            jax.ShapeDtypeStruct((LEVELS + 1, 4 * PEERS, WIDTH), jnp.bfloat16),
            jax.ShapeDtypeStruct((OUTCOMES, 4 * PEERS), jnp.float32),
        ),
        in_specs=[SMEM, pl.BlockSpec((SIDE, DIRECT, WIDTH), lambda t: (t, 0, 0))]
        + [pl.BlockSpec((2 * LEVELS, WIDTH), lambda t: (t, 0))] * SIDE,
        out_specs=(
            pl.BlockSpec((LEVELS + 1, 4 * SIDE, WIDTH), lambda t: (0, t, 0)),
            pl.BlockSpec((OUTCOMES, 4 * PEERS), lambda t: (0, 0)),
        ),
        scratch_shapes=[
            pltpu.VMEM((SIDE, 2 * LEVELS, WIDTH), jnp.bfloat16),
            pltpu.VMEM((4 * PEERS, WIDTH), jnp.bfloat16),
        ],
        compiler_params=pltpu.CompilerParams(vmem_limit_bytes=12 << 20),
        cost_estimate=pl.CostEstimate(flops=2 << 30, bytes_accessed=14 << 20, transcendentals=0),
        name="settle",
    )(side, direct, *lasts)


def pack_direct(low, dest, cache):
    return pl.pallas_call(
        functools.partial(direct_kernel, low),
        out_shape=jax.ShapeDtypeStruct((PEERS, DIRECT, WIDTH), jnp.bfloat16),
        in_specs=[SMEM, pl.BlockSpec(memory_space=pltpu.VMEM)],
        out_specs=ANY,
        scratch_shapes=[
            pltpu.SMEM((PEERS,), jnp.int32),
            pltpu.VMEM((LEVELS, WIDTH), jnp.bfloat16),
            pltpu.SemaphoreType.DMA,
        ],
        cost_estimate=pl.CostEstimate(flops=0, bytes_accessed=10 << 20, transcendentals=0),
        compiler_params=pltpu.CompilerParams(vmem_limit_bytes=8 << 20),
        name="pack_direct",
    )(dest, cache)


def exchanged(x, groups=None):
    return lax.all_to_all(
        x, "sample", split_axis=0, concat_axis=0, tiled=True, axis_index_groups=groups
    )


def xor_pairs(size, bit):
    return [(i, i ^ bit) for i in range(size)]


def tree_sum(x, axis, size, bits):
    terms = [x] + [lax.ppermute(x, axis, xor_pairs(size, bit)) for bit in bits]
    while len(terms) > 1:
        terms = [terms[i] + terms[i + 1] for i in range(0, len(terms), 2)]
    return terms[0]


def bf16_terms(x):
    terms = []
    for _ in range(3):
        term = lax.reduce_precision(x, 8, 7)
        terms.append(term.astype(jnp.bfloat16))
        x = x - term
    return terms


def on_device(tokens, cache, gain, w_query, w_key, w_value, w_out, w_head, coef, chosen, dest):
    target = dest[:, 0]
    me = lax.axis_index("sample")
    y, core = lax.rem(lax.div(me, 2), 4), lax.rem(me, 2)

    relay = pl.pallas_call(
        relay_kernel,
        out_shape=jax.ShapeDtypeStruct((PLANES, PIECE, WIDTH), jnp.bfloat16),
        in_specs=[SMEM, ANY],
        out_specs=ANY,
        scratch_shapes=[
            pltpu.SMEM((PEERS,), jnp.int32),
            pltpu.SMEM((PLANES + 1,), jnp.int32),
            pltpu.VMEM((PLANES, 8, WIDTH), jnp.float32),
            pltpu.VMEM((PLANES, PIECE, WIDTH), jnp.bfloat16),
            pltpu.SemaphoreType.DMA,
            pltpu.SemaphoreType.DMA,
        ],
        compiler_params=pltpu.CompilerParams(vmem_limit_bytes=4 << 20),
        name="pack_relay",
    )(target, cache)
    relayed = exchanged(relay, [[z * SIDE + i for z in range(PLANES)] for i in range(SIDE)])

    both, logp, grad_out, grad_head = decode_rows(
        tokens, cache, coef, chosen, gain, w_query, w_key, w_value, w_out, w_head
    )
    sums = jnp.concatenate([grad_out, grad_head], 0)
    target_now, sums = lax.optimization_barrier((target, sums))
    packed = pack_direct(0, target_now, cache)
    sums = tree_sum(sums, "rep", 4, (1, 2, 3))
    packed, sums = lax.optimization_barrier((packed, sums))
    sums = tree_sum(sums, "sample", PEERS, (2, 4, 6))
    sums = tree_sum(sums, "sample", PEERS, (1,))
    rows = jnp.arange(ROWS, dtype=jnp.int32)
    same = (target[:, None] == target[None, :]) & (rows[:, None] < rows[None, :])
    place = target * 4 + jnp.sum(same.astype(jnp.int32), 0)
    slot = (jnp.arange(4 * PEERS, dtype=jnp.int32)[:, None] == place[None, :]).astype(jnp.bfloat16)
    small = jnp.concatenate([both] + bf16_terms(logp), -1)
    slotted = jnp.dot(slot, small, preferred_element_type=jnp.float32).astype(jnp.bfloat16)
    new_rows = slotted[:, :WIDTH].reshape(PEERS, 4, WIDTH)
    mine = y * 2 + core
    share = sums[:ROWS].reshape(SIDE, 2, SIDE, ROWS)
    share = lax.dynamic_index_in_dim(share, mine, 2, keepdims=False).reshape(SIDE, WIDTH)
    share = jnp.stack(bf16_terms(share), 1)[None]
    share = jnp.broadcast_to(share, (PLANES, SIDE, 3, WIDTH)).reshape(PEERS, 3, WIDTH)
    head = jnp.swapaxes(sums[ROWS:].reshape(OUTCOMES, 2, HEAD), 0, 1).reshape(SIDE, HEAD)
    head = lax.dynamic_index_in_dim(head, mine, 0, keepdims=False)
    head = jnp.broadcast_to(jnp.concatenate(bf16_terms(head)), (PEERS, 3 * HEAD))
    logp_row = slotted[:, WIDTH:].reshape(PEERS, 12 * OUTCOMES)
    gap = jnp.zeros((PEERS, WIDTH - 12 * OUTCOMES - 3 * HEAD), jnp.bfloat16)
    mixed = jnp.concatenate([logp_row, gap, head], -1)[:, None]
    tiles = jnp.concatenate([new_rows, mixed, share], 1)
    packed = pl.pallas_call(
        tile_kernel,
        out_shape=jax.ShapeDtypeStruct(packed.shape, packed.dtype),
        in_specs=[pl.BlockSpec(memory_space=pltpu.VMEM), ANY],
        out_specs=ANY,
        scratch_shapes=[pltpu.SemaphoreType.DMA],
        input_output_aliases={1: 0},
        compiler_params=pltpu.CompilerParams(vmem_limit_bytes=2 << 20),
        name="pack_tiles",
    )(tiles, packed)
    direct = exchanged(packed)

    codes = relayed[:, RELAY * LEVELS, : 2 * RELAY].astype(jnp.int32)
    shifts = [(0, 0), (1, 0), (3, 0), (2, 0), (2, 1), (1, 1), (3, 1), (0, 1)]
    onto = jnp.stack([lax.rem(y + dy, 4) * 2 + (core ^ dc) for dy, dc in shifts])
    came = jnp.stack([lax.rem(y - dy + 4, 4) * 2 + (core ^ dc) for dy, dc in shifts])
    onward = pl.pallas_call(
        forward_kernel,
        out_shape=[jax.ShapeDtypeStruct((LAST, WIDTH), jnp.bfloat16)] * SIDE,
        in_specs=[SMEM, SMEM, ANY],
        out_specs=[ANY] * SIDE,
        scratch_shapes=[
            pltpu.SMEM((SIDE * 2 * PLANES,), jnp.int32),
            pltpu.VMEM((PLANES, PIECE, WIDTH), jnp.bfloat16),
            pltpu.VMEM((LEVELS, WIDTH), jnp.bfloat16),
            pltpu.VMEM((8, WIDTH), jnp.bfloat16),
            pltpu.SemaphoreType.DMA((SIDE,)),
            pltpu.SemaphoreType.DMA((SIDE,)),
            pltpu.SemaphoreType.DMA,
        ],
        cost_estimate=pl.CostEstimate(flops=0, bytes_accessed=5 << 20, transcendentals=0),
        compiler_params=pltpu.CompilerParams(vmem_limit_bytes=4 << 20),
        name="pack_plane",
    )(codes, onto.astype(jnp.int32), relayed)
    def in_plane(x, k):
        dy, dc = shifts[k]
        pairs = [
            ((z * 4 + y0) * 2 + c0, (z * 4 + (y0 + dy) % 4) * 2 + (c0 ^ dc))
            for z in range(PLANES)
            for y0 in range(4)
            for c0 in range(2)
        ]
        return lax.ppermute(x, "sample", pairs)

    lasts = [onward[0]] + [in_plane(onward[k], k) for k in range(1, SIDE)]
    came = came.astype(jnp.int32)
    over = pl.pallas_call(
        flag_kernel,
        grid=(1,),
        out_shape=jax.ShapeDtypeStruct((1,), jnp.int32),
        in_specs=[pl.BlockSpec((8, 128), lambda t: (LAST // 8 - 1, 0))] * SIDE,
        out_specs=SMEM,
        compiler_params=pltpu.CompilerParams(vmem_limit_bytes=2 << 20),
        name="flag",
    )(*lasts)

    def by_relay(lasts):
        return lasts

    def by_pairs(lasts):
        high = exchanged(pack_direct(2, target, cache))
        high = high[:, : 2 * LEVELS].reshape(PLANES, SIDE, 2 * LEVELS, WIDTH)
        high = jnp.swapaxes(high, 0, 1).reshape(SIDE, 2 * PLANES * LEVELS, WIDTH)
        high = jnp.pad(high, ((0, 0), (0, LAST - 2 * PLANES * LEVELS), (0, 0)))
        return [lax.dynamic_index_in_dim(high, came[k], 0, keepdims=False) for k in range(SIDE)]

    piece, head = pl.pallas_call(
        plane_sum_kernel,
        grid=(1,),
        out_shape=(
            jax.ShapeDtypeStruct((2 * SIDE, ROWS), jnp.float32),
            jax.ShapeDtypeStruct((OUTCOMES, ROWS), jnp.float32),
        ),
        in_specs=[pl.BlockSpec((PEERS, 8, WIDTH), lambda t: (0, 2 * LEVELS // 8, 0))],
        out_specs=(
            pl.BlockSpec((2 * SIDE, ROWS), lambda t: (0, 0)),
            pl.BlockSpec((OUTCOMES, ROWS), lambda t: (0, 0)),
        ),
        compiler_params=pltpu.CompilerParams(vmem_limit_bytes=4 << 20),
        name="plane_sum",
    )(direct)
    other = lax.ppermute(piece, "sample", xor_pairs(PEERS, 1))
    piece = jnp.where(
        core == 0, jnp.concatenate([piece, other], 0), jnp.concatenate([other, piece], 0)
    )
    direct, lasts, piece = lax.optimization_barrier((direct, lasts, piece))
    lasts = lax.cond(over[0] > 0, by_pairs, by_relay, lasts)
    piece, lasts = lax.optimization_barrier((piece, lasts))
    shares = jnp.stack([piece] + [in_plane(piece, shifts.index((dy, 0))) for dy in (1, 2, 3)])
    rows_y = jnp.arange(4, dtype=jnp.int32)
    ours = (lax.rem(y - rows_y + 4, 4)[:, None] == rows_y[None, :])[..., None, None]
    grad_out = jnp.sum(jnp.where(ours, shares[None], 0.0), 1).reshape(ROWS, ROWS)
    new_cache, log_probs = settle(came, direct, lasts)
    return (jnp.swapaxes(new_cache, 0, 1), log_probs.T, grad_out, head.T)


def solution(mesh):
    split = P(("sample", "rep"))
    whole = P()
    return jax.shard_map(
        on_device,
        mesh=mesh,
        in_specs=(split, split) + (whole,) * 6 + (split,) * 3,
        out_specs=(split, split, whole, whole),
        check_vma=False,
    )
```

```python
import functools
import math

import jax
import jax.numpy as jnp
from jax import lax
from jax.experimental import pallas as pl
from jax.experimental.pallas import tpu as pltpu
from jax.sharding import PartitionSpec as P

HEADS = 4
OUTCOMES = 4
HEAD = 64
ROWS = 128
LEVELS = 48
WIDTH = 256
PEERS = 64
PLANES = 8
SIDE = 8
RELAY = 8
DIRECT = 2 * LEVELS + 8
PIECE = RELAY * LEVELS + 8
LAST = 2 * PLANES * LEVELS + 8
ANY = pl.BlockSpec(memory_space=pl.ANY)
SMEM = pl.BlockSpec(memory_space=pltpu.SMEM)


def decode_rows(tokens, cache, coef, chosen, gain, w_query, w_key, w_value, w_out, w_head):
    count = tokens.shape[0]
    width = tokens.shape[1]
    levels = cache.shape[1]
    size = width // HEADS
    xf = tokens.astype(jnp.float32)
    normed = (xf * lax.rsqrt(jnp.mean(xf * xf, -1, keepdims=True) + 1e-05) * gain).astype(
        jnp.bfloat16
    )
    query = (
        jnp.dot(normed, w_query, preferred_element_type=jnp.float32) * (1.0 / math.sqrt(size))
    ).astype(jnp.bfloat16)
    key_new = jnp.dot(normed, w_key, preferred_element_type=jnp.float32).astype(jnp.bfloat16)
    value_new = jnp.dot(normed, w_value, preferred_element_type=jnp.float32).astype(jnp.bfloat16)
    query_heads = query.reshape(count, HEADS, size)
    key_rows = cache[:, :, :width].reshape(count, levels, HEADS, size)
    value_rows = cache[:, :, width:].reshape(count, levels, HEADS, size)
    cached_scores = jnp.einsum(
        "yfn,yjfn->yfj", query_heads, key_rows, preferred_element_type=jnp.float32
    )
    score_self = jnp.sum(
        query_heads.astype(jnp.float32) * key_new.astype(jnp.float32).reshape(count, HEADS, size),
        -1,
    )
    top = jnp.maximum(jnp.max(cached_scores, -1), score_self)
    exp_cache = jnp.exp(cached_scores - top[..., None])
    exp_self = jnp.exp(score_self - top)
    total = jnp.sum(exp_cache, -1) + exp_self
    cached_weights = (exp_cache / total[..., None]).astype(jnp.bfloat16)
    weight_self = (exp_self / total).astype(jnp.bfloat16)
    attention_output = jnp.einsum(
        "jat,jtaf->jaf", cached_weights, value_rows, preferred_element_type=jnp.float32
    )
    attention_output = attention_output + weight_self.astype(jnp.float32)[
        ..., None
    ] * value_new.astype(jnp.float32).reshape(count, HEADS, size)
    attention_output = attention_output.reshape(count, width).astype(jnp.bfloat16)
    hidden = (xf + jnp.dot(attention_output, w_out, preferred_element_type=jnp.float32)).astype(
        jnp.bfloat16
    )
    logits = jnp.dot(hidden, w_head, preferred_element_type=jnp.float32)
    logp = jax.nn.log_softmax(logits, -1)
    picked = (chosen[:, None] == jnp.arange(OUTCOMES, dtype=jnp.int32)[None, :]).astype(jnp.float32)
    dlog = coef[:, None] * (picked - jnp.exp(logp))
    grad_head = jnp.dot(dlog.T, hidden.astype(jnp.float32), precision=lax.Precision.HIGHEST)
    hidden_gradient = jnp.dot(dlog, w_head.astype(jnp.float32).T, precision=lax.Precision.HIGHEST)
    grad_out = jnp.dot(
        attention_output.astype(jnp.float32).T, hidden_gradient, precision=lax.Precision.HIGHEST
    )
    both = jnp.concatenate([key_new, value_new], -1)
    return (both, logp, grad_out, grad_head)


def cleared(ref, count):
    for i in range(count):
        ref[i] = 0


def relay_kernel(dest, cache, out, count, filled, meta, held, rows_sem, out_sem):
    cleared(count, PEERS)
    cleared(filled, PLANES + 1)
    meta[...] = jnp.full(meta.shape, -1.0, jnp.float32)
    lane = lax.broadcasted_iota(jnp.int32, (8, WIDTH), 1)

    @pl.loop(0, ROWS, unroll=8)
    def _(i):
        d = dest[i]
        rank = count[d]
        count[d] = rank + 1

        @pl.when(rank >= 2)
        def _():
            plane = lax.div(d, SIDE)
            at = filled[plane]
            filled[plane] = at + 1

            @pl.when(at < RELAY)
            def _():
                start = pl.multiple_of(at * LEVELS, LEVELS)
                pltpu.make_async_copy(
                    cache.at[i], held.at[plane, pl.ds(start, LEVELS)], rows_sem
                ).start()
                code = lax.rem(d, SIDE) * 2 + rank - 2
                meta[plane] = jnp.where(lane == at, code.astype(jnp.float32), meta[plane])
                filled[PLANES] += 1

    most = filled[0]
    for plane in range(1, PLANES):
        most = jnp.maximum(most, filled[plane])
    over = jnp.where(most > RELAY, 1.0, 0.0)
    for plane in range(PLANES):
        tile = jnp.where(lane == RELAY, over, meta[plane])
        held[plane, RELAY * LEVELS :, :] = tile.astype(jnp.bfloat16)

    @pl.loop(0, filled[PLANES])
    def _(i):
        pltpu.make_async_copy(cache.at[0], held.at[0, pl.ds(0, LEVELS)], rows_sem).wait()

    whole = pltpu.make_async_copy(held, out, out_sem)
    whole.start()
    whole.wait()


def direct_kernel(low, dest, cache, out, count, zero, rows_sem):
    cleared(count, PEERS)
    zero[...] = jnp.zeros(zero.shape, zero.dtype)

    @pl.loop(0, ROWS)
    def _(i):
        d = dest[i]
        rank = count[d]
        count[d] = rank + 1

        @pl.when((rank >= low) & (rank < low + 2))
        def _():
            start = pl.multiple_of((rank - low) * LEVELS, LEVELS)
            pltpu.make_async_copy(cache.at[i], out.at[d, pl.ds(start, LEVELS)], rows_sem).start()

    @pl.loop(0, PEERS)
    def _(d):
        for r in range(2):

            @pl.when(count[d] <= low + r)
            def _():
                pltpu.make_async_copy(zero, out.at[d, pl.ds(r * LEVELS, LEVELS)], rows_sem).start()

    whole = out.at[:, pl.ds(0, 2 * LEVELS)]
    pltpu.make_async_copy(whole, whole, rows_sem).wait()


def tile_kernel(tiles, rows, out, sem):
    copy = pltpu.make_async_copy(tiles, out.at[:, pl.ds(2 * LEVELS, 8)], sem)
    copy.start()
    copy.wait()


def plane_sum_kernel(tiles, out, head):
    x = jnp.sum(tiles[...].astype(jnp.float32).reshape(PLANES, SIDE, 8, WIDTH), 0)
    piece = x[:, 5, :] + (x[:, 6, :] + x[:, 7, :])
    out[...] = jnp.concatenate([piece[:, :ROWS], piece[:, ROWS:]], 0)
    part = x[:, 4, HEAD : 2 * HEAD] + (x[:, 4, 2 * HEAD : 3 * HEAD] + x[:, 4, 3 * HEAD :])
    head[...] = jnp.concatenate([part[:OUTCOMES], part[OUTCOMES:]], 1)


def forward_kernel(codes, side, got, *refs):
    outs, (source, held, zero, tile, rows_sem, tile_sem, got_sem) = refs[:SIDE], refs[SIDE:]
    load = pltpu.make_async_copy(got, held, got_sem)
    load.start()
    zero[...] = jnp.zeros(zero.shape, zero.dtype)

    @pl.loop(0, SIDE * 2 * PLANES)
    def _(i):
        source[i] = -1

    over = codes[0, RELAY]
    for plane in range(PLANES):
        over = jnp.maximum(over, codes[plane, RELAY])
        for at in range(RELAY):
            code = codes[plane, at]

            @pl.when(code >= 0)
            def _():
                source[code * PLANES + plane] = at

    tile[...] = jnp.full(tile.shape, over.astype(jnp.float32)).astype(jnp.bfloat16)
    load.wait()
    for k, out in enumerate(outs):
        pltpu.make_async_copy(tile, out.at[pl.ds(LAST - 8, 8)], tile_sem.at[k]).start()
        peer = side[k]

        @pl.loop(0, 2 * PLANES)
        def _(i):
            plane = lax.div(i, 2)
            r = lax.rem(i, 2)
            at = source[(peer * 2 + r) * PLANES + plane]
            to = out.at[pl.ds(pl.multiple_of(i * LEVELS, LEVELS), LEVELS)]

            @pl.when(at >= 0)
            def _():
                start = pl.multiple_of(at * LEVELS, LEVELS)
                pltpu.make_async_copy(
                    held.at[plane, pl.ds(start, LEVELS)], to, rows_sem.at[k]
                ).start()

            @pl.when(at < 0)
            def _():
                pltpu.make_async_copy(zero, to, rows_sem.at[k]).start()

    for k, out in enumerate(outs):
        whole = out.at[pl.ds(0, LAST - 8)]
        pltpu.make_async_copy(whole, whole, rows_sem.at[k]).wait()
        pltpu.make_async_copy(tile, out.at[pl.ds(LAST - 8, 8)], tile_sem.at[k]).wait()


def flag_kernel(*refs):
    most = refs[0][...].astype(jnp.float32)
    for ref in refs[1:SIDE]:
        most = jnp.maximum(most, ref[...].astype(jnp.float32))
    refs[SIDE][0] = jnp.where(jnp.max(most) > 0, 1, 0).astype(jnp.int32)


def chosen_rows(count, size, pick):
    i = lax.broadcasted_iota(jnp.int32, (count, size), 0)
    j = lax.broadcasted_iota(jnp.int32, (count, size), 1)
    return (j == pick(i)).astype(jnp.float32).astype(jnp.bfloat16)


def settle_kernel(side, direct, *refs):
    lasts, (out, logp, held, kept) = refs[:SIDE], refs[SIDE:]
    t = pl.program_id(0)
    for k, last in enumerate(lasts):
        held[side[k]] = last[...]
    turn = chosen_rows(WIDTH, WIDTH, lambda i: lax.rem(i, 16) * 16 + lax.div(i, 16))
    for group in range(2):
        for low in range(0, LEVELS, 16):
            parts = []
            for j in range(4 * group, 4 * group + 4):
                for ref in (direct, held):
                    for r in range(2):
                        start = r * LEVELS + low
                        parts.append(ref[j, start : start + 16, :])
            turned = jnp.dot(turn, jnp.concatenate(parts, 0), preferred_element_type=jnp.float32)
            turned = turned.astype(jnp.bfloat16).reshape(16, 16, WIDTH)
            out[low : low + 16, 16 * group : 16 * group + 16, :] = turned
    tiles = jnp.concatenate([direct[j, 2 * LEVELS :, :] for j in range(SIDE)], 0)
    new = chosen_rows(4 * SIDE, 8 * SIDE, lambda i: lax.div(i, 4) * 8 + lax.rem(i, 4))
    out[LEVELS] = jnp.dot(new, tiles, preferred_element_type=jnp.float32).astype(jnp.bfloat16)
    spread = chosen_rows(4 * SIDE, 8 * SIDE, lambda i: lax.div(i, 4) * 8 + 4)
    terms = jnp.dot(spread, tiles, preferred_element_type=jnp.float32)
    slot = lax.broadcasted_iota(jnp.int32, terms.shape, 0)
    lane = lax.broadcasted_iota(jnp.int32, terms.shape, 1)
    mine = lax.div(lane, 3 * OUTCOMES) == lax.rem(slot, 4)
    rows = pl.ds(pl.multiple_of(t * 4 * SIDE, 4 * SIDE), 4 * SIDE)
    kept[rows, :] = jnp.where(mine, terms, 0.0).astype(jnp.bfloat16)

    @pl.when(t == PLANES - 1)
    def _():
        outcome = lax.broadcasted_iota(jnp.int32, (8, WIDTH), 0)
        lane = lax.broadcasted_iota(jnp.int32, (8, WIDTH), 1)
        gather = (lax.rem(lane, OUTCOMES) == outcome).astype(jnp.float32).astype(jnp.bfloat16)
        found = lax.dot_general(
            gather, kept[...], (((1,), (1,)), ((), ())), preferred_element_type=jnp.float32
        )
        logp[...] = found[:OUTCOMES]


def settle(side, direct, lasts):
    return pl.pallas_call(
        settle_kernel,
        grid=(PLANES,),
        out_shape=(
            jax.ShapeDtypeStruct((LEVELS + 1, 4 * PEERS, WIDTH), jnp.bfloat16),
            jax.ShapeDtypeStruct((OUTCOMES, 4 * PEERS), jnp.float32),
        ),
        in_specs=[SMEM, pl.BlockSpec((SIDE, DIRECT, WIDTH), lambda t: (t, 0, 0))]
        + [pl.BlockSpec((2 * LEVELS, WIDTH), lambda t: (t, 0))] * SIDE,
        out_specs=(
            pl.BlockSpec((LEVELS + 1, 4 * SIDE, WIDTH), lambda t: (0, t, 0)),
            pl.BlockSpec((OUTCOMES, 4 * PEERS), lambda t: (0, 0)),
        ),
        scratch_shapes=[
            pltpu.VMEM((SIDE, 2 * LEVELS, WIDTH), jnp.bfloat16),
            pltpu.VMEM((4 * PEERS, WIDTH), jnp.bfloat16),
        ],
        compiler_params=pltpu.CompilerParams(vmem_limit_bytes=12 << 20),
        cost_estimate=pl.CostEstimate(flops=2 << 30, bytes_accessed=14 << 20, transcendentals=0),
        name="settle",
    )(side, direct, *lasts)


def pack_direct(low, dest, cache):
    return pl.pallas_call(
        functools.partial(direct_kernel, low),
        out_shape=jax.ShapeDtypeStruct((PEERS, DIRECT, WIDTH), jnp.bfloat16),
        in_specs=[SMEM, pl.BlockSpec(memory_space=pltpu.VMEM)],
        out_specs=ANY,
        scratch_shapes=[
            pltpu.SMEM((PEERS,), jnp.int32),
            pltpu.VMEM((LEVELS, WIDTH), jnp.bfloat16),
            pltpu.SemaphoreType.DMA,
        ],
        cost_estimate=pl.CostEstimate(flops=0, bytes_accessed=10 << 20, transcendentals=0),
        compiler_params=pltpu.CompilerParams(vmem_limit_bytes=8 << 20),
        name="pack_direct",
    )(dest, cache)


def exchanged(x, groups=None):
    return lax.all_to_all(
        x, "sample", split_axis=0, concat_axis=0, tiled=True, axis_index_groups=groups
    )


def xor_pairs(size, bit):
    return [(i, i ^ bit) for i in range(size)]


def tree_sum(x, axis, size, bits):
    terms = [x] + [lax.ppermute(x, axis, xor_pairs(size, bit)) for bit in bits]
    while len(terms) > 1:
        terms = [terms[i] + terms[i + 1] for i in range(0, len(terms), 2)]
    return terms[0]


def bf16_terms(x):
    terms = []
    for _ in range(3):
        term = lax.reduce_precision(x, 8, 7)
        terms.append(term.astype(jnp.bfloat16))
        x = x - term
    return terms


def on_device(tokens, cache, gain, w_query, w_key, w_value, w_out, w_head, coef, chosen, dest):
    target = dest[:, 0]
    me = lax.axis_index("sample")
    y, core = lax.rem(lax.div(me, 2), 4), lax.rem(me, 2)

    relay = pl.pallas_call(
        relay_kernel,
        out_shape=jax.ShapeDtypeStruct((PLANES, PIECE, WIDTH), jnp.bfloat16),
        in_specs=[SMEM, ANY],
        out_specs=ANY,
        scratch_shapes=[
            pltpu.SMEM((PEERS,), jnp.int32),
            pltpu.SMEM((PLANES + 1,), jnp.int32),
            pltpu.VMEM((PLANES, 8, WIDTH), jnp.float32),
            pltpu.VMEM((PLANES, PIECE, WIDTH), jnp.bfloat16),
            pltpu.SemaphoreType.DMA,
            pltpu.SemaphoreType.DMA,
        ],
        compiler_params=pltpu.CompilerParams(vmem_limit_bytes=4 << 20),
        name="pack_relay",
    )(target, cache)
    relayed = exchanged(relay, [[z * SIDE + i for z in range(PLANES)] for i in range(SIDE)])

    both, logp, grad_out, grad_head = decode_rows(
        tokens, cache, coef, chosen, gain, w_query, w_key, w_value, w_out, w_head
    )
    sums = jnp.concatenate([grad_out, grad_head], 0)
    target_now, sums = lax.optimization_barrier((target, sums))
    packed = pack_direct(0, target_now, cache)
    sums = tree_sum(sums, "rep", 4, (1, 2, 3))
    packed, sums = lax.optimization_barrier((packed, sums))
    sums = tree_sum(sums, "sample", PEERS, (2, 4, 6))
    sums = tree_sum(sums, "sample", PEERS, (1,))
    rows = jnp.arange(ROWS, dtype=jnp.int32)
    same = (target[:, None] == target[None, :]) & (rows[:, None] < rows[None, :])
    place = target * 4 + jnp.sum(same.astype(jnp.int32), 0)
    slot = (jnp.arange(4 * PEERS, dtype=jnp.int32)[:, None] == place[None, :]).astype(jnp.bfloat16)
    small = jnp.concatenate([both] + bf16_terms(logp), -1)
    slotted = jnp.dot(slot, small, preferred_element_type=jnp.float32).astype(jnp.bfloat16)
    new_rows = slotted[:, :WIDTH].reshape(PEERS, 4, WIDTH)
    mine = y * 2 + core
    share = sums[:ROWS].reshape(SIDE, 2, SIDE, ROWS)
    share = lax.dynamic_index_in_dim(share, mine, 2, keepdims=False).reshape(SIDE, WIDTH)
    share = jnp.stack(bf16_terms(share), 1)[None]
    share = jnp.broadcast_to(share, (PLANES, SIDE, 3, WIDTH)).reshape(PEERS, 3, WIDTH)
    head = jnp.swapaxes(sums[ROWS:].reshape(OUTCOMES, 2, HEAD), 0, 1).reshape(SIDE, HEAD)
    head = lax.dynamic_index_in_dim(head, mine, 0, keepdims=False)
    head = jnp.broadcast_to(jnp.concatenate(bf16_terms(head)), (PEERS, 3 * HEAD))
    logp_row = slotted[:, WIDTH:].reshape(PEERS, 12 * OUTCOMES)
    gap = jnp.zeros((PEERS, WIDTH - 12 * OUTCOMES - 3 * HEAD), jnp.bfloat16)
    mixed = jnp.concatenate([logp_row, gap, head], -1)[:, None]
    tiles = jnp.concatenate([new_rows, mixed, share], 1)
    packed = pl.pallas_call(
        tile_kernel,
        out_shape=jax.ShapeDtypeStruct(packed.shape, packed.dtype),
        in_specs=[pl.BlockSpec(memory_space=pltpu.VMEM), ANY],
        out_specs=ANY,
        scratch_shapes=[pltpu.SemaphoreType.DMA],
        input_output_aliases={1: 0},
        compiler_params=pltpu.CompilerParams(vmem_limit_bytes=2 << 20),
        name="pack_tiles",
    )(tiles, packed)
    direct = exchanged(packed)

    codes = relayed[:, RELAY * LEVELS, : 2 * RELAY].astype(jnp.int32)
    shifts = [(0, 0), (1, 0), (3, 0), (2, 0), (2, 1), (1, 1), (3, 1), (0, 1)]
    onto = jnp.stack([lax.rem(y + dy, 4) * 2 + (core ^ dc) for dy, dc in shifts])
    came = jnp.stack([lax.rem(y - dy + 4, 4) * 2 + (core ^ dc) for dy, dc in shifts])
    onward = pl.pallas_call(
        forward_kernel,
        out_shape=[jax.ShapeDtypeStruct((LAST, WIDTH), jnp.bfloat16)] * SIDE,
        in_specs=[SMEM, SMEM, ANY],
        out_specs=[ANY] * SIDE,
        scratch_shapes=[
            pltpu.SMEM((SIDE * 2 * PLANES,), jnp.int32),
            pltpu.VMEM((PLANES, PIECE, WIDTH), jnp.bfloat16),
            pltpu.VMEM((LEVELS, WIDTH), jnp.bfloat16),
            pltpu.VMEM((8, WIDTH), jnp.bfloat16),
            pltpu.SemaphoreType.DMA((SIDE,)),
            pltpu.SemaphoreType.DMA((SIDE,)),
            pltpu.SemaphoreType.DMA,
        ],
        cost_estimate=pl.CostEstimate(flops=0, bytes_accessed=5 << 20, transcendentals=0),
        compiler_params=pltpu.CompilerParams(vmem_limit_bytes=4 << 20),
        name="pack_plane",
    )(codes, onto.astype(jnp.int32), relayed)
    def in_plane(x, k):
        dy, dc = shifts[k]
        pairs = [
            ((z * 4 + y0) * 2 + c0, (z * 4 + (y0 + dy) % 4) * 2 + (c0 ^ dc))
            for z in range(PLANES)
            for y0 in range(4)
            for c0 in range(2)
        ]
        return lax.ppermute(x, "sample", pairs)

    lasts = [onward[0]] + [in_plane(onward[k], k) for k in range(1, SIDE)]
    came = came.astype(jnp.int32)
    over = pl.pallas_call(
        flag_kernel,
        grid=(1,),
        out_shape=jax.ShapeDtypeStruct((1,), jnp.int32),
        in_specs=[pl.BlockSpec((8, 128), lambda t: (LAST // 8 - 1, 0))] * SIDE,
        out_specs=SMEM,
        compiler_params=pltpu.CompilerParams(vmem_limit_bytes=2 << 20),
        name="flag",
    )(*lasts)

    def by_relay(lasts):
        return lasts

    def by_pairs(lasts):
        high = exchanged(pack_direct(2, target, cache))
        high = high[:, : 2 * LEVELS].reshape(PLANES, SIDE, 2 * LEVELS, WIDTH)
        high = jnp.swapaxes(high, 0, 1).reshape(SIDE, 2 * PLANES * LEVELS, WIDTH)
        high = jnp.pad(high, ((0, 0), (0, LAST - 2 * PLANES * LEVELS), (0, 0)))
        return [lax.dynamic_index_in_dim(high, came[k], 0, keepdims=False) for k in range(SIDE)]

    direct, over = lax.optimization_barrier((direct, over))
    piece, head = pl.pallas_call(
        plane_sum_kernel,
        grid=(1,),
        out_shape=(
            jax.ShapeDtypeStruct((2 * SIDE, ROWS), jnp.float32),
            jax.ShapeDtypeStruct((OUTCOMES, ROWS), jnp.float32),
        ),
        in_specs=[pl.BlockSpec((PEERS, 8, WIDTH), lambda t: (0, 2 * LEVELS // 8, 0))],
        out_specs=(
            pl.BlockSpec((2 * SIDE, ROWS), lambda t: (0, 0)),
            pl.BlockSpec((OUTCOMES, ROWS), lambda t: (0, 0)),
        ),
        compiler_params=pltpu.CompilerParams(vmem_limit_bytes=4 << 20),
        name="plane_sum",
    )(direct)
    other = lax.ppermute(piece, "sample", xor_pairs(PEERS, 1))
    piece = jnp.where(
        core == 0, jnp.concatenate([piece, other], 0), jnp.concatenate([other, piece], 0)
    )
    direct, lasts, piece = lax.optimization_barrier((direct, lasts, piece))
    lasts = lax.cond(over[0] > 0, by_pairs, by_relay, lasts)
    piece, lasts = lax.optimization_barrier((piece, lasts))
    shares = jnp.stack([piece] + [in_plane(piece, shifts.index((dy, 0))) for dy in (1, 2, 3)])
    rows_y = jnp.arange(4, dtype=jnp.int32)
    ours = (lax.rem(y - rows_y + 4, 4)[:, None] == rows_y[None, :])[..., None, None]
    grad_out = jnp.sum(jnp.where(ours, shares[None], 0.0), 1).reshape(ROWS, ROWS)
    new_cache, log_probs = settle(came, direct, lasts)
    return (jnp.swapaxes(new_cache, 0, 1), log_probs.T, grad_out, head.T)


def solution(mesh):
    split = P(("sample", "rep"))
    whole = P()
    return jax.shard_map(
        on_device,
        mesh=mesh,
        in_specs=(split, split) + (whole,) * 6 + (split,) * 3,
        out_specs=(split, split, whole, whole),
        check_vma=False,
    )
```

```python
import functools
import math

import jax
import jax.numpy as jnp
from jax import lax
from jax.experimental import pallas as pl
from jax.experimental.pallas import tpu as pltpu
from jax.sharding import PartitionSpec as P

HEADS = 4
OUTCOMES = 4
HEAD = 64
ROWS = 128
LEVELS = 48
WIDTH = 256
PEERS = 64
PLANES = 8
SIDE = 8
RELAY = 8
DIRECT = 2 * LEVELS + 8
PIECE = RELAY * LEVELS + 8
LAST = 2 * PLANES * LEVELS + 8
ANY = pl.BlockSpec(memory_space=pl.ANY)
SMEM = pl.BlockSpec(memory_space=pltpu.SMEM)


def decode_rows(tokens, cache, coef, chosen, gain, w_query, w_key, w_value, w_out, w_head):
    count = tokens.shape[0]
    width = tokens.shape[1]
    levels = cache.shape[1]
    size = width // HEADS
    xf = tokens.astype(jnp.float32)
    normed = (xf * lax.rsqrt(jnp.mean(xf * xf, -1, keepdims=True) + 1e-05) * gain).astype(
        jnp.bfloat16
    )
    query = (
        jnp.dot(normed, w_query, preferred_element_type=jnp.float32) * (1.0 / math.sqrt(size))
    ).astype(jnp.bfloat16)
    key_new = jnp.dot(normed, w_key, preferred_element_type=jnp.float32).astype(jnp.bfloat16)
    value_new = jnp.dot(normed, w_value, preferred_element_type=jnp.float32).astype(jnp.bfloat16)
    query_heads = query.reshape(count, HEADS, size)
    key_rows = cache[:, :, :width].reshape(count, levels, HEADS, size)
    value_rows = cache[:, :, width:].reshape(count, levels, HEADS, size)
    cached_scores = jnp.einsum(
        "yfn,yjfn->yfj", query_heads, key_rows, preferred_element_type=jnp.float32
    )
    score_self = jnp.sum(
        query_heads.astype(jnp.float32) * key_new.astype(jnp.float32).reshape(count, HEADS, size),
        -1,
    )
    top = jnp.maximum(jnp.max(cached_scores, -1), score_self)
    exp_cache = jnp.exp(cached_scores - top[..., None])
    exp_self = jnp.exp(score_self - top)
    total = jnp.sum(exp_cache, -1) + exp_self
    cached_weights = (exp_cache / total[..., None]).astype(jnp.bfloat16)
    weight_self = (exp_self / total).astype(jnp.bfloat16)
    attention_output = jnp.einsum(
        "jat,jtaf->jaf", cached_weights, value_rows, preferred_element_type=jnp.float32
    )
    attention_output = attention_output + weight_self.astype(jnp.float32)[
        ..., None
    ] * value_new.astype(jnp.float32).reshape(count, HEADS, size)
    attention_output = attention_output.reshape(count, width).astype(jnp.bfloat16)
    hidden = (xf + jnp.dot(attention_output, w_out, preferred_element_type=jnp.float32)).astype(
        jnp.bfloat16
    )
    logits = jnp.dot(hidden, w_head, preferred_element_type=jnp.float32)
    logp = jax.nn.log_softmax(logits, -1)
    picked = (chosen[:, None] == jnp.arange(OUTCOMES, dtype=jnp.int32)[None, :]).astype(jnp.float32)
    dlog = coef[:, None] * (picked - jnp.exp(logp))
    grad_head = jnp.dot(dlog.T, hidden.astype(jnp.float32), precision=lax.Precision.HIGHEST)
    hidden_gradient = jnp.dot(dlog, w_head.astype(jnp.float32).T, precision=lax.Precision.HIGHEST)
    grad_out = jnp.dot(
        attention_output.astype(jnp.float32).T, hidden_gradient, precision=lax.Precision.HIGHEST
    )
    both = jnp.concatenate([key_new, value_new], -1)
    return (both, logp, grad_out, grad_head)


def cleared(ref, count):
    for i in range(count):
        ref[i] = 0


def relay_kernel(dest, cache, out, count, filled, meta, held, rows_sem, out_sem):
    cleared(count, PEERS)
    cleared(filled, PLANES + 1)
    meta[...] = jnp.full(meta.shape, -1.0, jnp.float32)
    lane = lax.broadcasted_iota(jnp.int32, (8, WIDTH), 1)

    @pl.loop(0, ROWS, unroll=8)
    def _(i):
        d = dest[i]
        rank = count[d]
        count[d] = rank + 1

        @pl.when(rank >= 2)
        def _():
            plane = lax.div(d, SIDE)
            at = filled[plane]
            filled[plane] = at + 1

            @pl.when(at < RELAY)
            def _():
                start = pl.multiple_of(at * LEVELS, LEVELS)
                pltpu.make_async_copy(
                    cache.at[i], held.at[plane, pl.ds(start, LEVELS)], rows_sem
                ).start()
                code = lax.rem(d, SIDE) * 2 + rank - 2
                meta[plane] = jnp.where(lane == at, code.astype(jnp.float32), meta[plane])
                filled[PLANES] += 1

    most = filled[0]
    for plane in range(1, PLANES):
        most = jnp.maximum(most, filled[plane])
    over = jnp.where(most > RELAY, 1.0, 0.0)
    for plane in range(PLANES):
        tile = jnp.where(lane == RELAY, over, meta[plane])
        held[plane, RELAY * LEVELS :, :] = tile.astype(jnp.bfloat16)

    @pl.loop(0, filled[PLANES])
    def _(i):
        pltpu.make_async_copy(cache.at[0], held.at[0, pl.ds(0, LEVELS)], rows_sem).wait()

    whole = pltpu.make_async_copy(held, out, out_sem)
    whole.start()
    whole.wait()


def direct_kernel(low, dest, cache, out, count, zero, rows_sem):
    cleared(count, PEERS)
    zero[...] = jnp.zeros(zero.shape, zero.dtype)

    @pl.loop(0, ROWS)
    def _(i):
        d = dest[i]
        rank = count[d]
        count[d] = rank + 1

        @pl.when((rank >= low) & (rank < low + 2))
        def _():
            start = pl.multiple_of((rank - low) * LEVELS, LEVELS)
            pltpu.make_async_copy(cache.at[i], out.at[d, pl.ds(start, LEVELS)], rows_sem).start()

    @pl.loop(0, PEERS)
    def _(d):
        for r in range(2):

            @pl.when(count[d] <= low + r)
            def _():
                pltpu.make_async_copy(zero, out.at[d, pl.ds(r * LEVELS, LEVELS)], rows_sem).start()

    whole = out.at[:, pl.ds(0, 2 * LEVELS)]
    pltpu.make_async_copy(whole, whole, rows_sem).wait()


def tile_kernel(tiles, rows, out, sem):
    copy = pltpu.make_async_copy(tiles, out.at[:, pl.ds(2 * LEVELS, 8)], sem)
    copy.start()
    copy.wait()


def plane_sum_kernel(tiles, out, head):
    x = jnp.sum(tiles[...].astype(jnp.float32).reshape(PLANES, SIDE, 8, WIDTH), 0)
    piece = x[:, 5, :] + (x[:, 6, :] + x[:, 7, :])
    out[...] = jnp.concatenate([piece[:, :ROWS], piece[:, ROWS:]], 0)
    part = x[:, 4, HEAD : 2 * HEAD] + (x[:, 4, 2 * HEAD : 3 * HEAD] + x[:, 4, 3 * HEAD :])
    head[...] = jnp.concatenate([part[:OUTCOMES], part[OUTCOMES:]], 1)


def forward_kernel(codes, side, got, *refs):
    outs, (source, held, zero, tile, rows_sem, tile_sem, got_sem) = refs[:SIDE], refs[SIDE:]
    load = pltpu.make_async_copy(got, held, got_sem)
    load.start()
    zero[...] = jnp.zeros(zero.shape, zero.dtype)

    @pl.loop(0, SIDE * 2 * PLANES)
    def _(i):
        source[i] = -1

    over = codes[0, RELAY]
    for plane in range(PLANES):
        over = jnp.maximum(over, codes[plane, RELAY])
        for at in range(RELAY):
            code = codes[plane, at]

            @pl.when(code >= 0)
            def _():
                source[code * PLANES + plane] = at

    tile[...] = jnp.full(tile.shape, over.astype(jnp.float32)).astype(jnp.bfloat16)
    load.wait()
    for k, out in enumerate(outs):
        pltpu.make_async_copy(tile, out.at[pl.ds(LAST - 8, 8)], tile_sem.at[k]).start()
        peer = side[k]

        @pl.loop(0, 2 * PLANES)
        def _(i):
            plane = lax.div(i, 2)
            r = lax.rem(i, 2)
            at = source[(peer * 2 + r) * PLANES + plane]
            to = out.at[pl.ds(pl.multiple_of(i * LEVELS, LEVELS), LEVELS)]

            @pl.when(at >= 0)
            def _():
                start = pl.multiple_of(at * LEVELS, LEVELS)
                pltpu.make_async_copy(
                    held.at[plane, pl.ds(start, LEVELS)], to, rows_sem.at[k]
                ).start()

            @pl.when(at < 0)
            def _():
                pltpu.make_async_copy(zero, to, rows_sem.at[k]).start()

    for k, out in enumerate(outs):
        whole = out.at[pl.ds(0, LAST - 8)]
        pltpu.make_async_copy(whole, whole, rows_sem.at[k]).wait()
        pltpu.make_async_copy(tile, out.at[pl.ds(LAST - 8, 8)], tile_sem.at[k]).wait()


def flag_kernel(*refs):
    most = refs[0][...].astype(jnp.float32)
    for ref in refs[1:SIDE]:
        most = jnp.maximum(most, ref[...].astype(jnp.float32))
    refs[SIDE][0] = jnp.where(jnp.max(most) > 0, 1, 0).astype(jnp.int32)


def chosen_rows(count, size, pick):
    i = lax.broadcasted_iota(jnp.int32, (count, size), 0)
    j = lax.broadcasted_iota(jnp.int32, (count, size), 1)
    return (j == pick(i)).astype(jnp.float32).astype(jnp.bfloat16)


def settle_kernel(side, direct, *refs):
    lasts, (out, logp, held, kept) = refs[:SIDE], refs[SIDE:]
    t = pl.program_id(0)
    for k, last in enumerate(lasts):
        held[side[k]] = last[...]
    turn = chosen_rows(WIDTH, WIDTH, lambda i: lax.rem(i, 16) * 16 + lax.div(i, 16))
    for group in range(2):
        for low in range(0, LEVELS, 16):
            parts = []
            for j in range(4 * group, 4 * group + 4):
                for ref in (direct, held):
                    for r in range(2):
                        start = r * LEVELS + low
                        parts.append(ref[j, start : start + 16, :])
            turned = jnp.dot(turn, jnp.concatenate(parts, 0), preferred_element_type=jnp.float32)
            turned = turned.astype(jnp.bfloat16).reshape(16, 16, WIDTH)
            out[low : low + 16, 16 * group : 16 * group + 16, :] = turned
    tiles = jnp.concatenate([direct[j, 2 * LEVELS :, :] for j in range(SIDE)], 0)
    new = chosen_rows(4 * SIDE, 8 * SIDE, lambda i: lax.div(i, 4) * 8 + lax.rem(i, 4))
    out[LEVELS] = jnp.dot(new, tiles, preferred_element_type=jnp.float32).astype(jnp.bfloat16)
    spread = chosen_rows(4 * SIDE, 8 * SIDE, lambda i: lax.div(i, 4) * 8 + 4)
    terms = jnp.dot(spread, tiles, preferred_element_type=jnp.float32)
    slot = lax.broadcasted_iota(jnp.int32, terms.shape, 0)
    lane = lax.broadcasted_iota(jnp.int32, terms.shape, 1)
    mine = lax.div(lane, 3 * OUTCOMES) == lax.rem(slot, 4)
    rows = pl.ds(pl.multiple_of(t * 4 * SIDE, 4 * SIDE), 4 * SIDE)
    kept[rows, :] = jnp.where(mine, terms, 0.0).astype(jnp.bfloat16)

    @pl.when(t == PLANES - 1)
    def _():
        outcome = lax.broadcasted_iota(jnp.int32, (8, WIDTH), 0)
        lane = lax.broadcasted_iota(jnp.int32, (8, WIDTH), 1)
        gather = (lax.rem(lane, OUTCOMES) == outcome).astype(jnp.float32).astype(jnp.bfloat16)
        found = lax.dot_general(
            gather, kept[...], (((1,), (1,)), ((), ())), preferred_element_type=jnp.float32
        )
        logp[...] = found[:OUTCOMES]


def settle(side, direct, lasts):
    return pl.pallas_call(
        settle_kernel,
        grid=(PLANES,),
        out_shape=(
            jax.ShapeDtypeStruct((LEVELS + 1, 4 * PEERS, WIDTH), jnp.bfloat16),
            jax.ShapeDtypeStruct((OUTCOMES, 4 * PEERS), jnp.float32),
        ),
        in_specs=[SMEM, pl.BlockSpec((SIDE, DIRECT, WIDTH), lambda t: (t, 0, 0))]
        + [pl.BlockSpec((2 * LEVELS, WIDTH), lambda t: (t, 0))] * SIDE,
        out_specs=(
            pl.BlockSpec((LEVELS + 1, 4 * SIDE, WIDTH), lambda t: (0, t, 0)),
            pl.BlockSpec((OUTCOMES, 4 * PEERS), lambda t: (0, 0)),
        ),
        scratch_shapes=[
            pltpu.VMEM((SIDE, 2 * LEVELS, WIDTH), jnp.bfloat16),
            pltpu.VMEM((4 * PEERS, WIDTH), jnp.bfloat16),
        ],
        compiler_params=pltpu.CompilerParams(vmem_limit_bytes=12 << 20),
        cost_estimate=pl.CostEstimate(flops=2 << 30, bytes_accessed=14 << 20, transcendentals=0),
        name="settle",
    )(side, direct, *lasts)


def pack_direct(low, dest, cache):
    return pl.pallas_call(
        functools.partial(direct_kernel, low),
        out_shape=jax.ShapeDtypeStruct((PEERS, DIRECT, WIDTH), jnp.bfloat16),
        in_specs=[SMEM, pl.BlockSpec(memory_space=pltpu.VMEM)],
        out_specs=ANY,
        scratch_shapes=[
            pltpu.SMEM((PEERS,), jnp.int32),
            pltpu.VMEM((LEVELS, WIDTH), jnp.bfloat16),
            pltpu.SemaphoreType.DMA,
        ],
        cost_estimate=pl.CostEstimate(flops=0, bytes_accessed=10 << 20, transcendentals=0),
        compiler_params=pltpu.CompilerParams(vmem_limit_bytes=8 << 20),
        name="pack_direct",
    )(dest, cache)


def exchanged(x, groups=None):
    return lax.all_to_all(
        x, "sample", split_axis=0, concat_axis=0, tiled=True, axis_index_groups=groups
    )


def xor_pairs(size, bit):
    return [(i, i ^ bit) for i in range(size)]


def tree_sum(x, axis, size, bits):
    terms = [x] + [lax.ppermute(x, axis, xor_pairs(size, bit)) for bit in bits]
    while len(terms) > 1:
        terms = [terms[i] + terms[i + 1] for i in range(0, len(terms), 2)]
    return terms[0]


def bf16_terms(x):
    terms = []
    for _ in range(3):
        term = lax.reduce_precision(x, 8, 7)
        terms.append(term.astype(jnp.bfloat16))
        x = x - term
    return terms


def on_device(tokens, cache, gain, w_query, w_key, w_value, w_out, w_head, coef, chosen, dest):
    target = dest[:, 0]
    me = lax.axis_index("sample")
    y, core = lax.rem(lax.div(me, 2), 4), lax.rem(me, 2)

    relay = pl.pallas_call(
        relay_kernel,
        out_shape=jax.ShapeDtypeStruct((PLANES, PIECE, WIDTH), jnp.bfloat16),
        in_specs=[SMEM, ANY],
        out_specs=ANY,
        scratch_shapes=[
            pltpu.SMEM((PEERS,), jnp.int32),
            pltpu.SMEM((PLANES + 1,), jnp.int32),
            pltpu.VMEM((PLANES, 8, WIDTH), jnp.float32),
            pltpu.VMEM((PLANES, PIECE, WIDTH), jnp.bfloat16),
            pltpu.SemaphoreType.DMA,
            pltpu.SemaphoreType.DMA,
        ],
        compiler_params=pltpu.CompilerParams(vmem_limit_bytes=4 << 20),
        name="pack_relay",
    )(target, cache)
    relayed = exchanged(relay, [[z * SIDE + i for z in range(PLANES)] for i in range(SIDE)])

    both, logp, grad_out, grad_head = decode_rows(
        tokens, cache, coef, chosen, gain, w_query, w_key, w_value, w_out, w_head
    )
    sums = jnp.concatenate([grad_out, grad_head], 0)
    target_now, sums = lax.optimization_barrier((target, sums))
    packed = pack_direct(0, target_now, cache)
    sums = tree_sum(sums, "rep", 4, (1, 2, 3))
    packed, sums = lax.optimization_barrier((packed, sums))
    sums = tree_sum(sums, "sample", PEERS, (2, 4, 6))
    sums = tree_sum(sums, "sample", PEERS, (1,))
    rows = jnp.arange(ROWS, dtype=jnp.int32)
    same = (target[:, None] == target[None, :]) & (rows[:, None] < rows[None, :])
    place = target * 4 + jnp.sum(same.astype(jnp.int32), 0)
    slot = (jnp.arange(4 * PEERS, dtype=jnp.int32)[:, None] == place[None, :]).astype(jnp.bfloat16)
    small = jnp.concatenate([both] + bf16_terms(logp), -1)
    slotted = jnp.dot(slot, small, preferred_element_type=jnp.float32).astype(jnp.bfloat16)
    new_rows = slotted[:, :WIDTH].reshape(PEERS, 4, WIDTH)
    mine = y * 2 + core
    share = sums[:ROWS].reshape(SIDE, 2, SIDE, ROWS)
    share = lax.dynamic_index_in_dim(share, mine, 2, keepdims=False).reshape(SIDE, WIDTH)
    share = jnp.stack(bf16_terms(share), 1)[None]
    share = jnp.broadcast_to(share, (PLANES, SIDE, 3, WIDTH)).reshape(PEERS, 3, WIDTH)
    head = jnp.swapaxes(sums[ROWS:].reshape(OUTCOMES, 2, HEAD), 0, 1).reshape(SIDE, HEAD)
    head = lax.dynamic_index_in_dim(head, mine, 0, keepdims=False)
    head = jnp.broadcast_to(jnp.concatenate(bf16_terms(head)), (PEERS, 3 * HEAD))
    logp_row = slotted[:, WIDTH:].reshape(PEERS, 12 * OUTCOMES)
    gap = jnp.zeros((PEERS, WIDTH - 12 * OUTCOMES - 3 * HEAD), jnp.bfloat16)
    mixed = jnp.concatenate([logp_row, gap, head], -1)[:, None]
    tiles = jnp.concatenate([new_rows, mixed, share], 1)
    packed = pl.pallas_call(
        tile_kernel,
        out_shape=jax.ShapeDtypeStruct(packed.shape, packed.dtype),
        in_specs=[pl.BlockSpec(memory_space=pltpu.VMEM), ANY],
        out_specs=ANY,
        scratch_shapes=[pltpu.SemaphoreType.DMA],
        input_output_aliases={1: 0},
        compiler_params=pltpu.CompilerParams(vmem_limit_bytes=2 << 20),
        name="pack_tiles",
    )(tiles, packed)
    direct = exchanged(packed)

    codes = relayed[:, RELAY * LEVELS, : 2 * RELAY].astype(jnp.int32)
    shifts = [(0, 0), (1, 0), (3, 0), (2, 0), (2, 1), (1, 1), (3, 1), (0, 1)]
    onto = jnp.stack([lax.rem(y + dy, 4) * 2 + (core ^ dc) for dy, dc in shifts])
    came = jnp.stack([lax.rem(y - dy + 4, 4) * 2 + (core ^ dc) for dy, dc in shifts])
    onward = pl.pallas_call(
        forward_kernel,
        out_shape=[jax.ShapeDtypeStruct((LAST, WIDTH), jnp.bfloat16)] * SIDE,
        in_specs=[SMEM, SMEM, ANY],
        out_specs=[ANY] * SIDE,
        scratch_shapes=[
            pltpu.SMEM((SIDE * 2 * PLANES,), jnp.int32),
            pltpu.VMEM((PLANES, PIECE, WIDTH), jnp.bfloat16),
            pltpu.VMEM((LEVELS, WIDTH), jnp.bfloat16),
            pltpu.VMEM((8, WIDTH), jnp.bfloat16),
            pltpu.SemaphoreType.DMA((SIDE,)),
            pltpu.SemaphoreType.DMA((SIDE,)),
            pltpu.SemaphoreType.DMA,
        ],
        cost_estimate=pl.CostEstimate(flops=0, bytes_accessed=5 << 20, transcendentals=0),
        compiler_params=pltpu.CompilerParams(vmem_limit_bytes=4 << 20),
        name="pack_plane",
    )(codes, onto.astype(jnp.int32), relayed)
    def in_plane(x, k):
        dy, dc = shifts[k]
        pairs = [
            ((z * 4 + y0) * 2 + c0, (z * 4 + (y0 + dy) % 4) * 2 + (c0 ^ dc))
            for z in range(PLANES)
            for y0 in range(4)
            for c0 in range(2)
        ]
        return lax.ppermute(x, "sample", pairs)

    lasts = [onward[0]] + [in_plane(onward[k], k) for k in range(1, SIDE)]
    came = came.astype(jnp.int32)
    over = pl.pallas_call(
        flag_kernel,
        grid=(1,),
        out_shape=jax.ShapeDtypeStruct((1,), jnp.int32),
        in_specs=[pl.BlockSpec((8, 128), lambda t: (LAST // 8 - 1, 0))] * SIDE,
        out_specs=SMEM,
        compiler_params=pltpu.CompilerParams(vmem_limit_bytes=2 << 20),
        name="flag",
    )(*lasts)

    direct, over = lax.optimization_barrier((direct, over))
    piece, head = pl.pallas_call(
        plane_sum_kernel,
        grid=(1,),
        out_shape=(
            jax.ShapeDtypeStruct((2 * SIDE, ROWS), jnp.float32),
            jax.ShapeDtypeStruct((OUTCOMES, ROWS), jnp.float32),
        ),
        in_specs=[pl.BlockSpec((PEERS, 8, WIDTH), lambda t: (0, 2 * LEVELS // 8, 0))],
        out_specs=(
            pl.BlockSpec((2 * SIDE, ROWS), lambda t: (0, 0)),
            pl.BlockSpec((OUTCOMES, ROWS), lambda t: (0, 0)),
        ),
        compiler_params=pltpu.CompilerParams(vmem_limit_bytes=4 << 20),
        name="plane_sum",
    )(direct)
    other = lax.ppermute(piece, "sample", xor_pairs(PEERS, 1))
    piece = jnp.where(
        core == 0, jnp.concatenate([piece, other], 0), jnp.concatenate([other, piece], 0)
    )
    direct, lasts, piece = lax.optimization_barrier((direct, lasts, piece))
    shares = jnp.stack([piece] + [in_plane(piece, shifts.index((dy, 0))) for dy in (1, 2, 3)])
    rows_y = jnp.arange(4, dtype=jnp.int32)
    ours = (lax.rem(y - rows_y + 4, 4)[:, None] == rows_y[None, :])[..., None, None]
    grad_out = jnp.sum(jnp.where(ours, shares[None], 0.0), 1).reshape(ROWS, ROWS)
    new_cache, log_probs = settle(came, direct, lasts)

    def by_relay(new_cache):
        return new_cache

    def by_pairs(new_cache):
        high = exchanged(pack_direct(2, target, cache))
        high = high[:, : 2 * LEVELS].reshape(PLANES, SIDE, 2 * LEVELS, WIDTH)
        high = jnp.swapaxes(high, 0, 1).reshape(SIDE, 2 * PLANES * LEVELS, WIDTH)
        high = jnp.pad(high, ((0, 0), (0, LAST - 2 * PLANES * LEVELS), (0, 0)))
        lasts = [lax.dynamic_index_in_dim(high, came[k], 0, keepdims=False) for k in range(SIDE)]
        return settle(came, direct, lasts)[0]

    new_cache = lax.cond(over[0] > 0, by_pairs, by_relay, new_cache)
    return (jnp.swapaxes(new_cache, 0, 1), log_probs.T, grad_out, head.T)


def solution(mesh):
    split = P(("sample", "rep"))
    whole = P()
    return jax.shard_map(
        on_device,
        mesh=mesh,
        in_specs=(split, split) + (whole,) * 6 + (split,) * 3,
        out_specs=(split, split, whole, whole),
        check_vma=False,
    )
```

```python
import functools
import math

import jax
import jax.numpy as jnp
from jax import lax
from jax.experimental import pallas as pl
from jax.experimental.pallas import tpu as pltpu
from jax.sharding import PartitionSpec as P

HEADS = 4
OUTCOMES = 4
HEAD = 64
ROWS = 128
LEVELS = 48
WIDTH = 256
PEERS = 64
PLANES = 8
SIDE = 8
RELAY = 8
DIRECT = 2 * LEVELS + 8
PIECE = RELAY * LEVELS + 8
LAST = 2 * PLANES * LEVELS + 8
ANY = pl.BlockSpec(memory_space=pl.ANY)
SMEM = pl.BlockSpec(memory_space=pltpu.SMEM)


def decode_rows(tokens, cache, coef, chosen, gain, w_query, w_key, w_value, w_out, w_head):
    count = tokens.shape[0]
    width = tokens.shape[1]
    levels = cache.shape[1]
    size = width // HEADS
    xf = tokens.astype(jnp.float32)
    normed = (xf * lax.rsqrt(jnp.mean(xf * xf, -1, keepdims=True) + 1e-05) * gain).astype(
        jnp.bfloat16
    )
    query = (
        jnp.dot(normed, w_query, preferred_element_type=jnp.float32) * (1.0 / math.sqrt(size))
    ).astype(jnp.bfloat16)
    key_new = jnp.dot(normed, w_key, preferred_element_type=jnp.float32).astype(jnp.bfloat16)
    value_new = jnp.dot(normed, w_value, preferred_element_type=jnp.float32).astype(jnp.bfloat16)
    query_heads = query.reshape(count, HEADS, size)
    key_rows = cache[:, :, :width].reshape(count, levels, HEADS, size)
    value_rows = cache[:, :, width:].reshape(count, levels, HEADS, size)
    cached_scores = jnp.einsum(
        "yfn,yjfn->yfj", query_heads, key_rows, preferred_element_type=jnp.float32
    )
    score_self = jnp.sum(
        query_heads.astype(jnp.float32) * key_new.astype(jnp.float32).reshape(count, HEADS, size),
        -1,
    )
    top = jnp.maximum(jnp.max(cached_scores, -1), score_self)
    exp_cache = jnp.exp(cached_scores - top[..., None])
    exp_self = jnp.exp(score_self - top)
    total = jnp.sum(exp_cache, -1) + exp_self
    cached_weights = (exp_cache / total[..., None]).astype(jnp.bfloat16)
    weight_self = (exp_self / total).astype(jnp.bfloat16)
    attention_output = jnp.einsum(
        "jat,jtaf->jaf", cached_weights, value_rows, preferred_element_type=jnp.float32
    )
    attention_output = attention_output + weight_self.astype(jnp.float32)[
        ..., None
    ] * value_new.astype(jnp.float32).reshape(count, HEADS, size)
    attention_output = attention_output.reshape(count, width).astype(jnp.bfloat16)
    hidden = (xf + jnp.dot(attention_output, w_out, preferred_element_type=jnp.float32)).astype(
        jnp.bfloat16
    )
    logits = jnp.dot(hidden, w_head, preferred_element_type=jnp.float32)
    logp = jax.nn.log_softmax(logits, -1)
    picked = (chosen[:, None] == jnp.arange(OUTCOMES, dtype=jnp.int32)[None, :]).astype(jnp.float32)
    dlog = coef[:, None] * (picked - jnp.exp(logp))
    grad_head = jnp.dot(dlog.T, hidden.astype(jnp.float32), precision=lax.Precision.HIGHEST)
    hidden_gradient = jnp.dot(dlog, w_head.astype(jnp.float32).T, precision=lax.Precision.HIGHEST)
    grad_out = jnp.dot(
        attention_output.astype(jnp.float32).T, hidden_gradient, precision=lax.Precision.HIGHEST
    )
    both = jnp.concatenate([key_new, value_new], -1)
    return (both, logp, grad_out, grad_head)


def cleared(ref, count):
    for i in range(count):
        ref[i] = 0


def relay_kernel(dest, cache, out, count, filled, meta, held, rows_sem, out_sem):
    cleared(count, PEERS)
    cleared(filled, PLANES + 1)
    meta[...] = jnp.full(meta.shape, -1.0, jnp.float32)
    lane = lax.broadcasted_iota(jnp.int32, (8, WIDTH), 1)

    @pl.loop(0, ROWS, unroll=8)
    def _(i):
        d = dest[i]
        rank = count[d]
        count[d] = rank + 1

        @pl.when(rank >= 2)
        def _():
            plane = lax.div(d, SIDE)
            at = filled[plane]
            filled[plane] = at + 1

            @pl.when(at < RELAY)
            def _():
                start = pl.multiple_of(at * LEVELS, LEVELS)
                pltpu.make_async_copy(
                    cache.at[i], held.at[plane, pl.ds(start, LEVELS)], rows_sem
                ).start()
                code = lax.rem(d, SIDE) * 2 + rank - 2
                meta[plane] = jnp.where(lane == at, code.astype(jnp.float32), meta[plane])
                filled[PLANES] += 1

    most = filled[0]
    for plane in range(1, PLANES):
        most = jnp.maximum(most, filled[plane])
    over = jnp.where(most > RELAY, 1.0, 0.0)
    for plane in range(PLANES):
        tile = jnp.where(lane == RELAY, over, meta[plane])
        held[plane, RELAY * LEVELS :, :] = tile.astype(jnp.bfloat16)

    @pl.loop(0, filled[PLANES])
    def _(i):
        pltpu.make_async_copy(cache.at[0], held.at[0, pl.ds(0, LEVELS)], rows_sem).wait()

    whole = pltpu.make_async_copy(held, out, out_sem)
    whole.start()
    whole.wait()


def direct_kernel(low, dest, cache, out, count, zero, rows_sem):
    cleared(count, PEERS)
    zero[...] = jnp.zeros(zero.shape, zero.dtype)

    @pl.loop(0, ROWS)
    def _(i):
        d = dest[i]
        rank = count[d]
        count[d] = rank + 1

        @pl.when((rank >= low) & (rank < low + 2))
        def _():
            start = pl.multiple_of((rank - low) * LEVELS, LEVELS)
            pltpu.make_async_copy(cache.at[i], out.at[d, pl.ds(start, LEVELS)], rows_sem).start()

    @pl.loop(0, PEERS)
    def _(d):
        for r in range(2):

            @pl.when(count[d] <= low + r)
            def _():
                pltpu.make_async_copy(zero, out.at[d, pl.ds(r * LEVELS, LEVELS)], rows_sem).start()

    whole = out.at[:, pl.ds(0, 2 * LEVELS)]
    pltpu.make_async_copy(whole, whole, rows_sem).wait()


def tile_kernel(tiles, rows, out, sem):
    copy = pltpu.make_async_copy(tiles, out.at[:, pl.ds(2 * LEVELS, 8)], sem)
    copy.start()
    copy.wait()


def plane_sum_kernel(tiles, out, head):
    x = jnp.sum(tiles[...].astype(jnp.float32).reshape(PLANES, SIDE, 8, WIDTH), 0)
    piece = x[:, 5, :] + (x[:, 6, :] + x[:, 7, :])
    out[...] = jnp.concatenate([piece[:, :ROWS], piece[:, ROWS:]], 0)
    part = x[:, 4, HEAD : 2 * HEAD] + (x[:, 4, 2 * HEAD : 3 * HEAD] + x[:, 4, 3 * HEAD :])
    head[...] = jnp.concatenate([part[:OUTCOMES], part[OUTCOMES:]], 1)


def forward_kernel(codes, side, got, *refs):
    outs, (source, held, zero, tile, rows_sem, tile_sem, got_sem) = refs[:SIDE], refs[SIDE:]
    load = pltpu.make_async_copy(got, held, got_sem)
    load.start()
    zero[...] = jnp.zeros(zero.shape, zero.dtype)

    @pl.loop(0, SIDE * 2 * PLANES)
    def _(i):
        source[i] = -1

    over = codes[0, RELAY]
    for plane in range(PLANES):
        over = jnp.maximum(over, codes[plane, RELAY])
        for at in range(RELAY):
            code = codes[plane, at]

            @pl.when(code >= 0)
            def _():
                source[code * PLANES + plane] = at

    tile[...] = jnp.full(tile.shape, over.astype(jnp.float32)).astype(jnp.bfloat16)
    load.wait()
    for k, out in enumerate(outs):
        pltpu.make_async_copy(tile, out.at[pl.ds(LAST - 8, 8)], tile_sem.at[k]).start()
        peer = side[k]

        @pl.loop(0, 2 * PLANES)
        def _(i):
            plane = lax.div(i, 2)
            r = lax.rem(i, 2)
            at = source[(peer * 2 + r) * PLANES + plane]
            to = out.at[pl.ds(pl.multiple_of(i * LEVELS, LEVELS), LEVELS)]

            @pl.when(at >= 0)
            def _():
                start = pl.multiple_of(at * LEVELS, LEVELS)
                pltpu.make_async_copy(
                    held.at[plane, pl.ds(start, LEVELS)], to, rows_sem.at[k]
                ).start()

            @pl.when(at < 0)
            def _():
                pltpu.make_async_copy(zero, to, rows_sem.at[k]).start()

    for k, out in enumerate(outs):
        whole = out.at[pl.ds(0, LAST - 8)]
        pltpu.make_async_copy(whole, whole, rows_sem.at[k]).wait()
        pltpu.make_async_copy(tile, out.at[pl.ds(LAST - 8, 8)], tile_sem.at[k]).wait()


def flag_kernel(*refs):
    most = refs[0][...].astype(jnp.float32)
    for ref in refs[1:SIDE]:
        most = jnp.maximum(most, ref[...].astype(jnp.float32))
    refs[SIDE][0] = jnp.where(jnp.max(most) > 0, 1, 0).astype(jnp.int32)


def chosen_rows(count, size, pick):
    i = lax.broadcasted_iota(jnp.int32, (count, size), 0)
    j = lax.broadcasted_iota(jnp.int32, (count, size), 1)
    return (j == pick(i)).astype(jnp.float32).astype(jnp.bfloat16)


def settle_kernel(side, direct, *refs):
    lasts, (out, logp, held, kept) = refs[:SIDE], refs[SIDE:]
    t = pl.program_id(0)
    for k, last in enumerate(lasts):
        held[side[k]] = last[...]
    turn = chosen_rows(WIDTH, WIDTH, lambda i: lax.rem(i, 16) * 16 + lax.div(i, 16))
    for group in range(2):
        for low in range(0, LEVELS, 16):
            parts = []
            for j in range(4 * group, 4 * group + 4):
                for ref in (direct, held):
                    for r in range(2):
                        start = r * LEVELS + low
                        parts.append(ref[j, start : start + 16, :])
            turned = jnp.dot(turn, jnp.concatenate(parts, 0), preferred_element_type=jnp.float32)
            turned = turned.astype(jnp.bfloat16).reshape(16, 16, WIDTH)
            out[low : low + 16, 16 * group : 16 * group + 16, :] = turned
    tiles = jnp.concatenate([direct[j, 2 * LEVELS :, :] for j in range(SIDE)], 0)
    new = chosen_rows(4 * SIDE, 8 * SIDE, lambda i: lax.div(i, 4) * 8 + lax.rem(i, 4))
    out[LEVELS] = jnp.dot(new, tiles, preferred_element_type=jnp.float32).astype(jnp.bfloat16)
    spread = chosen_rows(4 * SIDE, 8 * SIDE, lambda i: lax.div(i, 4) * 8 + 4)
    terms = jnp.dot(spread, tiles, preferred_element_type=jnp.float32)
    slot = lax.broadcasted_iota(jnp.int32, terms.shape, 0)
    lane = lax.broadcasted_iota(jnp.int32, terms.shape, 1)
    mine = lax.div(lane, 3 * OUTCOMES) == lax.rem(slot, 4)
    rows = pl.ds(pl.multiple_of(t * 4 * SIDE, 4 * SIDE), 4 * SIDE)
    kept[rows, :] = jnp.where(mine, terms, 0.0).astype(jnp.bfloat16)

    @pl.when(t == PLANES - 1)
    def _():
        outcome = lax.broadcasted_iota(jnp.int32, (8, WIDTH), 0)
        lane = lax.broadcasted_iota(jnp.int32, (8, WIDTH), 1)
        gather = (lax.rem(lane, OUTCOMES) == outcome).astype(jnp.float32).astype(jnp.bfloat16)
        found = lax.dot_general(
            gather, kept[...], (((1,), (1,)), ((), ())), preferred_element_type=jnp.float32
        )
        logp[...] = found[:OUTCOMES]


def settle(side, direct, lasts):
    return pl.pallas_call(
        settle_kernel,
        grid=(PLANES,),
        out_shape=(
            jax.ShapeDtypeStruct((LEVELS + 1, 4 * PEERS, WIDTH), jnp.bfloat16),
            jax.ShapeDtypeStruct((OUTCOMES, 4 * PEERS), jnp.float32),
        ),
        in_specs=[SMEM, pl.BlockSpec((SIDE, DIRECT, WIDTH), lambda t: (t, 0, 0))]
        + [pl.BlockSpec((2 * LEVELS, WIDTH), lambda t: (t, 0))] * SIDE,
        out_specs=(
            pl.BlockSpec((LEVELS + 1, 4 * SIDE, WIDTH), lambda t: (0, t, 0)),
            pl.BlockSpec((OUTCOMES, 4 * PEERS), lambda t: (0, 0)),
        ),
        scratch_shapes=[
            pltpu.VMEM((SIDE, 2 * LEVELS, WIDTH), jnp.bfloat16),
            pltpu.VMEM((4 * PEERS, WIDTH), jnp.bfloat16),
        ],
        compiler_params=pltpu.CompilerParams(vmem_limit_bytes=54 << 20),
        cost_estimate=pl.CostEstimate(flops=2 << 30, bytes_accessed=14 << 20, transcendentals=0),
        name="settle",
    )(side, direct, *lasts)


def patch_kernel(high, old, out):
    turn = chosen_rows(WIDTH, WIDTH, lambda i: lax.rem(i, 16) * 16 + lax.div(i, 16))
    slot = lax.broadcasted_iota(jnp.int32, (16, 16, WIDTH), 1)
    for group in range(2):
        for low in range(0, LEVELS, 16):
            parts = []
            for j in range(4 * group, 4 * group + 4):
                parts.append(jnp.zeros((32, WIDTH), jnp.bfloat16))
                for r in range(2):
                    start = r * LEVELS + low
                    parts.append(high[j, start : start + 16, :])
            turned = jnp.dot(turn, jnp.concatenate(parts, 0), preferred_element_type=jnp.float32)
            kept = old[low : low + 16, 16 * group : 16 * group + 16, :].astype(jnp.float32)
            both = jnp.where(lax.rem(slot, 4) >= 2, turned.reshape(16, 16, WIDTH), kept)
            out[low : low + 16, 16 * group : 16 * group + 16, :] = both.astype(jnp.bfloat16)
    out[LEVELS] = old[LEVELS]


def patch(high, new_cache):
    block = pl.BlockSpec((LEVELS + 1, 4 * SIDE, WIDTH), lambda t: (0, t, 0))
    return pl.pallas_call(
        patch_kernel,
        grid=(PLANES,),
        out_shape=jax.ShapeDtypeStruct(new_cache.shape, new_cache.dtype),
        in_specs=[pl.BlockSpec((SIDE, DIRECT, WIDTH), lambda t: (t, 0, 0)), block],
        out_specs=block,
        compiler_params=pltpu.CompilerParams(vmem_limit_bytes=16 << 20),
        name="patch",
    )(high, new_cache)


def pack_direct(low, dest, cache):
    return pl.pallas_call(
        functools.partial(direct_kernel, low),
        out_shape=jax.ShapeDtypeStruct((PEERS, DIRECT, WIDTH), jnp.bfloat16),
        in_specs=[SMEM, pl.BlockSpec(memory_space=pltpu.VMEM)],
        out_specs=ANY,
        scratch_shapes=[
            pltpu.SMEM((PEERS,), jnp.int32),
            pltpu.VMEM((LEVELS, WIDTH), jnp.bfloat16),
            pltpu.SemaphoreType.DMA,
        ],
        cost_estimate=pl.CostEstimate(flops=0, bytes_accessed=10 << 20, transcendentals=0),
        compiler_params=pltpu.CompilerParams(vmem_limit_bytes=8 << 20),
        name="pack_direct",
    )(dest, cache)


def exchanged(x, groups=None):
    return lax.all_to_all(
        x, "sample", split_axis=0, concat_axis=0, tiled=True, axis_index_groups=groups
    )


def xor_pairs(size, bit):
    return [(i, i ^ bit) for i in range(size)]


def tree_sum(x, axis, size, bits):
    terms = [x] + [lax.ppermute(x, axis, xor_pairs(size, bit)) for bit in bits]
    while len(terms) > 1:
        terms = [terms[i] + terms[i + 1] for i in range(0, len(terms), 2)]
    return terms[0]


def bf16_terms(x):
    terms = []
    for _ in range(3):
        term = lax.reduce_precision(x, 8, 7)
        terms.append(term.astype(jnp.bfloat16))
        x = x - term
    return terms


def on_device(tokens, cache, gain, w_query, w_key, w_value, w_out, w_head, coef, chosen, dest):
    target = dest[:, 0]
    me = lax.axis_index("sample")
    y, core = lax.rem(lax.div(me, 2), 4), lax.rem(me, 2)

    relay = pl.pallas_call(
        relay_kernel,
        out_shape=jax.ShapeDtypeStruct((PLANES, PIECE, WIDTH), jnp.bfloat16),
        in_specs=[SMEM, ANY],
        out_specs=ANY,
        scratch_shapes=[
            pltpu.SMEM((PEERS,), jnp.int32),
            pltpu.SMEM((PLANES + 1,), jnp.int32),
            pltpu.VMEM((PLANES, 8, WIDTH), jnp.float32),
            pltpu.VMEM((PLANES, PIECE, WIDTH), jnp.bfloat16),
            pltpu.SemaphoreType.DMA,
            pltpu.SemaphoreType.DMA,
        ],
        compiler_params=pltpu.CompilerParams(vmem_limit_bytes=4 << 20),
        name="pack_relay",
    )(target, cache)
    relayed = exchanged(relay, [[z * SIDE + i for z in range(PLANES)] for i in range(SIDE)])

    both, logp, grad_out, grad_head = decode_rows(
        tokens, cache, coef, chosen, gain, w_query, w_key, w_value, w_out, w_head
    )
    sums = jnp.concatenate([grad_out, grad_head], 0)
    target_now, sums = lax.optimization_barrier((target, sums))
    packed = pack_direct(0, target_now, cache)
    sums = tree_sum(sums, "rep", 4, (1, 2, 3))
    packed, sums = lax.optimization_barrier((packed, sums))
    sums = tree_sum(sums, "sample", PEERS, (2, 4, 6))
    sums = tree_sum(sums, "sample", PEERS, (1,))
    rows = jnp.arange(ROWS, dtype=jnp.int32)
    same = (target[:, None] == target[None, :]) & (rows[:, None] < rows[None, :])
    place = target * 4 + jnp.sum(same.astype(jnp.int32), 0)
    slot = (jnp.arange(4 * PEERS, dtype=jnp.int32)[:, None] == place[None, :]).astype(jnp.bfloat16)
    small = jnp.concatenate([both] + bf16_terms(logp), -1)
    slotted = jnp.dot(slot, small, preferred_element_type=jnp.float32).astype(jnp.bfloat16)
    new_rows = slotted[:, :WIDTH].reshape(PEERS, 4, WIDTH)
    mine = y * 2 + core
    share = sums[:ROWS].reshape(SIDE, 2, SIDE, ROWS)
    share = lax.dynamic_index_in_dim(share, mine, 2, keepdims=False).reshape(SIDE, WIDTH)
    share = jnp.stack(bf16_terms(share), 1)[None]
    share = jnp.broadcast_to(share, (PLANES, SIDE, 3, WIDTH)).reshape(PEERS, 3, WIDTH)
    head = jnp.swapaxes(sums[ROWS:].reshape(OUTCOMES, 2, HEAD), 0, 1).reshape(SIDE, HEAD)
    head = lax.dynamic_index_in_dim(head, mine, 0, keepdims=False)
    head = jnp.broadcast_to(jnp.concatenate(bf16_terms(head)), (PEERS, 3 * HEAD))
    logp_row = slotted[:, WIDTH:].reshape(PEERS, 12 * OUTCOMES)
    gap = jnp.zeros((PEERS, WIDTH - 12 * OUTCOMES - 3 * HEAD), jnp.bfloat16)
    mixed = jnp.concatenate([logp_row, gap, head], -1)[:, None]
    tiles = jnp.concatenate([new_rows, mixed, share], 1)
    packed = pl.pallas_call(
        tile_kernel,
        out_shape=jax.ShapeDtypeStruct(packed.shape, packed.dtype),
        in_specs=[pl.BlockSpec(memory_space=pltpu.VMEM), ANY],
        out_specs=ANY,
        scratch_shapes=[pltpu.SemaphoreType.DMA],
        input_output_aliases={1: 0},
        compiler_params=pltpu.CompilerParams(vmem_limit_bytes=2 << 20),
        name="pack_tiles",
    )(tiles, packed)
    direct = exchanged(packed)

    codes = relayed[:, RELAY * LEVELS, : 2 * RELAY].astype(jnp.int32)
    shifts = [(0, 0), (1, 0), (3, 0), (2, 0), (2, 1), (1, 1), (3, 1), (0, 1)]
    onto = jnp.stack([lax.rem(y + dy, 4) * 2 + (core ^ dc) for dy, dc in shifts])
    came = jnp.stack([lax.rem(y - dy + 4, 4) * 2 + (core ^ dc) for dy, dc in shifts])
    onward = pl.pallas_call(
        forward_kernel,
        out_shape=[jax.ShapeDtypeStruct((LAST, WIDTH), jnp.bfloat16)] * SIDE,
        in_specs=[SMEM, SMEM, ANY],
        out_specs=[ANY] * SIDE,
        scratch_shapes=[
            pltpu.SMEM((SIDE * 2 * PLANES,), jnp.int32),
            pltpu.VMEM((PLANES, PIECE, WIDTH), jnp.bfloat16),
            pltpu.VMEM((LEVELS, WIDTH), jnp.bfloat16),
            pltpu.VMEM((8, WIDTH), jnp.bfloat16),
            pltpu.SemaphoreType.DMA((SIDE,)),
            pltpu.SemaphoreType.DMA((SIDE,)),
            pltpu.SemaphoreType.DMA,
        ],
        cost_estimate=pl.CostEstimate(flops=0, bytes_accessed=5 << 20, transcendentals=0),
        compiler_params=pltpu.CompilerParams(vmem_limit_bytes=4 << 20),
        name="pack_plane",
    )(codes, onto.astype(jnp.int32), relayed)
    def in_plane(x, k):
        dy, dc = shifts[k]
        pairs = [
            ((z * 4 + y0) * 2 + c0, (z * 4 + (y0 + dy) % 4) * 2 + (c0 ^ dc))
            for z in range(PLANES)
            for y0 in range(4)
            for c0 in range(2)
        ]
        return lax.ppermute(x, "sample", pairs)

    lasts = [onward[0]] + [in_plane(onward[k], k) for k in range(1, SIDE)]
    came = came.astype(jnp.int32)
    over = pl.pallas_call(
        flag_kernel,
        grid=(1,),
        out_shape=jax.ShapeDtypeStruct((1,), jnp.int32),
        in_specs=[pl.BlockSpec((8, 128), lambda t: (LAST // 8 - 1, 0))] * SIDE,
        out_specs=SMEM,
        compiler_params=pltpu.CompilerParams(vmem_limit_bytes=2 << 20),
        name="flag",
    )(*lasts)

    direct, over = lax.optimization_barrier((direct, over))
    piece, head = pl.pallas_call(
        plane_sum_kernel,
        grid=(1,),
        out_shape=(
            jax.ShapeDtypeStruct((2 * SIDE, ROWS), jnp.float32),
            jax.ShapeDtypeStruct((OUTCOMES, ROWS), jnp.float32),
        ),
        in_specs=[pl.BlockSpec((PEERS, 8, WIDTH), lambda t: (0, 2 * LEVELS // 8, 0))],
        out_specs=(
            pl.BlockSpec((2 * SIDE, ROWS), lambda t: (0, 0)),
            pl.BlockSpec((OUTCOMES, ROWS), lambda t: (0, 0)),
        ),
        compiler_params=pltpu.CompilerParams(vmem_limit_bytes=4 << 20),
        name="plane_sum",
    )(direct)
    other = lax.ppermute(piece, "sample", xor_pairs(PEERS, 1))
    piece = jnp.where(
        core == 0, jnp.concatenate([piece, other], 0), jnp.concatenate([other, piece], 0)
    )
    direct, piece = lax.optimization_barrier((direct, piece))
    shares = jnp.stack([piece] + [in_plane(piece, shifts.index((dy, 0))) for dy in (1, 2, 3)])
    rows_y = jnp.arange(4, dtype=jnp.int32)
    ours = (lax.rem(y - rows_y + 4, 4)[:, None] == rows_y[None, :])[..., None, None]
    grad_out = jnp.sum(jnp.where(ours, shares[None], 0.0), 1).reshape(ROWS, ROWS)
    new_cache, log_probs = settle(came, direct, lasts)

    def by_relay(new_cache):
        return new_cache

    def by_pairs(new_cache):
        high = exchanged(pack_direct(2, target, cache))
        return patch(high, new_cache)

    new_cache = lax.cond(over[0] > 0, by_pairs, by_relay, new_cache)
    return (jnp.swapaxes(new_cache, 0, 1), log_probs.T, grad_out, head.T)


def solution(mesh):
    split = P(("sample", "rep"))
    whole = P()
    return jax.shard_map(
        on_device,
        mesh=mesh,
        in_specs=(split, split) + (whole,) * 6 + (split,) * 3,
        out_specs=(split, split, whole, whole),
        check_vma=False,
    )
```
